32 devices in a mesh: shard: 2 (over core), context: 4 (over z), tensor: 4 (over y, x).
Axes of the slice: x: 2, y: 2, z: 4, core: 2. Of those that a mesh axis runs over, the one named last changes fastest.
Arguments:
- tokens: bfloat16 [2, 4096, 2048], P('shard', 'context'), may hold values from -6 to 6
- ln1_gain: bfloat16 [2048], replicated, may hold values from 0.099609375 to 1.8984375
- ln1_shift: bfloat16 [2048], replicated, may hold values from -1.25 to 1.25
- q_weight: bfloat16 [2048, 2048], P('shard', 'tensor'), may hold values from -0.125 to 0.125
- k_weight: bfloat16 [2048, 2048], P('shard', 'tensor'), may hold values from -0.125 to 0.125
- v_weight: bfloat16 [2048, 2048], P('shard', 'tensor'), may hold values from -0.125 to 0.125
- q_bias: bfloat16 [2048], P('tensor'), may hold values from -1.75 to 1.75
- k_bias: bfloat16 [512], P('tensor'), may hold values from -3 to 3
- v_bias: bfloat16 [2048], P('tensor'), may hold values from -1.75 to 1.75
- o_weight: bfloat16 [2048, 2048], P('tensor', 'shard'), may hold values from -0.25 to 0.25
- ln2_gain: bfloat16 [2048], replicated, may hold values from 0.099609375 to 1.8984375
- ln2_shift: bfloat16 [2048], replicated, may hold values from -1.25 to 1.25
- gate_weight: bfloat16 [2048, 5632], P('shard', 'tensor'), may hold values from -0.125 to 0.125
- up_weight: bfloat16 [2048, 5632], P('shard', 'tensor'), may hold values from -0.125 to 0.125
- down_weight: bfloat16 [5632, 2048], P('tensor', 'shard'), may hold values from -0.109375 to 0.109375
- cotangent: bfloat16 [2, 4096, 2048], P('shard', 'context'), may hold values from -6 to 6
- doc_lengths: int32 [2, 4], P('shard'), may hold values from 1 to 2560, 4096 in all within a row
- picture_starts: int32 [2, 4], P('shard'), may hold values from 0 to 3840
Outputs:
- output: bfloat16 [2, 4096, 2048], P('shard', ('context', 'tensor'))
- tokens_grad: float32 [2, 4096, 2048], P('shard', ('context', 'tensor'))
- ln1_gain_grad: float32 [2048], replicated
- ln1_shift_grad: float32 [2048], replicated
- q_weight_grad: float32 [2048, 2048], P(('shard', 'context'), 'tensor')
- k_weight_grad: float32 [2048, 2048], P(('shard', 'context'), 'tensor')
- v_weight_grad: float32 [2048, 2048], P(('shard', 'context'), 'tensor')
- q_bias_grad: float32 [2048], P('tensor')
- k_bias_grad: float32 [512], P('tensor')
- v_bias_grad: float32 [2048], P('tensor')
- o_weight_grad: float32 [2048, 2048], P('tensor', ('shard', 'context'))
- ln2_gain_grad: float32 [2048], replicated
- ln2_shift_grad: float32 [2048], replicated
- gate_weight_grad: float32 [2048, 5632], P(('shard', 'context'), 'tensor')
- up_weight_grad: float32 [2048, 5632], P(('shard', 'context'), 'tensor')
- down_weight_grad: float32 [5632, 2048], P('tensor', ('shard', 'context'))
The draws below stay inside these ranges and needn't reach their ends.
Inputs may be any that keep to these rules, and one draw needn't show every extreme that they name: `doc_lengths`: each row of 4 document lengths sums to 4096; the documents follow one another from position 0. `picture_starts`: each picture span [s, s + 256) lies within its sequence; spans may share positions and may cross a document's bound.
All inputs are finite; a program needn't handle non-finite values.
Results may differ from the reference program's by a relative error of at most 0.03.
Values may be sent and summed in bfloat16 or wider, within the bound.
No kernel may reach another device: no remote copies, remote signals or barrier semaphores. Data moves between devices by JAX's collectives and lax.ppermute only.
A program may use at most 256 MiB of HBM per device.

```python
import math
import jax
import jax.numpy as jnp
import numpy as np
from jax import lax

D = 2048
FF = 5632
HEADS = 32
HEAD_DIM = 64
ROT = 16
SPAN = 256
DOCS = 4
PICS = 4
LENGTH = 4096
SEQS = 2


def set_ends(entries, own_key, low, high):
    dims = entries.shape
    spot = [jax.random.randint(jax.random.fold_in(own_key, axis), (), 0, dims[axis]) for axis in range(len(dims))]
    entries = entries.at[tuple(spot)].set(low)
    longest = dims.index(max(dims))
    spot[longest] = (spot[longest] + 1) % dims[longest]
    return entries.at[tuple(spot)].set(high)


def levels(stream_key, dims, cuts, low, largest):
    gain, own = 1.0, jax.random.fold_in(stream_key, 6)
    for dim, blocks in cuts:
        draws = jnp.exp(jax.random.uniform(jax.random.fold_in(own, dim), (blocks,), jnp.float32, low / len(cuts), largest / len(cuts)))
        gain = gain * jnp.repeat(draws, dims[dim] // blocks).reshape([-1 if axis == dim else 1 for axis in range(len(dims))])
    return gain


def profile(number_of, total, limit, slope):
    weights = [(1 << 20) // math.isqrt(standing ** slope) + 1 for standing in range(2, number_of + 1)]
    spare, counts = total - limit - (number_of - 1), [1] * (number_of - 1)
    while spare > 0:
        movable = [i for i in range(number_of - 1) if counts[i] < limit]
        whole, budget = sum([weights[i] for i in movable]), spare
        for i in movable:
            addition = min(limit - counts[i], max(1, budget * weights[i] // whole), spare)
            counts[i] = counts[i] + addition
            spare = spare - addition
    return np.array([limit] + counts)


def ragged(key, number_of, total, most, lean):
    if number_of == 2:
        one = jax.random.randint(key, (), max(1, total - most), min(most, total - 1) + 1)
        return jnp.stack([one, total - one])
    lengths = jnp.asarray(profile(number_of, total, most, lean), jnp.int32)
    pairs = (number_of - 1) // 2
    giver, receiver = lengths[1:1 + 2 * pairs:2], lengths[2:2 + 2 * pairs:2]
    slack = jnp.minimum(giver - 1, most - receiver)
    passed = jax.random.randint(jax.random.fold_in(key, 1), (pairs,), 0, 1 << 20) % (slack + 1)
    lengths = lengths.at[1:1 + 2 * pairs:2].set(giver - passed).at[2:2 + 2 * pairs:2].set(receiver + passed)
    return lengths[jax.random.permutation(jax.random.fold_in(key, 2), number_of)]


def noise(own_key, dims, spread, reach, pieces=(), kind=jnp.bfloat16):
    entries = jax.random.normal(own_key, dims, jnp.float32) * spread
    if len(pieces) > 0:
        entries = levels(own_key, dims, pieces, -0.22, 0.18) * entries
    return jnp.clip(entries, min=-reach, max=reach).astype(kind)


def setup_inputs(seed: int = 0) -> dict:
    streams_of = jax.random.split(jax.random.key(seed), 19)
    tokens = noise(streams_of[0], (SEQS, LENGTH, D), 1.0, 6.0, ((0, 2), (1, 4)))
    ln1_gain = jnp.clip(1.0 + 0.18 * jax.random.normal(streams_of[1], (D,), jnp.float32), 0.099609375, 1.8984375).astype(jnp.bfloat16)
    ln1_shift = noise(streams_of[2], (D,), 0.2, 1.25)
    q_weight = noise(streams_of[3], (D, D), D ** -0.5, 0.125, ((0, 2), (1, 4)))
    k_weight = noise(streams_of[4], (D, D), D ** -0.5, 0.125, ((0, 2), (1, 4)))
    v_weight = noise(streams_of[5], (D, D), D ** -0.5, 0.125, ((0, 2), (1, 4)))
    q_bias = noise(streams_of[6], (D,), 0.3, 1.75, ((0, 4),))
    k_bias = noise(streams_of[7], (HEADS * ROT,), 0.5, 3.0, ((0, 4),))
    v_bias = noise(streams_of[8], (D,), 0.3, 1.75, ((0, 4),))
    o_weight = noise(streams_of[9], (D, D), (D // 4) ** -0.5, 0.25, ((0, 4), (1, 2)))
    ln2_gain = jnp.clip(1.0 + 0.18 * jax.random.normal(streams_of[10], (D,), jnp.float32), 0.099609375, 1.8984375).astype(jnp.bfloat16)
    ln2_shift = noise(streams_of[11], (D,), 0.2, 1.25)
    gate_weight = noise(streams_of[12], (D, FF), D ** -0.5, 0.125, ((0, 2), (1, 4)))
    up_weight = noise(streams_of[13], (D, FF), D ** -0.5, 0.125, ((0, 2), (1, 4)))
    down_weight = noise(streams_of[14], (FF, D), (FF // 2) ** -0.5, 0.109375, ((0, 4), (1, 2)))
    cotangent = noise(streams_of[15], (SEQS, LENGTH, D), 1.0, 6.0, ((0, 2), (1, 4)))
    doc_lengths = jax.vmap(lambda own: ragged(own, DOCS, LENGTH, 5 * LENGTH // 8, 1))(jax.random.split(streams_of[16], SEQS)).reshape((SEQS, DOCS)).astype(jnp.int32)
    picture_starts = set_ends(jax.random.randint(streams_of[17], (SEQS, PICS), 0, LENGTH - SPAN + 1), jax.random.fold_in(streams_of[17], 1), 0, LENGTH - SPAN).astype(jnp.int32)
    return dict(tokens=tokens, ln1_gain=ln1_gain, ln1_shift=ln1_shift, q_weight=q_weight, k_weight=k_weight, v_weight=v_weight, q_bias=q_bias, k_bias=k_bias, v_bias=v_bias, o_weight=o_weight, ln2_gain=ln2_gain, ln2_shift=ln2_shift, gate_weight=gate_weight, up_weight=up_weight, down_weight=down_weight, cotangent=cotangent, doc_lengths=doc_lengths, picture_starts=picture_starts)


@jax.custom_vjp
def low(v):
    return lax.optimization_barrier(v.astype(jnp.bfloat16)).astype(jnp.float32)

@jax.custom_vjp
def low_back(v):
    return v

def low_keep(v):
    return (low(v), None)

def low_pass(kept, grad):
    return (grad,)

def back_keep(v):
    return (v, None)

def back_low(kept, grad):
    return (low(grad),)
low.defvjp(low_keep, low_pass)
low_back.defvjp(back_keep, back_low)
norm_eps = 1e-05
masked_score = -1e+30
highest = lax.Precision.HIGHEST

def matmul(left_side, right_side):
    return jnp.dot(left_side, right_side, precision=highest)

def layer_norm(row_block, gain_vec, shift_vec):
    row_mean = lax.optimization_barrier(jnp.mean(row_block, axis=-1, keepdims=True))
    centered = row_block - row_mean
    inv_std = lax.rsqrt(lax.optimization_barrier(jnp.mean(centered * centered, axis=-1, keepdims=True)) + norm_eps)
    return centered * inv_std * gain_vec + shift_vec

def rotary_tables(positions):
    half_rot = ROT // 2
    inverse_freq = 10000.0 ** (-(2.0 * jnp.arange(half_rot).astype(jnp.float32)) / ROT)
    angles = positions.astype(jnp.float32)[:, None] * inverse_freq[None, :]
    cosine_table = jnp.concatenate([jnp.cos(angles), jnp.cos(angles)], axis=-1)
    sine_table = jnp.concatenate([jnp.sin(angles), jnp.sin(angles)], axis=-1)
    return (cosine_table, sine_table)

def apply_rotary(tensor, cosine_table, sine_table):
    half_rot = ROT // 2
    rot_part = tensor[..., :ROT]
    turned = jnp.concatenate([-rot_part[..., half_rot:], rot_part[..., :half_rot]], axis=-1)
    rotated = rot_part * cosine_table[:, None, :] + turned * sine_table[:, None, :]
    return jnp.concatenate([rotated, tensor[..., ROT:]], axis=-1)

def doc_ids(lengths_row):
    doc_ends = jnp.cumsum(lengths_row).astype(jnp.int32)
    positions = jnp.arange(LENGTH, dtype=jnp.int32)
    return lax.optimization_barrier(jnp.sum((positions[:, None] >= doc_ends[None, :]).astype(jnp.int32), axis=-1))

def picture_flags(starts_row):
    positions = jnp.arange(LENGTH, dtype=jnp.int32)
    return (positions[:, None] >= starts_row[None, :]) & (positions[:, None] < starts_row[None, :] + SPAN)

def attend_sequence(members):
    query_seq, key_seq, value_seq, doc_seq, flag_seq = members
    block_rows = math.gcd(LENGTH, 512)
    positions = jnp.arange(LENGTH, dtype=jnp.int32)

    def one_block(block_index):
        first_row = block_index * block_rows
        query_block = lax.dynamic_slice_in_dim(query_seq, first_row, block_rows, 0)
        query_pos = first_row + jnp.arange(block_rows, dtype=jnp.int32)
        query_doc = lax.dynamic_slice_in_dim(doc_seq, first_row, block_rows, 0)
        query_flag = lax.dynamic_slice_in_dim(flag_seq, first_row, block_rows, 0)
        shared = jnp.any(query_flag[:, None, :] & flag_seq[None, :, :], axis=-1)
        permitted = (query_doc[:, None] == doc_seq[None, :]) & ((positions[None, :] <= query_pos[:, None]) | shared)
        scores = low_back(jnp.einsum('qhd,khd->hqk', query_block, key_seq, precision=highest) * HEAD_DIM ** (-0.5))
        scores = jnp.where(permitted[None], scores, masked_score)
        prob_rows = low(jax.nn.softmax(scores, axis=-1))
        return jnp.einsum('hqk,khd->qhd', prob_rows, value_seq, precision=highest)
    blocks = lax.map(jax.checkpoint(one_block), jnp.arange(LENGTH // block_rows, dtype=jnp.int32))
    return blocks.reshape(LENGTH, HEADS, HEAD_DIM)

def reference(tokens, ln1_gain, ln1_shift, q_weight, k_weight, v_weight, q_bias, k_bias, v_bias, o_weight, ln2_gain, ln2_shift, gate_weight, up_weight, down_weight, cotangent, doc_lengths, picture_starts):
    doc_table = jax.vmap(doc_ids)(doc_lengths)
    flag_table = jax.vmap(picture_flags)(picture_starts)
    cosine_table, sine_table = rotary_tables(jnp.arange(LENGTH, dtype=jnp.int32))

    def forward(params):
        tokens_f, ln1_gain, ln1_shift, q_weight, k_weight, v_weight, q_bias, k_bias, v_bias, o_weight, ln2_gain, ln2_shift, gate_weight, up_weight, down_weight = params
        all_rows = tokens_f.reshape(SEQS * LENGTH, D)
        normed_one = low(layer_norm(all_rows, ln1_gain, ln1_shift))
        query_pre = low_back(matmul(normed_one, q_weight) + q_bias)
        key_lin = matmul(normed_one, k_weight).reshape(SEQS * LENGTH, HEADS, HEAD_DIM)
        key_pre = low_back(jnp.concatenate([key_lin[..., :ROT] + k_bias.reshape(HEADS, ROT), key_lin[..., ROT:]], axis=-1))
        value_pre = low(low_back(matmul(normed_one, v_weight) + v_bias))
        query_rot = low(apply_rotary(query_pre.reshape(SEQS, LENGTH, HEADS, HEAD_DIM), cosine_table, sine_table))
        key_rot = low(apply_rotary(key_pre.reshape(SEQS, LENGTH, HEADS, HEAD_DIM), cosine_table, sine_table))
        value_heads = value_pre.reshape(SEQS, LENGTH, HEADS, HEAD_DIM)
        mixed_heads = lax.map(attend_sequence, (query_rot, key_rot, value_heads, doc_table, flag_table))
        mixed_heads = low(low_back(mixed_heads.reshape(SEQS * LENGTH, D)))
        attn_out = low_back(matmul(mixed_heads, o_weight))
        middle = all_rows + attn_out
        normed_two = low(layer_norm(middle, ln2_gain, ln2_shift))
        gate_pre = low_back(matmul(normed_two, gate_weight))
        up_pre = low_back(matmul(normed_two, up_weight))
        hidden = low(jax.nn.silu(gate_pre) * up_pre)
        return (middle + matmul(hidden, down_weight)).reshape(SEQS, LENGTH, D)
    float_args = jax.tree.map(lambda member: member.astype(jnp.float32), (tokens, ln1_gain, ln1_shift, q_weight, k_weight, v_weight, q_bias, k_bias, v_bias, o_weight, ln2_gain, ln2_shift, gate_weight, up_weight, down_weight))
    output_f, pullback = jax.vjp(forward, float_args)
    gradients = pullback(cotangent.astype(jnp.float32))[0]
    return (output_f.astype(jnp.bfloat16), gradients[0], gradients[1], gradients[2], gradients[3], gradients[4], gradients[5], gradients[6], gradients[7], gradients[8], gradients[9], gradients[10], gradients[11], gradients[12], gradients[13], gradients[14])
```

```python
import functools

import jax
import jax.numpy as jnp
from jax import lax
from jax.experimental import pallas as pl
from jax.experimental.pallas import tpu as pltpu
from jax.sharding import PartitionSpec as P

HEAD_DIM = 64
ROT = 16
SPAN = 256
PAIR = 128
EPS = 1e-05
LOW = -1e30
LOWER = -2e30
SCALE = HEAD_DIM ** (-0.5)

f32 = jnp.float32
bf16 = jnp.bfloat16


NT = (((1,), (1,)), ((), ()))
NN = (((1,), (0,)), ((), ()))
TN = (((0,), (0,)), ((), ()))


def dot(a, b, dims=NN):
    return lax.dot_general(a, b, dims, preferred_element_type=f32)


def swap_with(x, axis, bit):
    size = lax.axis_size(axis)
    return lax.ppermute(x, axis, [(i, i ^ bit) for i in range(size)])


def sum_over(x, axis):
    size = lax.axis_size(axis)
    bit = 1
    while bit < size:
        x = x + swap_with(x, axis, bit)
        bit *= 2
    return x


def rotary_tables(positions):
    half = ROT // 2
    freq = 10000.0 ** (-(2.0 * jnp.arange(half).astype(f32)) / ROT)
    angles = freq[:, None] * positions.astype(f32)[None, :]
    parts = jnp.concatenate([jnp.cos(angles), jnp.sin(angles)], axis=0)
    lane = jnp.arange(PAIR) % HEAD_DIM
    row = jnp.arange(half)[:, None]
    hit = (lane[None, :] % half == row) & (lane[None, :] < ROT)
    spread_cos = jnp.concatenate([hit, jnp.zeros_like(hit)], axis=0).astype(f32)
    sign = jnp.where(lane < half, -1.0, 1.0)[None, :]
    spread_sin = jnp.concatenate([jnp.zeros_like(hit), hit], axis=0).astype(f32) * sign
    expand = functools.partial(
        lax.dot_general,
        dimension_numbers=TN,
        precision=lax.Precision.HIGHEST,
        preferred_element_type=f32,
    )
    rest = jnp.where(lane < ROT, 0.0, 1.0).astype(f32)
    return expand(parts, spread_cos) + rest[None, :], expand(parts, spread_sin)


def swap_halves(x):
    lane = lax.broadcasted_iota(jnp.int32, x.shape, 1) % HEAD_DIM
    return jnp.where(lane < ROT // 2, pltpu.roll(x, PAIR - ROT // 2, 1), pltpu.roll(x, ROT // 2, 1))


def project_kernel(
    groups,
    ids,
    x_own,
    x_oth,
    gain_own,
    gain_oth,
    shift_own,
    shift_oth,
    wq_own,
    wk_own,
    wv_own,
    wq_oth,
    wk_oth,
    wv_oth,
    q_bias,
    k_bias,
    v_bias,
    cos_ref,
    sin_ref,
    *rest,
):
    h_ref, pieces, (qs, ks, vs) = rest[0], rest[1 : 1 + groups], rest[1 + groups :]
    half = x_own.shape[1]
    a = x_own[...].astype(f32)
    b = x_oth[...].astype(f32)
    count = 1.0 / (2 * half)
    mean = (jnp.sum(a, axis=1, keepdims=True) + jnp.sum(b, axis=1, keepdims=True)) * count
    a = a - mean
    b = b - mean
    var = (jnp.sum(a * a, axis=1, keepdims=True) + jnp.sum(b * b, axis=1, keepdims=True)) * count
    inv = lax.rsqrt(var + EPS)
    ha = (a * inv * gain_own[...].astype(f32) + shift_own[...].astype(f32)).astype(bf16)
    hb = (b * inv * gain_oth[...].astype(f32) + shift_oth[...].astype(f32)).astype(bf16)
    h_ref[:, :half] = ha
    h_ref[:, half:] = hb
    qs[...] = dot(ha, wq_own[...]) + dot(hb, wq_oth[...]) + q_bias[...]
    ks[...] = dot(ha, wk_own[...]) + dot(hb, wk_oth[...]) + k_bias[...]
    vs[...] = dot(ha, wv_own[...]) + dot(hb, wv_oth[...]) + v_bias[...]
    cos = cos_ref[...]
    sin = sin_ref[...]
    for s in range(groups):
        group = (ids[1] & (groups - 1)) ^ s
        cols = pl.ds(pl.multiple_of(group * PAIR, PAIR), PAIR)
        q = qs[:, cols]
        k = ks[:, cols]
        pieces[s][:, :PAIR] = (q * cos + swap_halves(q) * sin).astype(bf16)
        pieces[s][:, PAIR : 2 * PAIR] = (k * cos + swap_halves(k) * sin).astype(bf16)
        pieces[s][:, 2 * PAIR :] = vs[:, cols].astype(bf16)


def project(ids, tokens, gain, shift, own, other, biases, tables, groups, slots):
    rows, width = tokens.shape
    half = width // 2
    share = rows // slots
    inner = own[0].shape[1]

    def row_block(i, ids):
        return ids[2] ^ i

    whole = lambda i, ids: (0, 0)
    weight = pl.BlockSpec((half, inner), whole)
    bias = pl.BlockSpec((1, inner), whole)
    in_specs = [
        pl.BlockSpec((share, half), lambda i, ids: (row_block(i, ids), ids[0])),
        pl.BlockSpec((share, half), lambda i, ids: (row_block(i, ids), 1 - ids[0])),
        pl.BlockSpec((1, half), lambda i, ids: (0, ids[0])),
        pl.BlockSpec((1, half), lambda i, ids: (0, 1 - ids[0])),
        pl.BlockSpec((1, half), lambda i, ids: (0, ids[0])),
        pl.BlockSpec((1, half), lambda i, ids: (0, 1 - ids[0])),
    ]
    in_specs += [weight] * 6 + [bias] * 3
    in_specs += [pl.BlockSpec((share, PAIR), lambda i, ids: (row_block(i, ids), 0))] * 2
    out = pl.pallas_call(
        functools.partial(project_kernel, groups),
        grid_spec=pltpu.PrefetchScalarGridSpec(
            num_scalar_prefetch=1,
            grid=(slots,),
            in_specs=in_specs,
            out_specs=[pl.BlockSpec((share, width), lambda i, ids: (i, 0))]
            + [pl.BlockSpec((share, 3 * PAIR), lambda i, ids: (i, 0))] * groups,
            scratch_shapes=[pltpu.VMEM((share, inner), f32)] * 3,
        ),
        out_shape=[jax.ShapeDtypeStruct((rows, width), bf16)]
        + [jax.ShapeDtypeStruct((rows, 3 * PAIR), bf16)] * groups,
        compiler_params=pltpu.CompilerParams(vmem_limit_bytes=56 << 20),
        cost_estimate=pl.CostEstimate(
            flops=2 * rows * width * inner * 3,
            bytes_accessed=rows * width * 4 + 3 * width * inner * 2 + rows * inner * 6,
            transcendentals=rows,
        ),
        name="project",
    )(ids, tokens, tokens, gain, gain, shift, shift, *own, *other, *biases, *tables)
    return out[0], out[1:]


def reach(ids, p, docs, pics, length):
    start = jnp.zeros_like(p)
    end = jnp.full_like(p, length)
    for j in range(docs):
        e = ids[4 + j]
        start = jnp.where(p >= e, jnp.maximum(start, e), start)
        end = jnp.where(p < e, jnp.minimum(end, e), end)
    far = p + 1
    for j in range(pics):
        b = ids[4 + docs + j]
        inside = (p >= b) & (p < b + SPAN)
        far = jnp.where(inside, jnp.maximum(far, jnp.minimum(b + SPAN, end)), far)
    return start, far


def block_ranges(ids, first, bq, bk, docs, pics, length):
    lo_a, hi_a = reach(ids, first, docs, pics, length)
    lo_b, hi_b = reach(ids, first + (bq - 1), docs, pics, length)
    begin = lo_a // bk
    stop = (hi_b + (bk - 1)) // bk
    full_begin = jnp.clip((lo_b + (bk - 1)) // bk, begin, stop)
    full_stop = jnp.clip(hi_a // bk, full_begin, stop)
    return begin, full_begin, full_stop, stop


def piece_copies(ids, pieces, whole, sems, slots, share, outward=False):
    copies = []
    for s, piece in enumerate(pieces):
        for i in range(slots):
            first = ((ids[1] ^ s) * slots + (ids[2] ^ i)) * share
            there = whole.at[pl.ds(pl.multiple_of(first, share), share)]
            here = piece.at[pl.ds(i * share, share)]
            src, dst = (there, here) if outward else (here, there)
            copies.append(pltpu.make_async_copy(src, dst, sems.at[s * slots + i]))
    return copies


def attend_kernel(dims, ids, *refs):
    pieces, groups, slots, share, length, docs, pics, bq, bk = dims
    ins = refs[:pieces]
    outs = refs[pieces : pieces + groups]
    o_t, lse = refs[pieces + groups : pieces + groups + 2]
    qkv, vx, ob, acc, m_ref, sem_in, sem_out = refs[pieces + groups + 2 :]
    loads = piece_copies(ids, ins, qkv, sem_in, slots, share)
    for c in loads:
        c.start()
    for c in loads:
        c.wait()

    def prepare(j, _):
        rows = pl.ds(pl.multiple_of(j * bk, bk), bk)
        v_t = qkv[rows, 2 * PAIR :].astype(f32).T
        ones = jnp.ones((16, bk), bf16)
        for h in range(2):
            vx[h, :HEAD_DIM, rows] = v_t[h * HEAD_DIM : (h + 1) * HEAD_DIM].astype(bf16)
            vx[h, HEAD_DIM:, rows] = ones
        return 0

    lax.fori_loop(0, length // bk, prepare, 0)
    lane = lax.broadcasted_iota(jnp.int32, (bq, PAIR), 1)

    def query_block(i, _):
        first = i * bq
        rows = pl.ds(pl.multiple_of(first, bq), bq)
        q = qkv[rows, :PAIR].astype(f32) * SCALE
        heads = [
            jnp.where((lane < HEAD_DIM) == (h == 0), q, 0.0).astype(bf16) for h in range(2)
        ]
        for h in range(2):
            acc[h] = jnp.zeros_like(acc[h])
            m_ref[h] = jnp.full_like(m_ref[h], LOW)
        lo, hi = reach(
            ids, first + lax.broadcasted_iota(jnp.int32, (1, bq), 1), docs, pics, length
        )
        begin, full_begin, full_stop, stop = block_ranges(
            ids, first, bq, bk, docs, pics, length
        )

        def visit(masked, j, _):
            keys = pl.ds(pl.multiple_of(j * bk, bk), bk)
            k = qkv[keys, PAIR : 2 * PAIR]
            if masked:
                p = j * bk + lax.broadcasted_iota(jnp.int32, (bk, bq), 0)
                ok = (p >= lo) & (p < hi)
            for h in range(2):
                s = dot(k, heads[h], NT)
                if masked:
                    s = jnp.where(ok, s, LOWER)
                old = m_ref[h, 0:1]
                new = jnp.maximum(old, jnp.max(s, axis=0, keepdims=True))
                w = jnp.exp(s - new).astype(bf16)
                acc[h] = acc[h] * jnp.exp(old - new) + dot(vx[h, :, keys], w)
                m_ref[h, 0:1] = new
            return 0

        lax.fori_loop(begin, full_begin, functools.partial(visit, True), 0)
        lax.fori_loop(full_begin, full_stop, functools.partial(visit, False), 0)
        lax.fori_loop(full_stop, stop, functools.partial(visit, True), 0)
        for h in range(2):
            total = acc[h, HEAD_DIM : HEAD_DIM + 1]
            o_t[h * HEAD_DIM : (h + 1) * HEAD_DIM, rows] = acc[h, :HEAD_DIM] / total
            lse[h : h + 1, rows] = m_ref[h, 0:1] + jnp.log(total)
        ob[rows] = o_t[:, rows].T.astype(bf16)
        return 0

    lax.fori_loop(0, length // bq, query_block, 0)
    stores = piece_copies(ids, outs, ob, sem_out, slots, share, outward=True)
    for c in stores:
        c.start()
    for c in stores:
        c.wait()


def attend_cost(length, matmuls):
    pairs = length * length // 2
    return pl.CostEstimate(
        flops=2 * pairs * 256 * 2 * matmuls,
        bytes_accessed=length * PAIR * 2 * 8,
        transcendentals=2 * pairs,
    )


def attend(ids, pieces, groups, slots, docs, pics, bq, bk):
    rows = pieces[0].shape[0]
    n = len(pieces)
    length = rows * n
    share = rows // slots
    dims = (n, groups, slots, share, length, docs, pics, bq, bk)
    anywhere = pl.BlockSpec(memory_space=pl.ANY)
    out = pl.pallas_call(
        functools.partial(attend_kernel, dims),
        grid_spec=pltpu.PrefetchScalarGridSpec(
            num_scalar_prefetch=1,
            grid=(1,),
            in_specs=[anywhere] * n,
            out_specs=[anywhere] * groups
            + [
                pl.BlockSpec((PAIR, length), lambda i, ids: (0, 0)),
                pl.BlockSpec((8, length), lambda i, ids: (0, 0)),
            ],
            scratch_shapes=[
                pltpu.VMEM((length, 3 * PAIR), bf16),
                pltpu.VMEM((2, HEAD_DIM + 16, length), bf16),
                pltpu.VMEM((length, PAIR), bf16),
                pltpu.VMEM((2, HEAD_DIM + 16, bq), f32),
                pltpu.VMEM((2, 8, bq), f32),
                pltpu.SemaphoreType.DMA((n * slots,)),
                pltpu.SemaphoreType.DMA((groups * slots,)),
            ],
        ),
        out_shape=[jax.ShapeDtypeStruct((rows, PAIR), bf16)] * groups
        + [
            jax.ShapeDtypeStruct((PAIR, length), f32),
            jax.ShapeDtypeStruct((8, length), f32),
        ],
        compiler_params=pltpu.CompilerParams(vmem_limit_bytes=56 << 20),
        cost_estimate=attend_cost(length, 2),
        name="attend",
    )(ids, *pieces)
    return out[:groups], out[groups], out[groups + 1]


def attend_back_kernel(dims, ids, *refs):
    pieces, groups, slots, share, length, docs, pics, bq, bk = dims
    ins = refs[:pieces]
    grads = refs[pieces : 2 * pieces]
    o_t, lse, cos_ref, sin_ref = refs[2 * pieces : 2 * pieces + 4]
    outs = refs[2 * pieces + 4 : 2 * pieces + 4 + groups]
    qkv, dob, kt, dq_t, dk, dv, sem_in, sem_grad, sem_out = refs[2 * pieces + 4 + groups :]
    loads = piece_copies(ids, ins, qkv, sem_in, slots, share)
    loads += piece_copies(ids, grads, dob, sem_grad, slots, share)
    for c in loads:
        c.start()
    for c in loads:
        c.wait()

    def prepare(j, _):
        rows = pl.ds(pl.multiple_of(j * bk, bk), bk)
        kt[:, rows] = qkv[rows, PAIR : 2 * PAIR].astype(f32).T.astype(bf16)
        dk[rows] = jnp.zeros((bk, PAIR), f32)
        dv[rows] = jnp.zeros((bk, PAIR), f32)
        return 0

    lax.fori_loop(0, length // bk, prepare, 0)
    lane = lax.broadcasted_iota(jnp.int32, (bq, PAIR), 1)

    def turn_back(x, rows):
        return x * cos_ref[rows] - swap_halves(x) * sin_ref[rows]

    def query_block(i, _):
        first = i * bq
        rows = pl.ds(pl.multiple_of(first, bq), bq)
        q = qkv[rows, :PAIR].astype(f32) * SCALE
        do = dob[rows].astype(f32)
        q_of = []
        do_of = []
        for h in range(2):
            mine = (lane < HEAD_DIM) == (h == 0)
            q_of.append(jnp.where(mine, q, 0.0).astype(bf16))
            do_of.append(jnp.where(mine, do, 0.0).astype(bf16))
        prod = do.T * o_t[:, rows]
        delta = [
            jnp.sum(prod[h * HEAD_DIM : (h + 1) * HEAD_DIM], axis=0, keepdims=True)
            for h in range(2)
        ]
        dq_t[...] = jnp.zeros_like(dq_t)
        lo, hi = reach(
            ids, first + lax.broadcasted_iota(jnp.int32, (1, bq), 1), docs, pics, length
        )
        begin, full_begin, full_stop, stop = block_ranges(
            ids, first, bq, bk, docs, pics, length
        )

        def visit(masked, j, _):
            keys = pl.ds(pl.multiple_of(j * bk, bk), bk)
            k = qkv[keys, PAIR : 2 * PAIR]
            v = qkv[keys, 2 * PAIR :]
            if masked:
                p = j * bk + lax.broadcasted_iota(jnp.int32, (bk, bq), 0)
                ok = (p >= lo) & (p < hi)
            dk_sum = dk[keys]
            dv_sum = dv[keys]
            for h in range(2):
                feats = slice(h * HEAD_DIM, (h + 1) * HEAD_DIM)
                s = dot(k, q_of[h], NT)
                if masked:
                    s = jnp.where(ok, s, LOWER)
                w = jnp.exp(s - lse[h : h + 1, rows])
                dw = dot(v, do_of[h], NT)
                ds = (w * (dw - delta[h])).astype(bf16)
                dv_sum = dv_sum + dot(w.astype(bf16), do_of[h])
                dk_sum = dk_sum + dot(ds, q_of[h])
                dq_t[feats] += dot(kt[feats, keys], ds)
            dk[keys] = dk_sum
            dv[keys] = dv_sum
            return 0

        lax.fori_loop(begin, full_begin, functools.partial(visit, True), 0)
        lax.fori_loop(full_begin, full_stop, functools.partial(visit, False), 0)
        lax.fori_loop(full_stop, stop, functools.partial(visit, True), 0)
        dq = dq_t[...].T * SCALE
        qkv[rows, :PAIR] = turn_back(dq, rows).astype(bf16)
        return 0

    lax.fori_loop(0, length // bq, query_block, 0)

    def finish(j, _):
        rows = pl.ds(pl.multiple_of(j * bk, bk), bk)
        qkv[rows, PAIR : 2 * PAIR] = turn_back(dk[rows], rows).astype(bf16)
        qkv[rows, 2 * PAIR :] = dv[rows].astype(bf16)
        return 0

    lax.fori_loop(0, length // bk, finish, 0)
    stores = piece_copies(ids, outs, qkv, sem_out, slots, share, outward=True)
    for c in stores:
        c.start()
    for c in stores:
        c.wait()


def attend_back(ids, pieces, grads, o_t, lse, tables, groups, slots, docs, pics, bq, bk):
    rows = pieces[0].shape[0]
    n = len(pieces)
    length = rows * n
    share = rows // slots
    dims = (n, groups, slots, share, length, docs, pics, bq, bk)
    anywhere = pl.BlockSpec(memory_space=pl.ANY)
    once = dict(pipeline_mode=pl.Buffered(1))
    return pl.pallas_call(
        functools.partial(attend_back_kernel, dims),
        grid_spec=pltpu.PrefetchScalarGridSpec(
            num_scalar_prefetch=1,
            grid=(1,),
            in_specs=[anywhere] * (2 * n)
            + [
                pl.BlockSpec((PAIR, length), lambda i, ids: (0, 0), **once),
                pl.BlockSpec((8, length), lambda i, ids: (0, 0), **once),
                pl.BlockSpec((length, PAIR), lambda i, ids: (0, 0), **once),
                pl.BlockSpec((length, PAIR), lambda i, ids: (0, 0), **once),
            ],
            out_specs=[anywhere] * groups,
            scratch_shapes=[
                pltpu.VMEM((length, 3 * PAIR), bf16),
                pltpu.VMEM((length, PAIR), bf16),
                pltpu.VMEM((PAIR, length), bf16),
                pltpu.VMEM((PAIR, bq), f32),
                pltpu.VMEM((length, PAIR), f32),
                pltpu.VMEM((length, PAIR), f32),
                pltpu.SemaphoreType.DMA((n * slots,)),
                pltpu.SemaphoreType.DMA((n * slots,)),
                pltpu.SemaphoreType.DMA((groups * slots,)),
            ],
        ),
        out_shape=[jax.ShapeDtypeStruct((rows, 3 * PAIR), bf16)] * groups,
        compiler_params=pltpu.CompilerParams(vmem_limit_bytes=56 << 20),
        cost_estimate=attend_cost(length, 5),
        name="attend_back",
    )(ids, *pieces, *grads, o_t, lse, *tables)


def local(
    tokens,
    ln1_gain,
    ln1_shift,
    q_weight,
    k_weight,
    v_weight,
    q_bias,
    k_bias,
    v_bias,
    o_weight,
    ln2_gain,
    ln2_shift,
    gate_weight,
    up_weight,
    down_weight,
    cotangent,
    doc_lengths,
    picture_starts,
):
    me = lax.axis_index("shard")
    ctx = lax.axis_index("context")
    ctxs = lax.axis_size("context")
    ten = lax.axis_index("tensor")
    slots = lax.axis_size("tensor")
    rows, width = tokens.shape[1:]
    half = width // 2
    share = rows // slots
    inner = q_weight.shape[1]
    hidden_here = gate_weight.shape[1]
    groups = inner // PAIR
    heads_here = inner // HEAD_DIM
    docs = doc_lengths.shape[1]
    pics = picture_starts.shape[1]
    length = ctxs * rows
    quarter = half // ctxs
    bq = min(512, rows)
    bk = min(512, rows)
    assert ctxs % groups == 0 and ctxs & (ctxs - 1) == 0 and slots & (slots - 1) == 0

    def by_shard(x):
        turned = jnp.concatenate([x[..., half:], x[..., :half]], axis=-1)
        return jnp.where(me == 0, x, turned)

    def slot_rows(x, i):
        return lax.dynamic_slice_in_dim(x, (ten ^ i) * share, share, 0)

    def group_order(x, axis):
        size = x.shape[axis] // groups
        first = ctx & (groups - 1)
        return jnp.concatenate(
            [lax.dynamic_slice_in_dim(x, (first ^ s) * size, size, axis) for s in range(groups)],
            axis=axis,
        )

    def other_half(x):
        return swap_with(x, "shard", 1)

    own_qkv = (q_weight, k_weight, v_weight)
    oth_qkv = tuple(other_half(w) for w in own_qkv)
    oth_o = other_half(o_weight)
    oth_gate = other_half(gate_weight)
    oth_up = other_half(up_weight)
    oth_down = other_half(down_weight)

    doc_ends = jnp.cumsum(doc_lengths[0])
    ids = jnp.concatenate(
        [
            jnp.stack([me, ctx, ten, ctx * 0]).astype(jnp.int32),
            doc_ends.astype(jnp.int32),
            picture_starts[0].astype(jnp.int32),
        ]
    )
    local_tables = rotary_tables(ctx * rows + jnp.arange(rows, dtype=jnp.int32))
    k_bias_wide = jnp.pad(
        k_bias.astype(f32).reshape(heads_here, ROT), ((0, 0), (0, HEAD_DIM - ROT))
    ).reshape(1, inner)
    h1, send = project(
        ids,
        tokens[0],
        ln1_gain.reshape(1, width),
        ln1_shift.reshape(1, width),
        own_qkv,
        oth_qkv,
        (q_bias.astype(f32).reshape(1, inner), k_bias_wide, v_bias.astype(f32).reshape(1, inner)),
        local_tables,
        groups,
        slots,
    )
    pieces = [send[0]] + [swap_with(send[s % groups], "context", s) for s in range(1, ctxs)]

    o_full = jnp.concatenate([o_weight, oth_o], axis=1)
    gate_up = jnp.concatenate(
        [
            jnp.concatenate([gate_weight, up_weight], axis=1),
            jnp.concatenate([oth_gate, oth_up], axis=1),
        ],
        axis=0,
    )
    down_full = jnp.concatenate([down_weight, oth_down], axis=1)
    cot = [by_shard(slot_rows(cotangent[0], i)) for i in range(slots)]
    gain_two = by_shard(ln2_gain.astype(f32))
    shift_two = by_shard(ln2_shift.astype(f32))
    gain_one = by_shard(ln1_gain.astype(f32))
    x_share = by_shard(slot_rows(tokens[0], 0)).astype(f32)

    attn_send, o_t, lse = attend(ids, pieces, groups, slots, docs, pics, bq, bk)
    attn = [attn_send[0]] + [swap_with(attn_send[s], "context", s) for s in range(1, groups)]
    attn = group_order(jnp.concatenate(attn, axis=1), 1)

    def scatter_rows(parts):
        total = parts[0]
        for i in range(1, slots):
            total = total + swap_with(parts[i].astype(bf16), "tensor", i).astype(f32)
        return total

    def gather_rows(block):
        return [block] + [swap_with(block, "tensor", i) for i in range(1, slots)]

    order = list(range(1, slots)) + [0]
    attn_parts = [None] * slots
    for i in order:
        attn_parts[i] = dot(attn[i * share : (i + 1) * share], o_full)
    x1 = x_share + scatter_rows(attn_parts)
    mean2 = jnp.mean(x1, axis=-1, keepdims=True)
    cent2 = x1 - mean2
    inv2 = lax.rsqrt(jnp.mean(cent2 * cent2, axis=-1, keepdims=True) + EPS)
    unit2 = cent2 * inv2
    h2 = gather_rows((unit2 * gain_two + shift_two).astype(bf16))

    hidden = []
    gate_up_grad = []
    norm2_parts = []
    for i in range(slots):
        dm = dot(cot[i], down_full, NT)
        gu = dot(h2[i], gate_up)
        g = gu[:, :hidden_here]
        u = gu[:, hidden_here:]
        sig = jax.nn.sigmoid(g)
        act = g * sig
        hidden.append((act * u).astype(bf16))
        dg = (dm * u * sig * (1.0 + g * (1.0 - sig))).astype(bf16)
        du = (dm * act).astype(bf16)
        gate_up_grad.append(jnp.concatenate([dg, du], axis=1))
        norm2_parts.append(dot(gate_up_grad[i], gate_up, NT))
    dh2 = scatter_rows(norm2_parts)

    out_parts = [dot(hidden[i], down_full) for i in range(slots)]
    output = by_shard((x1 + scatter_rows(out_parts)).astype(bf16))[None]

    cot_share = cot[0].astype(f32)
    e2 = dh2 * gain_two
    dx1 = cot_share + inv2 * (
        e2
        - jnp.mean(e2, axis=-1, keepdims=True)
        - unit2 * jnp.mean(e2 * unit2, axis=-1, keepdims=True)
    )
    dx1b = jnp.concatenate(gather_rows(dx1.astype(bf16)), axis=0)
    d_attn = dot(dx1b, o_full, NT).astype(bf16)
    d_send = [
        lax.dynamic_slice_in_dim(d_attn, ((ctx & (groups - 1)) ^ s) * PAIR, PAIR, 1)
        for s in range(groups)
    ]
    d_pieces = [d_send[0]] + [swap_with(d_send[s % groups], "context", s) for s in range(1, ctxs)]

    full_tables = rotary_tables(jnp.arange(length, dtype=jnp.int32))
    back = attend_back(
        ids, pieces, d_pieces, o_t, lse, full_tables, groups, slots, docs, pics, bq, bk
    )
    d_qkv = [back[0]] + [swap_with(back[s], "context", s) for s in range(1, groups)]
    d_qkv = group_order(jnp.concatenate(d_qkv, axis=1), 1)

    def by_kind(x, axis):
        return [
            jnp.concatenate(
                [
                    lax.slice_in_dim(x, (3 * s + j) * PAIR, (3 * s + j + 1) * PAIR, axis=axis)
                    for s in range(groups)
                ],
                axis=axis,
            )
            for j in range(3)
        ]

    qkv_full = jnp.concatenate(
        [
            jnp.concatenate(
                [
                    w[:, s * PAIR : (s + 1) * PAIR]
                    for s in range(groups)
                    for w in pack
                ],
                axis=1,
            )
            for pack in (own_qkv, oth_qkv)
        ],
        axis=0,
    )
    norm1_parts = [None] * slots
    for i in order:
        norm1_parts[i] = dot(d_qkv[i * share : (i + 1) * share], qkv_full, NT)
    dh1 = scatter_rows(norm1_parts)

    mean1 = jnp.mean(x_share, axis=-1, keepdims=True)
    cent1 = x_share - mean1
    inv1 = lax.rsqrt(jnp.mean(cent1 * cent1, axis=-1, keepdims=True) + EPS)
    unit1 = cent1 * inv1
    e1 = dh1 * gain_one
    tokens_grad = dx1 + inv1 * (
        e1
        - jnp.mean(e1, axis=-1, keepdims=True)
        - unit1 * jnp.mean(e1 * unit1, axis=-1, keepdims=True)
    )
    tokens_grad = by_shard(tokens_grad)[None]

    def scatter_context(mine, axis):
        first = lax.dynamic_slice_in_dim(mine, ctx * quarter, quarter, axis).astype(f32)
        for s in range(1, ctxs):
            block = lax.dynamic_slice_in_dim(mine, (ctx ^ s) * quarter, quarter, axis)
            first = first + swap_with(block, "context", s).astype(f32)
        return first

    def reduce_grad(mine, theirs, axis):
        theirs = other_half(theirs.astype(bf16))
        return scatter_context((mine + theirs.astype(f32)).astype(bf16), axis)

    h2_all = jnp.concatenate(h2, axis=0)
    hidden_all = jnp.concatenate(hidden, axis=0)
    gu_all = jnp.concatenate(gate_up_grad, axis=0)
    cot_all = jnp.concatenate(cot, axis=0)
    down_grad = reduce_grad(
        dot(hidden_all, cot_all[:, :half], TN), dot(hidden_all, cot_all[:, half:], TN), 1
    )
    gu_grad = reduce_grad(dot(h2_all[:, :half], gu_all, TN), dot(h2_all[:, half:], gu_all, TN), 0)
    o_grad = reduce_grad(
        dot(attn, dx1b[:, :half], TN), dot(attn, dx1b[:, half:], TN), 1
    )
    qkv_grad = reduce_grad(dot(h1[:, :half], d_qkv, TN), dot(h1[:, half:], d_qkv, TN), 0)
    q_grad, k_grad, v_grad = by_kind(qkv_grad, 1)

    bias_row = jnp.sum(d_qkv.astype(f32), axis=0, keepdims=True)
    q_b, k_b, v_b = (x[0] for x in by_kind(bias_row, 1))
    bias = jnp.stack([q_b, k_b, v_b])
    bias = sum_over(sum_over(bias, "shard"), "context")
    k_b = bias[1].reshape(heads_here, HEAD_DIM)[:, :ROT].reshape(heads_here * ROT)

    norms = jnp.stack(
        [
            jnp.sum(dh1 * unit1, axis=0),
            jnp.sum(dh1, axis=0),
            jnp.sum(dh2 * unit2, axis=0),
            jnp.sum(dh2, axis=0),
        ]
    )
    norms = by_shard(norms)
    for axis in ("shard", "context", "tensor"):
        norms = sum_over(norms, axis)
    return (
        output,
        tokens_grad,
        norms[0],
        norms[1],
        q_grad,
        k_grad,
        v_grad,
        bias[0],
        k_b,
        bias[2],
        o_grad,
        norms[2],
        norms[3],
        gu_grad[:, :hidden_here],
        gu_grad[:, hidden_here:],
        down_grad,
    )


def solution(mesh):
    tokens = P("shard", "context", None)
    inward = P("shard", "tensor")
    outward = P("tensor", "shard")
    vector = P("tensor")
    placed = (
        tokens,
        P(),
        P(),
        inward,
        inward,
        inward,
        vector,
        vector,
        vector,
        outward,
        P(),
        P(),
        inward,
        inward,
        outward,
        tokens,
        P("shard", None),
        P("shard", None),
    )
    share = P("shard", ("context", "tensor"), None)
    grad_in = P(("shard", "context"), "tensor")
    grad_out = P("tensor", ("shard", "context"))
    return jax.shard_map(
        local,
        mesh=mesh,
        in_specs=placed,
        out_specs=(
            share,
            share,
            P(),
            P(),
            grad_in,
            grad_in,
            grad_in,
            vector,
            vector,
            vector,
            grad_out,
            P(),
            P(),
            grad_in,
            grad_in,
            grad_out,
        ),
        check_vma=False,
    )
```

```python
import functools

import jax
import jax.numpy as jnp
from jax import lax
from jax.experimental import pallas as pl
from jax.experimental.pallas import tpu as pltpu
from jax.sharding import PartitionSpec as P

HEAD_DIM = 64
ROT = 16
SPAN = 256
PAIR = 128
EPS = 1e-05
LOW = -1e30
LOWER = -2e30
SCALE = HEAD_DIM ** (-0.5)

f32 = jnp.float32
bf16 = jnp.bfloat16


NT = (((1,), (1,)), ((), ()))
NN = (((1,), (0,)), ((), ()))
TN = (((0,), (0,)), ((), ()))


def dot(a, b, dims=NN):
    return lax.dot_general(a, b, dims, preferred_element_type=f32)


def swap_with(x, axis, bit):
    size = lax.axis_size(axis)
    return lax.ppermute(x, axis, [(i, i ^ bit) for i in range(size)])


def sum_over(x, axis):
    size = lax.axis_size(axis)
    bit = 1
    while bit < size:
        x = x + swap_with(x, axis, bit)
        bit *= 2
    return x


def rotary_tables(positions):
    half = ROT // 2
    freq = 10000.0 ** (-(2.0 * jnp.arange(half).astype(f32)) / ROT)
    angles = freq[:, None] * positions.astype(f32)[None, :]
    parts = jnp.concatenate([jnp.cos(angles), jnp.sin(angles)], axis=0)
    lane = jnp.arange(PAIR) % HEAD_DIM
    row = jnp.arange(half)[:, None]
    hit = (lane[None, :] % half == row) & (lane[None, :] < ROT)
    spread_cos = jnp.concatenate([hit, jnp.zeros_like(hit)], axis=0).astype(f32)
    sign = jnp.where(lane < half, -1.0, 1.0)[None, :]
    spread_sin = jnp.concatenate([jnp.zeros_like(hit), hit], axis=0).astype(f32) * sign
    expand = functools.partial(
        lax.dot_general,
        dimension_numbers=TN,
        precision=lax.Precision.HIGHEST,
        preferred_element_type=f32,
    )
    rest = jnp.where(lane < ROT, 0.0, 1.0).astype(f32)
    return expand(parts, spread_cos) + rest[None, :], expand(parts, spread_sin)


def swap_halves(x):
    lane = lax.broadcasted_iota(jnp.int32, x.shape, 1) % HEAD_DIM
    return jnp.where(lane < ROT // 2, pltpu.roll(x, PAIR - ROT // 2, 1), pltpu.roll(x, ROT // 2, 1))


def project_kernel(
    groups,
    ids,
    x_own,
    x_oth,
    gain_own,
    gain_oth,
    shift_own,
    shift_oth,
    wq_own,
    wk_own,
    wv_own,
    wq_oth,
    wk_oth,
    wv_oth,
    q_bias,
    k_bias,
    v_bias,
    cos_ref,
    sin_ref,
    *rest,
):
    h_ref, pieces, (qs, ks, vs) = rest[0], rest[1 : 1 + groups], rest[1 + groups :]
    half = x_own.shape[1]
    a = x_own[...].astype(f32)
    b = x_oth[...].astype(f32)
    count = 1.0 / (2 * half)
    mean = (jnp.sum(a, axis=1, keepdims=True) + jnp.sum(b, axis=1, keepdims=True)) * count
    a = a - mean
    b = b - mean
    var = (jnp.sum(a * a, axis=1, keepdims=True) + jnp.sum(b * b, axis=1, keepdims=True)) * count
    inv = lax.rsqrt(var + EPS)
    ha = (a * inv * gain_own[...].astype(f32) + shift_own[...].astype(f32)).astype(bf16)
    hb = (b * inv * gain_oth[...].astype(f32) + shift_oth[...].astype(f32)).astype(bf16)
    h_ref[:, :half] = ha
    h_ref[:, half:] = hb
    qs[...] = dot(ha, wq_own[...]) + dot(hb, wq_oth[...]) + q_bias[...]
    ks[...] = dot(ha, wk_own[...]) + dot(hb, wk_oth[...]) + k_bias[...]
    vs[...] = dot(ha, wv_own[...]) + dot(hb, wv_oth[...]) + v_bias[...]
    cos = cos_ref[...]
    sin = sin_ref[...]
    for s in range(groups):
        group = (ids[1] & (groups - 1)) ^ s
        cols = pl.ds(pl.multiple_of(group * PAIR, PAIR), PAIR)
        q = qs[:, cols]
        k = ks[:, cols]
        pieces[s][:, :PAIR] = (q * cos + swap_halves(q) * sin).astype(bf16)
        pieces[s][:, PAIR : 2 * PAIR] = (k * cos + swap_halves(k) * sin).astype(bf16)
        pieces[s][:, 2 * PAIR :] = vs[:, cols].astype(bf16)


def project(ids, tokens, gain, shift, own, other, biases, tables, groups, slots):
    rows, width = tokens.shape
    half = width // 2
    share = rows // slots
    inner = own[0].shape[1]

    def row_block(i, ids):
        return ids[2] ^ i

    whole = lambda i, ids: (0, 0)
    weight = pl.BlockSpec((half, inner), whole)
    bias = pl.BlockSpec((1, inner), whole)
    in_specs = [
        pl.BlockSpec((share, half), lambda i, ids: (row_block(i, ids), ids[0])),
        pl.BlockSpec((share, half), lambda i, ids: (row_block(i, ids), 1 - ids[0])),
        pl.BlockSpec((1, half), lambda i, ids: (0, ids[0])),
        pl.BlockSpec((1, half), lambda i, ids: (0, 1 - ids[0])),
        pl.BlockSpec((1, half), lambda i, ids: (0, ids[0])),
        pl.BlockSpec((1, half), lambda i, ids: (0, 1 - ids[0])),
    ]
    in_specs += [weight] * 6 + [bias] * 3
    in_specs += [pl.BlockSpec((share, PAIR), lambda i, ids: (row_block(i, ids), 0))] * 2
    out = pl.pallas_call(
        functools.partial(project_kernel, groups),
        grid_spec=pltpu.PrefetchScalarGridSpec(
            num_scalar_prefetch=1,
            grid=(slots,),
            in_specs=in_specs,
            out_specs=[pl.BlockSpec((share, width), lambda i, ids: (i, 0))]
            + [pl.BlockSpec((share, 3 * PAIR), lambda i, ids: (i, 0))] * groups,
            scratch_shapes=[pltpu.VMEM((share, inner), f32)] * 3,
        ),
        out_shape=[jax.ShapeDtypeStruct((rows, width), bf16)]
        + [jax.ShapeDtypeStruct((rows, 3 * PAIR), bf16)] * groups,
        compiler_params=pltpu.CompilerParams(vmem_limit_bytes=56 << 20),
        cost_estimate=pl.CostEstimate(
            flops=2 * rows * width * inner * 3,
            bytes_accessed=rows * width * 4 + 3 * width * inner * 2 + rows * inner * 6,
            transcendentals=rows,
        ),
        name="project",
    )(ids, tokens, tokens, gain, gain, shift, shift, *own, *other, *biases, *tables)
    return out[0], out[1:]


def reach(ids, p, docs, pics, length):
    start = jnp.zeros_like(p)
    end = jnp.full_like(p, length)
    for j in range(docs):
        e = ids[4 + j]
        start = jnp.where(p >= e, jnp.maximum(start, e), start)
        end = jnp.where(p < e, jnp.minimum(end, e), end)
    far = p + 1
    for j in range(pics):
        b = ids[4 + docs + j]
        inside = (p >= b) & (p < b + SPAN)
        far = jnp.where(inside, jnp.maximum(far, jnp.minimum(b + SPAN, end)), far)
    return start, far


def block_ranges(ids, first, bq, bk, docs, pics, length):
    lo_a, hi_a = reach(ids, first, docs, pics, length)
    lo_b, hi_b = reach(ids, first + (bq - 1), docs, pics, length)
    begin = lo_a // bk
    stop = (hi_b + (bk - 1)) // bk
    full_begin = jnp.clip((lo_b + (bk - 1)) // bk, begin, stop)
    full_stop = jnp.clip(hi_a // bk, full_begin, stop)
    return begin, full_begin, full_stop, stop


def piece_copies(ids, pieces, whole, sems, slots, share, outward=False):
    copies = []
    for s, piece in enumerate(pieces):
        for i in range(slots):
            first = ((ids[1] ^ s) * slots + (ids[2] ^ i)) * share
            there = whole.at[pl.ds(pl.multiple_of(first, share), share)]
            here = piece.at[pl.ds(i * share, share)]
            src, dst = (there, here) if outward else (here, there)
            copies.append(pltpu.make_async_copy(src, dst, sems.at[s * slots + i]))
    return copies


def attend_kernel(dims, ids, *refs):
    pieces, groups, slots, share, length, docs, pics, bq, bk = dims
    ins = refs[:pieces]
    outs = refs[pieces : pieces + groups]
    o_t, lse = refs[pieces + groups : pieces + groups + 2]
    qkv, vx, ob, acc, m_ref, sem_in, sem_out = refs[pieces + groups + 2 :]
    loads = piece_copies(ids, ins, qkv, sem_in, slots, share)
    for c in loads:
        c.start()
    for c in loads:
        c.wait()

    def prepare(j, _):
        rows = pl.ds(pl.multiple_of(j * bk, bk), bk)
        v_t = qkv[rows, 2 * PAIR :].astype(f32).T
        ones = jnp.ones((16, bk), bf16)
        for h in range(2):
            vx[h, :HEAD_DIM, rows] = v_t[h * HEAD_DIM : (h + 1) * HEAD_DIM].astype(bf16)
            vx[h, HEAD_DIM:, rows] = ones
        return 0

    lax.fori_loop(0, length // bk, prepare, 0)
    lane = lax.broadcasted_iota(jnp.int32, (bq, PAIR), 1)

    def query_block(i, _):
        first = i * bq
        rows = pl.ds(pl.multiple_of(first, bq), bq)
        q = qkv[rows, :PAIR].astype(f32) * SCALE
        heads = [
            jnp.where((lane < HEAD_DIM) == (h == 0), q, 0.0).astype(bf16) for h in range(2)
        ]
        for h in range(2):
            acc[h] = jnp.zeros_like(acc[h])
            m_ref[h] = jnp.full_like(m_ref[h], LOW)
        lo, hi = reach(
            ids, first + lax.broadcasted_iota(jnp.int32, (1, bq), 1), docs, pics, length
        )
        begin, full_begin, full_stop, stop = block_ranges(
            ids, first, bq, bk, docs, pics, length
        )

        def visit(masked, j, _):
            keys = pl.ds(pl.multiple_of(j * bk, bk), bk)
            k = qkv[keys, PAIR : 2 * PAIR]
            if masked:
                p = j * bk + lax.broadcasted_iota(jnp.int32, (bk, bq), 0)
                ok = (p >= lo) & (p < hi)
            for h in range(2):
                s = dot(k, heads[h], NT)
                if masked:
                    s = jnp.where(ok, s, LOWER)
                old = m_ref[h, 0:1]
                new = jnp.maximum(old, jnp.max(s, axis=0, keepdims=True))
                w = jnp.exp(s - new).astype(bf16)
                acc[h] = acc[h] * jnp.exp(old - new) + dot(vx[h, :, keys], w)
                m_ref[h, 0:1] = new
            return 0

        lax.fori_loop(begin, full_begin, functools.partial(visit, True), 0)
        lax.fori_loop(full_begin, full_stop, functools.partial(visit, False), 0)
        lax.fori_loop(full_stop, stop, functools.partial(visit, True), 0)
        for h in range(2):
            total = acc[h, HEAD_DIM : HEAD_DIM + 1]
            o_t[h * HEAD_DIM : (h + 1) * HEAD_DIM, rows] = acc[h, :HEAD_DIM] / total
            lse[h : h + 1, rows] = m_ref[h, 0:1] + jnp.log(total)
        ob[rows] = o_t[:, rows].T.astype(bf16)
        return 0

    lax.fori_loop(0, length // bq, query_block, 0)
    stores = piece_copies(ids, outs, ob, sem_out, slots, share, outward=True)
    for c in stores:
        c.start()
    for c in stores:
        c.wait()


def attend_cost(length, matmuls):
    pairs = length * length // 2
    return pl.CostEstimate(
        flops=2 * pairs * 256 * 2 * matmuls,
        bytes_accessed=length * PAIR * 2 * 8,
        transcendentals=2 * pairs,
    )


def attend(ids, pieces, groups, slots, docs, pics, bq, bk):
    rows = pieces[0].shape[0]
    n = len(pieces)
    length = rows * n
    share = rows // slots
    dims = (n, groups, slots, share, length, docs, pics, bq, bk)
    anywhere = pl.BlockSpec(memory_space=pl.ANY)
    out = pl.pallas_call(
        functools.partial(attend_kernel, dims),
        grid_spec=pltpu.PrefetchScalarGridSpec(
            num_scalar_prefetch=1,
            grid=(1,),
            in_specs=[anywhere] * n,
            out_specs=[anywhere] * groups
            + [
                pl.BlockSpec((PAIR, length), lambda i, ids: (0, 0)),
                pl.BlockSpec((8, length), lambda i, ids: (0, 0)),
            ],
            scratch_shapes=[
                pltpu.VMEM((length, 3 * PAIR), bf16),
                pltpu.VMEM((2, HEAD_DIM + 16, length), bf16),
                pltpu.VMEM((length, PAIR), bf16),
                pltpu.VMEM((2, HEAD_DIM + 16, bq), f32),
                pltpu.VMEM((2, 8, bq), f32),
                pltpu.SemaphoreType.DMA((n * slots,)),
                pltpu.SemaphoreType.DMA((groups * slots,)),
            ],
        ),
        out_shape=[jax.ShapeDtypeStruct((rows, PAIR), bf16)] * groups
        + [
            jax.ShapeDtypeStruct((PAIR, length), f32),
            jax.ShapeDtypeStruct((8, length), f32),
        ],
        compiler_params=pltpu.CompilerParams(vmem_limit_bytes=56 << 20),
        cost_estimate=attend_cost(length, 2),
        name="attend",
    )(ids, *pieces)
    return out[:groups], out[groups], out[groups + 1]


def attend_back_kernel(dims, ids, *refs):
    pieces, groups, slots, share, length, docs, pics, bq, bk = dims
    ins = refs[:pieces]
    grads = refs[pieces : 2 * pieces]
    o_t, lse, cos_ref, sin_ref = refs[2 * pieces : 2 * pieces + 4]
    outs = refs[2 * pieces + 4 : 2 * pieces + 4 + groups]
    qkv, dob, kt, dq_t, dk, dv, sem_in, sem_grad, sem_out = refs[2 * pieces + 4 + groups :]
    loads = piece_copies(ids, ins, qkv, sem_in, slots, share)
    loads += piece_copies(ids, grads, dob, sem_grad, slots, share)
    for c in loads:
        c.start()
    for c in loads:
        c.wait()

    def prepare(j, _):
        rows = pl.ds(pl.multiple_of(j * bk, bk), bk)
        kt[:, rows] = qkv[rows, PAIR : 2 * PAIR].astype(f32).T.astype(bf16)
        dk[rows] = jnp.zeros((bk, PAIR), f32)
        dv[rows] = jnp.zeros((bk, PAIR), f32)
        return 0

    lax.fori_loop(0, length // bk, prepare, 0)
    lane = lax.broadcasted_iota(jnp.int32, (bq, PAIR), 1)

    def turn_back(x, rows):
        return x * cos_ref[rows] - swap_halves(x) * sin_ref[rows]

    def query_block(i, _):
        first = i * bq
        rows = pl.ds(pl.multiple_of(first, bq), bq)
        q = qkv[rows, :PAIR].astype(f32) * SCALE
        do = dob[rows].astype(f32)
        q_of = []
        do_of = []
        for h in range(2):
            mine = (lane < HEAD_DIM) == (h == 0)
            q_of.append(jnp.where(mine, q, 0.0).astype(bf16))
            do_of.append(jnp.where(mine, do, 0.0).astype(bf16))
        prod = do.T * o_t[:, rows]
        delta = [
            jnp.sum(prod[h * HEAD_DIM : (h + 1) * HEAD_DIM], axis=0, keepdims=True)
            for h in range(2)
        ]
        dq_t[...] = jnp.zeros_like(dq_t)
        lo, hi = reach(
            ids, first + lax.broadcasted_iota(jnp.int32, (1, bq), 1), docs, pics, length
        )
        begin, full_begin, full_stop, stop = block_ranges(
            ids, first, bq, bk, docs, pics, length
        )

        def visit(masked, j, _):
            keys = pl.ds(pl.multiple_of(j * bk, bk), bk)
            k = qkv[keys, PAIR : 2 * PAIR]
            v = qkv[keys, 2 * PAIR :]
            if masked:
                p = j * bk + lax.broadcasted_iota(jnp.int32, (bk, bq), 0)
                ok = (p >= lo) & (p < hi)
            dk_sum = dk[keys]
            dv_sum = dv[keys]
            for h in range(2):
                feats = slice(h * HEAD_DIM, (h + 1) * HEAD_DIM)
                s = dot(k, q_of[h], NT)
                if masked:
                    s = jnp.where(ok, s, LOWER)
                w = jnp.exp(s - lse[h : h + 1, rows])
                dw = dot(v, do_of[h], NT)
                ds = (w * (dw - delta[h])).astype(bf16)
                dv_sum = dv_sum + dot(w.astype(bf16), do_of[h])
                dk_sum = dk_sum + dot(ds, q_of[h])
                dq_t[feats] += dot(kt[feats, keys], ds)
            dk[keys] = dk_sum
            dv[keys] = dv_sum
            return 0

        lax.fori_loop(begin, full_begin, functools.partial(visit, True), 0)
        lax.fori_loop(full_begin, full_stop, functools.partial(visit, False), 0)
        lax.fori_loop(full_stop, stop, functools.partial(visit, True), 0)
        dq = dq_t[...].T * SCALE
        qkv[rows, :PAIR] = turn_back(dq, rows).astype(bf16)
        return 0

    lax.fori_loop(0, length // bq, query_block, 0)

    def finish(j, _):
        rows = pl.ds(pl.multiple_of(j * bk, bk), bk)
        qkv[rows, PAIR : 2 * PAIR] = turn_back(dk[rows], rows).astype(bf16)
        qkv[rows, 2 * PAIR :] = dv[rows].astype(bf16)
        return 0

    lax.fori_loop(0, length // bk, finish, 0)
    stores = piece_copies(ids, outs, qkv, sem_out, slots, share, outward=True)
    for c in stores:
        c.start()
    for c in stores:
        c.wait()


def attend_back(ids, pieces, grads, o_t, lse, tables, groups, slots, docs, pics, bq, bk):
    rows = pieces[0].shape[0]
    n = len(pieces)
    length = rows * n
    share = rows // slots
    dims = (n, groups, slots, share, length, docs, pics, bq, bk)
    anywhere = pl.BlockSpec(memory_space=pl.ANY)
    once = dict(pipeline_mode=pl.Buffered(1))
    return pl.pallas_call(
        functools.partial(attend_back_kernel, dims),
        grid_spec=pltpu.PrefetchScalarGridSpec(
            num_scalar_prefetch=1,
            grid=(1,),
            in_specs=[anywhere] * (2 * n)
            + [
                pl.BlockSpec((PAIR, length), lambda i, ids: (0, 0), **once),
                pl.BlockSpec((8, length), lambda i, ids: (0, 0), **once),
                pl.BlockSpec((length, PAIR), lambda i, ids: (0, 0), **once),
                pl.BlockSpec((length, PAIR), lambda i, ids: (0, 0), **once),
            ],
            out_specs=[anywhere] * groups,
            scratch_shapes=[
                pltpu.VMEM((length, 3 * PAIR), bf16),
                pltpu.VMEM((length, PAIR), bf16),
                pltpu.VMEM((PAIR, length), bf16),
                pltpu.VMEM((PAIR, bq), f32),
                pltpu.VMEM((length, PAIR), f32),
                pltpu.VMEM((length, PAIR), f32),
                pltpu.SemaphoreType.DMA((n * slots,)),
                pltpu.SemaphoreType.DMA((n * slots,)),
                pltpu.SemaphoreType.DMA((groups * slots,)),
            ],
        ),
        out_shape=[jax.ShapeDtypeStruct((rows, 3 * PAIR), bf16)] * groups,
        compiler_params=pltpu.CompilerParams(vmem_limit_bytes=56 << 20),
        cost_estimate=attend_cost(length, 5),
        name="attend_back",
    )(ids, *pieces, *grads, o_t, lse, *tables)


def join_kernel(groups, kinds, slots, dims, ids, *refs):
    pieces = refs[:groups]
    own = refs[groups : groups + kinds]
    oth = refs[groups + kinds : groups + 2 * kinds]
    joined = refs[groups + 2 * kinds]
    parts = refs[groups + 2 * kinds + 1 :]
    inner = groups * PAIR
    half = parts[0].shape[1] // 2
    for s in range(groups):
        group = (ids[1] & (groups - 1)) ^ s
        for j in range(kinds):
            cols = pl.ds(pl.multiple_of(j * inner + group * PAIR, PAIR), PAIR)
            joined[:, cols] = pieces[s][:, j * PAIR : (j + 1) * PAIR]
    for side, weights in enumerate((own, oth)):
        total = None
        for j, w in enumerate(weights):
            term = dot(joined[:, j * inner : (j + 1) * inner], w[...], dims)
            total = term if total is None else total + term
        for i in range(slots):

            @pl.when(pl.program_id(0) == i)
            def _():
                parts[i][:, side * half : (side + 1) * half] = total.astype(parts[i].dtype)


def join(ids, pieces, own, oth, slots, dims):
    groups = len(pieces)
    kinds = len(own)
    rows = pieces[0].shape[0]
    share = rows // slots
    inner = groups * PAIR
    width = 2 * (own[0].shape[0] if dims == NT else own[0].shape[1])
    whole = lambda i, ids: (0, 0)
    by_row = lambda i, ids: (i, 0)
    out = pl.pallas_call(
        functools.partial(join_kernel, groups, kinds, slots, dims),
        grid_spec=pltpu.PrefetchScalarGridSpec(
            num_scalar_prefetch=1,
            grid=(slots,),
            in_specs=[pl.BlockSpec((share, kinds * PAIR), by_row)] * groups
            + [pl.BlockSpec(own[0].shape, whole)] * (2 * kinds),
            out_specs=[pl.BlockSpec((share, kinds * inner), by_row)]
            + [pl.BlockSpec((share, width), whole)] * slots,
        ),
        out_shape=[jax.ShapeDtypeStruct((rows, kinds * inner), bf16)]
        + [jax.ShapeDtypeStruct((share, width), f32 if i == 0 else bf16) for i in range(slots)],
        compiler_params=pltpu.CompilerParams(vmem_limit_bytes=44 << 20),
        cost_estimate=pl.CostEstimate(
            flops=2 * rows * width * inner * kinds,
            bytes_accessed=rows * width * 3 + kinds * (width * inner * 2 + rows * inner * 4),
            transcendentals=0,
        ),
    )(ids, *pieces, *own, *oth)
    return out[0], out[1:]


def fill(blocks, axis, origin):
    shape = list(blocks[0].shape)
    size = shape[axis]
    shape[axis] = size * len(blocks)
    out = jnp.zeros(shape, blocks[0].dtype)
    for i, block in enumerate(blocks):
        out = lax.dynamic_update_slice_in_dim(out, block, origin + i * size, axis)
    return out


def hold(*groups):
    return lax.optimization_barrier(groups)


def local(
    tokens,
    ln1_gain,
    ln1_shift,
    q_weight,
    k_weight,
    v_weight,
    q_bias,
    k_bias,
    v_bias,
    o_weight,
    ln2_gain,
    ln2_shift,
    gate_weight,
    up_weight,
    down_weight,
    cotangent,
    doc_lengths,
    picture_starts,
):
    me = lax.axis_index("shard")
    ctx = lax.axis_index("context")
    ctxs = lax.axis_size("context")
    ten = lax.axis_index("tensor")
    slots = lax.axis_size("tensor")
    rows, width = tokens.shape[1:]
    half = width // 2
    share = rows // slots
    inner = q_weight.shape[1]
    groups = inner // PAIR
    heads_here = inner // HEAD_DIM
    docs = doc_lengths.shape[1]
    pics = picture_starts.shape[1]
    length = ctxs * rows
    quarter = half // ctxs
    bq = min(512, rows)
    bk = min(512, rows)
    assert ctxs % groups == 0 and ctxs & (ctxs - 1) == 0 and slots & (slots - 1) == 0

    def by_shard(x):
        turned = jnp.concatenate([x[..., half:], x[..., :half]], axis=-1)
        return jnp.where(me == 0, x, turned)

    def slot_rows(x, i):
        return lax.dynamic_slice_in_dim(x, (ten ^ i) * share, share, 0)

    def other_half(x):
        return swap_with(x, "shard", 1)

    origin = jnp.minimum(me, 0)

    own_qkv = (q_weight, k_weight, v_weight)
    oth_qkv = tuple(other_half(w) for w in own_qkv)
    doc_ends = jnp.cumsum(doc_lengths[0])
    ids = jnp.concatenate(
        [
            jnp.stack([me, ctx, ten, ctx * 0]).astype(jnp.int32),
            doc_ends.astype(jnp.int32),
            picture_starts[0].astype(jnp.int32),
        ]
    )
    local_tables = rotary_tables(ctx * rows + jnp.arange(rows, dtype=jnp.int32))
    k_bias_wide = jnp.pad(
        k_bias.astype(f32).reshape(heads_here, ROT), ((0, 0), (0, HEAD_DIM - ROT))
    ).reshape(1, inner)
    h1, send = project(
        ids,
        tokens[0],
        ln1_gain.reshape(1, width),
        ln1_shift.reshape(1, width),
        own_qkv,
        oth_qkv,
        (q_bias.astype(f32).reshape(1, inner), k_bias_wide, v_bias.astype(f32).reshape(1, inner)),
        local_tables,
        groups,
        slots,
    )

    (send, later) = hold(
        send,
        (
            o_weight,
            gate_weight,
            up_weight,
            down_weight,
            cotangent[0],
            tokens[0],
            jnp.arange(length, dtype=jnp.int32),
        ),
    )
    o_weight, gate_weight, up_weight, down_weight, cot_rows, x_rows, positions = later
    pieces = [send[0]] + [swap_with(send[s % groups], "context", s) for s in range(1, ctxs)]
    down_oth, o_oth, gate_oth, up_oth = map(
        other_half, (down_weight, o_weight, gate_weight, up_weight)
    )
    full_tables = rotary_tables(positions)
    cot_all = by_shard(fill([slot_rows(cot_rows, i) for i in range(slots)], 0, origin))
    x_share = by_shard(slot_rows(x_rows, 0)).astype(f32)
    down_full = fill([down_weight, down_oth], 1, origin)
    o_full = fill([o_weight, o_oth], 1, origin)
    dm_all = dot(cot_all, down_full, NT)
    gate_full = fill([gate_weight, gate_oth], 0, origin)
    up_full = fill([up_weight, up_oth], 0, origin)
    gain_two = by_shard(ln2_gain.astype(f32))
    shift_two = by_shard(ln2_shift.astype(f32))
    gain_one = by_shard(ln1_gain.astype(f32))
    pieces, ready = hold(
        pieces, (down_full, o_full, gate_full, up_full, cot_all, dm_all, full_tables, x_share)
    )
    down_full, o_full, gate_full, up_full, cot_all, dm_all, full_tables, x_share = ready

    attn_send, o_t, lse = attend(ids, pieces, groups, slots, docs, pics, bq, bk)
    attn, attn_parts = join(
        ids,
        [attn_send[0]] + [swap_with(attn_send[s], "context", s) for s in range(1, groups)],
        (o_weight,),
        (o_oth,),
        slots,
        NN,
    )

    def send_rows(parts):
        return [swap_with(parts[i].astype(bf16), "tensor", i) for i in range(1, slots)]

    def add_rows(own, received):
        for part in received:
            own = own + part.astype(f32)
        return own

    def gather_rows(block):
        return [block] + [swap_with(block, "tensor", i) for i in range(1, slots)]

    def slot_of(x, i):
        return x[i * share : (i + 1) * share]

    x1 = x_share + add_rows(attn_parts[0], send_rows(attn_parts))
    mean2 = jnp.mean(x1, axis=-1, keepdims=True)
    cent2 = x1 - mean2
    inv2 = lax.rsqrt(jnp.mean(cent2 * cent2, axis=-1, keepdims=True) + EPS)
    unit2 = cent2 * inv2
    h2 = gather_rows((unit2 * gain_two + shift_two).astype(bf16))

    hidden = []
    gate_grad = []
    up_grad = []
    norm2_parts = []
    dh2_received = []
    for i in range(slots):
        dm = slot_of(dm_all, i)
        g = dot(h2[i], gate_full)
        u = dot(h2[i], up_full)
        sig = jax.nn.sigmoid(g)
        act = g * sig
        hidden.append((act * u).astype(bf16))
        gate_grad.append((dm * u * sig * (1.0 + g * (1.0 - sig))).astype(bf16))
        up_grad.append((dm * act).astype(bf16))
        part = dot(gate_grad[i], gate_full, NT) + dot(up_grad[i], up_full, NT)
        norm2_parts.append(part if i == 0 else part.astype(bf16))
        if i + 1 < slots:
            norm2_parts[i], h2[i + 1] = hold(norm2_parts[i], h2[i + 1])
        if i > 0:
            dh2_received.append(swap_with(norm2_parts[i], "tensor", i))

    def blocks_of(mine, theirs, axis):
        def block(x, d):
            return lax.dynamic_slice_in_dim(x, (ctx ^ d) * quarter, quarter, axis).astype(f32)

        return {d: block(mine, d) + block(theirs, d) for d in range(ctxs)}

    def scatter_step(parts, bit):
        parts = dict(parts)
        for d in sorted((d for d in parts if d & bit), reverse=True):
            parts[d ^ bit] += swap_with(parts.pop(d).astype(bf16), "context", bit).astype(f32)
        return parts

    def scatter_rest(parts):
        bit = 2
        while bit < ctxs:
            parts = scatter_step(parts, bit)
            bit *= 2
        return parts[0]

    h2_all, gate_all, up_all, hidden_all = (
        fill(blocks, 0, origin) for blocks in (h2, gate_grad, up_grad, hidden)
    )

    norm2_parts, h2_all, gate_all, up_all = hold(norm2_parts, h2_all, gate_all, up_all)
    gate_theirs = dot(h2_all[:, half:], gate_all, TN).astype(bf16)
    up_theirs = dot(h2_all[:, half:], up_all, TN).astype(bf16)
    h2_all, gate_theirs, up_theirs = hold(h2_all, gate_theirs, up_theirs)
    gate_theirs = other_half(gate_theirs)
    up_theirs = other_half(up_theirs)
    gate_mine = dot(h2_all[:, :half], gate_all, TN).astype(bf16)
    up_mine = dot(h2_all[:, :half], up_all, TN).astype(bf16)
    dh2_received, norm2_own, gate_mine, up_mine, gate_theirs, up_theirs = hold(
        dh2_received, norm2_parts[0], gate_mine, up_mine, gate_theirs, up_theirs
    )
    gate_parts = scatter_step(blocks_of(gate_mine, gate_theirs, 0), 1)
    up_parts = scatter_step(blocks_of(up_mine, up_theirs, 0), 1)
    dh2 = add_rows(norm2_own, dh2_received)
    cot_share = slot_of(cot_all, 0).astype(f32)
    e2 = dh2 * gain_two
    dx1 = cot_share + inv2 * (
        e2
        - jnp.mean(e2, axis=-1, keepdims=True)
        - unit2 * jnp.mean(e2 * unit2, axis=-1, keepdims=True)
    )
    dx1_slots = gather_rows(dx1.astype(bf16))

    hidden_all, cot_all, dx1_own = hold(hidden_all, cot_all, dx1_slots[0])
    down_theirs = dot(hidden_all, cot_all[:, half:], TN).astype(bf16)
    down_mine = dot(hidden_all, cot_all[:, :half], TN).astype(bf16)
    out_all = dot(hidden_all, down_full).astype(bf16)
    down_theirs = other_half(down_theirs)
    dx1_rest, dx1_own, out_all, down_mine = hold(dx1_slots[1:], dx1_own, out_all, down_mine)
    dx1b = fill([dx1_own] + dx1_rest, 0, origin)
    d_attn = dot(dx1b, o_full, NT).astype(bf16)
    d_send = [
        lax.dynamic_slice_in_dim(d_attn, ((ctx & (groups - 1)) ^ s) * PAIR, PAIR, 1)
        for s in range(groups)
    ]
    d_send, dx1b = hold(d_send, dx1b)
    d_pieces = [d_send[0]] + [swap_with(d_send[s % groups], "context", s) for s in range(1, ctxs)]

    o_theirs = dot(attn, dx1b[:, half:], TN).astype(bf16)
    o_mine = dot(attn, dx1b[:, :half], TN).astype(bf16)
    o_theirs = other_half(o_theirs)

    d_pieces, out_all, o_mine, o_theirs, down_mine, down_theirs, gate_parts, up_parts = hold(
        d_pieces, out_all, o_mine, o_theirs, down_mine, down_theirs, gate_parts, up_parts
    )
    out_received = send_rows([slot_of(out_all, i) for i in range(slots)])
    gate_out = scatter_rest(gate_parts)
    up_out = scatter_rest(up_parts)
    down_parts = scatter_step(blocks_of(down_mine, down_theirs, 1), 1)
    back = attend_back(
        ids, pieces, d_pieces, o_t, lse, full_tables, groups, slots, docs, pics, bq, bk
    )
    back_rest = [swap_with(back[s], "context", s) for s in range(1, groups)]

    back_own, out_received, down_parts, o_mine = hold(back[0], out_received, down_parts, o_mine)
    output = by_shard((x1 + add_rows(slot_of(out_all, 0).astype(f32), out_received)).astype(bf16))[None]
    o_parts = scatter_step(blocks_of(o_mine, o_theirs, 1), 1)
    down_grad = scatter_rest(down_parts)
    o_grad = scatter_rest(o_parts)
    back_rest, output = hold(back_rest, output)

    d_qkv, norm1_parts = join(ids, [back_own] + back_rest, own_qkv, oth_qkv, slots, NT)
    norm1_parts, d_qkv = hold(norm1_parts, d_qkv)
    dh1_received = send_rows(norm1_parts)
    qkv_theirs = other_half(dot(h1[:, half:], d_qkv, TN).astype(bf16))
    qkv_mine = dot(h1[:, :half], d_qkv, TN).astype(bf16)
    qkv_grad = scatter_rest(scatter_step(blocks_of(qkv_mine, qkv_theirs, 0), 1))
    bias = jnp.sum(d_qkv.astype(f32), axis=0, keepdims=True)
    bias = sum_over(sum_over(bias, "shard"), "context")[0]
    dh1_received, qkv_mine = hold(dh1_received, qkv_mine)
    dh1 = add_rows(norm1_parts[0], dh1_received)

    mean1 = jnp.mean(x_share, axis=-1, keepdims=True)
    cent1 = x_share - mean1
    inv1 = lax.rsqrt(jnp.mean(cent1 * cent1, axis=-1, keepdims=True) + EPS)
    unit1 = cent1 * inv1
    e1 = dh1 * gain_one
    tokens_grad = dx1 + inv1 * (
        e1
        - jnp.mean(e1, axis=-1, keepdims=True)
        - unit1 * jnp.mean(e1 * unit1, axis=-1, keepdims=True)
    )
    tokens_grad = by_shard(tokens_grad)[None]

    k_bias_grad = bias[inner : 2 * inner].reshape(heads_here, HEAD_DIM)[:, :ROT]
    norms = jnp.stack(
        [
            jnp.sum(dh1 * unit1, axis=0),
            jnp.sum(dh1, axis=0),
            jnp.sum(dh2 * unit2, axis=0),
            jnp.sum(dh2, axis=0),
        ]
    )
    norms = by_shard(norms)
    for axis in ("shard", "context", "tensor"):
        norms = sum_over(norms, axis)
    return (
        output,
        tokens_grad,
        norms[0],
        norms[1],
        qkv_grad[:, :inner],
        qkv_grad[:, inner : 2 * inner],
        qkv_grad[:, 2 * inner :],
        bias[:inner],
        k_bias_grad.reshape(heads_here * ROT),
        bias[2 * inner :],
        o_grad,
        norms[2],
        norms[3],
        gate_out,
        up_out,
        down_grad,
    )


def solution(mesh):
    tokens = P("shard", "context", None)
    inward = P("shard", "tensor")
    outward = P("tensor", "shard")
    vector = P("tensor")
    placed = (
        tokens,
        P(),
        P(),
        inward,
        inward,
        inward,
        vector,
        vector,
        vector,
        outward,
        P(),
        P(),
        inward,
        inward,
        outward,
        tokens,
        P("shard", None),
        P("shard", None),
    )
    share = P("shard", ("context", "tensor"), None)
    grad_in = P(("shard", "context"), "tensor")
    grad_out = P("tensor", ("shard", "context"))

    return jax.shard_map(
        local,
        mesh=mesh,
        in_specs=placed,
        out_specs=(
            share,
            share,
            P(),
            P(),
            grad_in,
            grad_in,
            grad_in,
            vector,
            vector,
            vector,
            grad_out,
            P(),
            P(),
            grad_in,
            grad_in,
            grad_out,
        ),
        check_vma=False,
    )
```

```python
import functools

import jax
import jax.numpy as jnp
from jax import lax
from jax.experimental import pallas as pl
from jax.experimental.pallas import tpu as pltpu
from jax.sharding import PartitionSpec as P

HEAD_DIM = 64
ROT = 16
SPAN = 256
PAIR = 128
EPS = 1e-05
LOW = -1e30
LOWER = -2e30
SCALE = HEAD_DIM ** (-0.5)

f32 = jnp.float32
bf16 = jnp.bfloat16


NT = (((1,), (1,)), ((), ()))
NN = (((1,), (0,)), ((), ()))
TN = (((0,), (0,)), ((), ()))


def dot(a, b, dims=NN):
    return lax.dot_general(a, b, dims, preferred_element_type=f32)


def swap_with(x, axis, bit):
    size = lax.axis_size(axis)
    return lax.ppermute(x, axis, [(i, i ^ bit) for i in range(size)])


def sum_over(x, axis):
    size = lax.axis_size(axis)
    bit = 1
    while bit < size:
        x = x + swap_with(x, axis, bit)
        bit *= 2
    return x


def rotary_tables(positions):
    half = ROT // 2
    freq = 10000.0 ** (-(2.0 * jnp.arange(half).astype(f32)) / ROT)
    angles = freq[:, None] * positions.astype(f32)[None, :]
    parts = jnp.concatenate([jnp.cos(angles), jnp.sin(angles)], axis=0)
    lane = jnp.arange(PAIR) % HEAD_DIM
    row = jnp.arange(half)[:, None]
    hit = (lane[None, :] % half == row) & (lane[None, :] < ROT)
    spread_cos = jnp.concatenate([hit, jnp.zeros_like(hit)], axis=0).astype(f32)
    sign = jnp.where(lane < half, -1.0, 1.0)[None, :]
    spread_sin = jnp.concatenate([jnp.zeros_like(hit), hit], axis=0).astype(f32) * sign
    expand = functools.partial(
        lax.dot_general,
        dimension_numbers=TN,
        precision=lax.Precision.HIGHEST,
        preferred_element_type=f32,
    )
    rest = jnp.where(lane < ROT, 0.0, 1.0).astype(f32)
    return expand(parts, spread_cos) + rest[None, :], expand(parts, spread_sin)


def swap_halves(x):
    lane = lax.broadcasted_iota(jnp.int32, x.shape, 1) % HEAD_DIM
    return jnp.where(lane < ROT // 2, pltpu.roll(x, PAIR - ROT // 2, 1), pltpu.roll(x, ROT // 2, 1))


def project_kernel(
    groups,
    ids,
    x_own,
    x_oth,
    gain_own,
    gain_oth,
    shift_own,
    shift_oth,
    wq_own,
    wk_own,
    wv_own,
    wq_oth,
    wk_oth,
    wv_oth,
    q_bias,
    k_bias,
    v_bias,
    cos_ref,
    sin_ref,
    *rest,
):
    h_ref, pieces, (qs, ks, vs) = rest[0], rest[1 : 1 + groups], rest[1 + groups :]
    half = x_own.shape[1]
    a = x_own[...].astype(f32)
    b = x_oth[...].astype(f32)
    count = 1.0 / (2 * half)
    mean = (jnp.sum(a, axis=1, keepdims=True) + jnp.sum(b, axis=1, keepdims=True)) * count
    a = a - mean
    b = b - mean
    var = (jnp.sum(a * a, axis=1, keepdims=True) + jnp.sum(b * b, axis=1, keepdims=True)) * count
    inv = lax.rsqrt(var + EPS)
    ha = (a * inv * gain_own[...].astype(f32) + shift_own[...].astype(f32)).astype(bf16)
    hb = (b * inv * gain_oth[...].astype(f32) + shift_oth[...].astype(f32)).astype(bf16)
    h_ref[:, :half] = ha
    h_ref[:, half:] = hb
    qs[...] = dot(ha, wq_own[...]) + dot(hb, wq_oth[...]) + q_bias[...]
    ks[...] = dot(ha, wk_own[...]) + dot(hb, wk_oth[...]) + k_bias[...]
    vs[...] = dot(ha, wv_own[...]) + dot(hb, wv_oth[...]) + v_bias[...]
    cos = cos_ref[...]
    sin = sin_ref[...]
    for s in range(groups):
        group = (ids[1] & (groups - 1)) ^ s
        cols = pl.ds(pl.multiple_of(group * PAIR, PAIR), PAIR)
        q = qs[:, cols]
        k = ks[:, cols]
        pieces[s][:, :PAIR] = (q * cos + swap_halves(q) * sin).astype(bf16)
        pieces[s][:, PAIR : 2 * PAIR] = (k * cos + swap_halves(k) * sin).astype(bf16)
        pieces[s][:, 2 * PAIR :] = vs[:, cols].astype(bf16)


def project(ids, tokens, gain, shift, own, other, biases, tables, groups, slots):
    rows, width = tokens.shape
    half = width // 2
    share = rows // slots
    inner = own[0].shape[1]

    def row_block(i, ids):
        return ids[2] ^ i

    whole = lambda i, ids: (0, 0)
    weight = pl.BlockSpec((half, inner), whole)
    bias = pl.BlockSpec((1, inner), whole)
    in_specs = [
        pl.BlockSpec((share, half), lambda i, ids: (row_block(i, ids), ids[0])),
        pl.BlockSpec((share, half), lambda i, ids: (row_block(i, ids), 1 - ids[0])),
        pl.BlockSpec((1, half), lambda i, ids: (0, ids[0])),
        pl.BlockSpec((1, half), lambda i, ids: (0, 1 - ids[0])),
        pl.BlockSpec((1, half), lambda i, ids: (0, ids[0])),
        pl.BlockSpec((1, half), lambda i, ids: (0, 1 - ids[0])),
    ]
    in_specs += [weight] * 6 + [bias] * 3
    in_specs += [pl.BlockSpec((share, PAIR), lambda i, ids: (row_block(i, ids), 0))] * 2
    out = pl.pallas_call(
        functools.partial(project_kernel, groups),
        grid_spec=pltpu.PrefetchScalarGridSpec(
            num_scalar_prefetch=1,
            grid=(slots,),
            in_specs=in_specs,
            out_specs=[pl.BlockSpec((share, width), lambda i, ids: (i, 0))]
            + [pl.BlockSpec((share, 3 * PAIR), lambda i, ids: (i, 0))] * groups,
            scratch_shapes=[pltpu.VMEM((share, inner), f32)] * 3,
        ),
        out_shape=[jax.ShapeDtypeStruct((rows, width), bf16)]
        + [jax.ShapeDtypeStruct((rows, 3 * PAIR), bf16)] * groups,
        compiler_params=pltpu.CompilerParams(vmem_limit_bytes=56 << 20),
        cost_estimate=pl.CostEstimate(
            flops=2 * rows * width * inner * 3,
            bytes_accessed=rows * width * 4 + 3 * width * inner * 2 + rows * inner * 6,
            transcendentals=rows,
        ),
        name="project",
    )(ids, tokens, tokens, gain, gain, shift, shift, *own, *other, *biases, *tables)
    return out[0], out[1:]


def reach(ids, p, docs, pics, length):
    start = jnp.zeros_like(p)
    end = jnp.full_like(p, length)
    for j in range(docs):
        e = ids[4 + j]
        start = jnp.where(p >= e, jnp.maximum(start, e), start)
        end = jnp.where(p < e, jnp.minimum(end, e), end)
    far = p + 1
    for j in range(pics):
        b = ids[4 + docs + j]
        inside = (p >= b) & (p < b + SPAN)
        far = jnp.where(inside, jnp.maximum(far, jnp.minimum(b + SPAN, end)), far)
    return start, far


def block_ranges(ids, first, bq, bk, docs, pics, length):
    lo_a, hi_a = reach(ids, first, docs, pics, length)
    lo_b, hi_b = reach(ids, first + (bq - 1), docs, pics, length)
    begin = lo_a // bk
    stop = (hi_b + (bk - 1)) // bk
    full_begin = jnp.clip((lo_b + (bk - 1)) // bk, begin, stop)
    full_stop = jnp.clip(hi_a // bk, full_begin, stop)
    return begin, full_begin, full_stop, stop


def piece_copies(ids, pieces, whole, sems, slots, share, outward=False):
    copies = []
    for s, piece in enumerate(pieces):
        for i in range(slots):
            first = ((ids[1] ^ s) * slots + (ids[2] ^ i)) * share
            there = whole.at[pl.ds(pl.multiple_of(first, share), share)]
            here = piece.at[pl.ds(i * share, share)]
            src, dst = (there, here) if outward else (here, there)
            copies.append(pltpu.make_async_copy(src, dst, sems.at[s * slots + i]))
    return copies


def attend_kernel(dims, ids, *refs):
    pieces, groups, slots, share, length, docs, pics, bq, bk = dims
    ins = refs[:pieces]
    outs = refs[pieces : pieces + groups]
    o_t, lse = refs[pieces + groups : pieces + groups + 2]
    qkv, vx, ob, acc, m_ref, sem_in, sem_out = refs[pieces + groups + 2 :]
    loads = piece_copies(ids, ins, qkv, sem_in, slots, share)
    for c in loads:
        c.start()
    for c in loads:
        c.wait()

    def prepare(j, _):
        rows = pl.ds(pl.multiple_of(j * bk, bk), bk)
        v_t = qkv[rows, 2 * PAIR :].astype(f32).T
        ones = jnp.ones((16, bk), bf16)
        for h in range(2):
            vx[h, :HEAD_DIM, rows] = v_t[h * HEAD_DIM : (h + 1) * HEAD_DIM].astype(bf16)
            vx[h, HEAD_DIM:, rows] = ones
        return 0

    lax.fori_loop(0, length // bk, prepare, 0)
    lane = lax.broadcasted_iota(jnp.int32, (bq, PAIR), 1)

    def query_block(i, _):
        first = i * bq
        rows = pl.ds(pl.multiple_of(first, bq), bq)
        q = qkv[rows, :PAIR].astype(f32) * SCALE
        heads = [
            jnp.where((lane < HEAD_DIM) == (h == 0), q, 0.0).astype(bf16) for h in range(2)
        ]
        for h in range(2):
            acc[h] = jnp.zeros_like(acc[h])
            m_ref[h] = jnp.full_like(m_ref[h], LOW)
        lo, hi = reach(
            ids, first + lax.broadcasted_iota(jnp.int32, (1, bq), 1), docs, pics, length
        )
        begin, full_begin, full_stop, stop = block_ranges(
            ids, first, bq, bk, docs, pics, length
        )

        def visit(masked, j, _):
            keys = pl.ds(pl.multiple_of(j * bk, bk), bk)
            k = qkv[keys, PAIR : 2 * PAIR]
            if masked:
                p = j * bk + lax.broadcasted_iota(jnp.int32, (bk, bq), 0)
                ok = (p >= lo) & (p < hi)
            for h in range(2):
                s = dot(k, heads[h], NT)
                if masked:
                    s = jnp.where(ok, s, LOWER)
                old = m_ref[h, 0:1]
                new = jnp.maximum(old, jnp.max(s, axis=0, keepdims=True))
                w = jnp.exp(s - new).astype(bf16)
                acc[h] = acc[h] * jnp.exp(old - new) + dot(vx[h, :, keys], w)
                m_ref[h, 0:1] = new
            return 0

        lax.fori_loop(begin, full_begin, functools.partial(visit, True), 0)
        lax.fori_loop(full_begin, full_stop, functools.partial(visit, False), 0)
        lax.fori_loop(full_stop, stop, functools.partial(visit, True), 0)
        for h in range(2):
            total = acc[h, HEAD_DIM : HEAD_DIM + 1]
            o_t[h * HEAD_DIM : (h + 1) * HEAD_DIM, rows] = acc[h, :HEAD_DIM] / total
            lse[h : h + 1, rows] = m_ref[h, 0:1] + jnp.log(total)
        ob[rows] = o_t[:, rows].T.astype(bf16)
        return 0

    lax.fori_loop(0, length // bq, query_block, 0)
    stores = piece_copies(ids, outs, ob, sem_out, slots, share, outward=True)
    for c in stores:
        c.start()
    for c in stores:
        c.wait()


def attend_cost(length, matmuls):
    pairs = length * length // 2
    return pl.CostEstimate(
        flops=2 * pairs * 256 * 2 * matmuls,
        bytes_accessed=length * PAIR * 2 * 8,
        transcendentals=2 * pairs,
    )


def attend(ids, pieces, groups, slots, docs, pics, bq, bk):
    rows = pieces[0].shape[0]
    n = len(pieces)
    length = rows * n
    share = rows // slots
    dims = (n, groups, slots, share, length, docs, pics, bq, bk)
    anywhere = pl.BlockSpec(memory_space=pl.ANY)
    out = pl.pallas_call(
        functools.partial(attend_kernel, dims),
        grid_spec=pltpu.PrefetchScalarGridSpec(
            num_scalar_prefetch=1,
            grid=(1,),
            in_specs=[anywhere] * n,
            out_specs=[anywhere] * groups
            + [
                pl.BlockSpec((PAIR, length), lambda i, ids: (0, 0)),
                pl.BlockSpec((8, length), lambda i, ids: (0, 0)),
            ],
            scratch_shapes=[
                pltpu.VMEM((length, 3 * PAIR), bf16),
                pltpu.VMEM((2, HEAD_DIM + 16, length), bf16),
                pltpu.VMEM((length, PAIR), bf16),
                pltpu.VMEM((2, HEAD_DIM + 16, bq), f32),
                pltpu.VMEM((2, 8, bq), f32),
                pltpu.SemaphoreType.DMA((n * slots,)),
                pltpu.SemaphoreType.DMA((groups * slots,)),
            ],
        ),
        out_shape=[jax.ShapeDtypeStruct((rows, PAIR), bf16)] * groups
        + [
            jax.ShapeDtypeStruct((PAIR, length), f32),
            jax.ShapeDtypeStruct((8, length), f32),
        ],
        compiler_params=pltpu.CompilerParams(vmem_limit_bytes=56 << 20),
        cost_estimate=attend_cost(length, 2),
        name="attend",
    )(ids, *pieces)
    return out[:groups], out[groups], out[groups + 1]


def attend_back_kernel(dims, ids, *refs):
    pieces, groups, slots, share, length, docs, pics, bq, bk = dims
    ins = refs[:pieces]
    grads = refs[pieces : 2 * pieces]
    o_t, lse, cos_ref, sin_ref = refs[2 * pieces : 2 * pieces + 4]
    outs = refs[2 * pieces + 4 : 2 * pieces + 4 + groups]
    qkv, dob, kt, dq_t, dk, dv, sem_in, sem_grad, sem_out = refs[2 * pieces + 4 + groups :]
    loads = piece_copies(ids, ins, qkv, sem_in, slots, share)
    loads += piece_copies(ids, grads, dob, sem_grad, slots, share)
    for c in loads:
        c.start()
    for c in loads:
        c.wait()

    def prepare(j, _):
        rows = pl.ds(pl.multiple_of(j * bk, bk), bk)
        kt[:, rows] = qkv[rows, PAIR : 2 * PAIR].astype(f32).T.astype(bf16)
        dk[rows] = jnp.zeros((bk, PAIR), f32)
        dv[rows] = jnp.zeros((bk, PAIR), f32)
        return 0

    lax.fori_loop(0, length // bk, prepare, 0)
    lane = lax.broadcasted_iota(jnp.int32, (bq, PAIR), 1)

    def turn_back(x, rows):
        return x * cos_ref[rows] - swap_halves(x) * sin_ref[rows]

    def query_block(i, _):
        first = i * bq
        rows = pl.ds(pl.multiple_of(first, bq), bq)
        q = qkv[rows, :PAIR].astype(f32) * SCALE
        do = dob[rows].astype(f32)
        q_of = []
        do_of = []
        for h in range(2):
            mine = (lane < HEAD_DIM) == (h == 0)
            q_of.append(jnp.where(mine, q, 0.0).astype(bf16))
            do_of.append(jnp.where(mine, do, 0.0).astype(bf16))
        prod = do.T * o_t[:, rows]
        delta = [
            jnp.sum(prod[h * HEAD_DIM : (h + 1) * HEAD_DIM], axis=0, keepdims=True)
            for h in range(2)
        ]
        dq_t[...] = jnp.zeros_like(dq_t)
        lo, hi = reach(
            ids, first + lax.broadcasted_iota(jnp.int32, (1, bq), 1), docs, pics, length
        )
        begin, full_begin, full_stop, stop = block_ranges(
            ids, first, bq, bk, docs, pics, length
        )

        def visit(masked, j, _):
            keys = pl.ds(pl.multiple_of(j * bk, bk), bk)
            k = qkv[keys, PAIR : 2 * PAIR]
            v = qkv[keys, 2 * PAIR :]
            if masked:
                p = j * bk + lax.broadcasted_iota(jnp.int32, (bk, bq), 0)
                ok = (p >= lo) & (p < hi)
            dk_sum = dk[keys]
            dv_sum = dv[keys]
            for h in range(2):
                feats = slice(h * HEAD_DIM, (h + 1) * HEAD_DIM)
                s = dot(k, q_of[h], NT)
                if masked:
                    s = jnp.where(ok, s, LOWER)
                w = jnp.exp(s - lse[h : h + 1, rows])
                dw = dot(v, do_of[h], NT)
                ds = (w * (dw - delta[h])).astype(bf16)
                dv_sum = dv_sum + dot(w.astype(bf16), do_of[h])
                dk_sum = dk_sum + dot(ds, q_of[h])
                dq_t[feats] += dot(kt[feats, keys], ds)
            dk[keys] = dk_sum
            dv[keys] = dv_sum
            return 0

        lax.fori_loop(begin, full_begin, functools.partial(visit, True), 0)
        lax.fori_loop(full_begin, full_stop, functools.partial(visit, False), 0)
        lax.fori_loop(full_stop, stop, functools.partial(visit, True), 0)
        dq = dq_t[...].T * SCALE
        qkv[rows, :PAIR] = turn_back(dq, rows).astype(bf16)
        return 0

    lax.fori_loop(0, length // bq, query_block, 0)

    def finish(j, _):
        rows = pl.ds(pl.multiple_of(j * bk, bk), bk)
        qkv[rows, PAIR : 2 * PAIR] = turn_back(dk[rows], rows).astype(bf16)
        qkv[rows, 2 * PAIR :] = dv[rows].astype(bf16)
        return 0

    lax.fori_loop(0, length // bk, finish, 0)
    stores = piece_copies(ids, outs, qkv, sem_out, slots, share, outward=True)
    for c in stores:
        c.start()
    for c in stores:
        c.wait()


def attend_back(ids, pieces, grads, o_t, lse, tables, groups, slots, docs, pics, bq, bk):
    rows = pieces[0].shape[0]
    n = len(pieces)
    length = rows * n
    share = rows // slots
    dims = (n, groups, slots, share, length, docs, pics, bq, bk)
    anywhere = pl.BlockSpec(memory_space=pl.ANY)
    once = dict(pipeline_mode=pl.Buffered(1))
    return pl.pallas_call(
        functools.partial(attend_back_kernel, dims),
        grid_spec=pltpu.PrefetchScalarGridSpec(
            num_scalar_prefetch=1,
            grid=(1,),
            in_specs=[anywhere] * (2 * n)
            + [
                pl.BlockSpec((PAIR, length), lambda i, ids: (0, 0), **once),
                pl.BlockSpec((8, length), lambda i, ids: (0, 0), **once),
                pl.BlockSpec((length, PAIR), lambda i, ids: (0, 0), **once),
                pl.BlockSpec((length, PAIR), lambda i, ids: (0, 0), **once),
            ],
            out_specs=[anywhere] * groups,
            scratch_shapes=[
                pltpu.VMEM((length, 3 * PAIR), bf16),
                pltpu.VMEM((length, PAIR), bf16),
                pltpu.VMEM((PAIR, length), bf16),
                pltpu.VMEM((PAIR, bq), f32),
                pltpu.VMEM((length, PAIR), f32),
                pltpu.VMEM((length, PAIR), f32),
                pltpu.SemaphoreType.DMA((n * slots,)),
                pltpu.SemaphoreType.DMA((n * slots,)),
                pltpu.SemaphoreType.DMA((groups * slots,)),
            ],
        ),
        out_shape=[jax.ShapeDtypeStruct((rows, 3 * PAIR), bf16)] * groups,
        compiler_params=pltpu.CompilerParams(vmem_limit_bytes=56 << 20),
        cost_estimate=attend_cost(length, 5),
        name="attend_back",
    )(ids, *pieces, *grads, o_t, lse, *tables)


def join_kernel(groups, kinds, slots, dims, ids, *refs):
    pieces = refs[:groups]
    own = refs[groups : groups + kinds]
    oth = refs[groups + kinds : groups + 2 * kinds]
    joined = refs[groups + 2 * kinds]
    parts = refs[groups + 2 * kinds + 1 :]
    inner = groups * PAIR
    half = parts[0].shape[1] // 2
    for s in range(groups):
        group = (ids[1] & (groups - 1)) ^ s
        for j in range(kinds):
            cols = pl.ds(pl.multiple_of(j * inner + group * PAIR, PAIR), PAIR)
            joined[:, cols] = pieces[s][:, j * PAIR : (j + 1) * PAIR]
    for side, weights in enumerate((own, oth)):
        total = None
        for j, w in enumerate(weights):
            term = dot(joined[:, j * inner : (j + 1) * inner], w[...], dims)
            total = term if total is None else total + term
        for i in range(slots):

            @pl.when(pl.program_id(0) == i)
            def _():
                parts[i][:, side * half : (side + 1) * half] = total.astype(parts[i].dtype)


def join(ids, pieces, own, oth, slots, dims):
    groups = len(pieces)
    kinds = len(own)
    rows = pieces[0].shape[0]
    share = rows // slots
    inner = groups * PAIR
    width = 2 * (own[0].shape[0] if dims == NT else own[0].shape[1])
    whole = lambda i, ids: (0, 0)
    by_row = lambda i, ids: (i, 0)
    out = pl.pallas_call(
        functools.partial(join_kernel, groups, kinds, slots, dims),
        grid_spec=pltpu.PrefetchScalarGridSpec(
            num_scalar_prefetch=1,
            grid=(slots,),
            in_specs=[pl.BlockSpec((share, kinds * PAIR), by_row)] * groups
            + [pl.BlockSpec(own[0].shape, whole)] * (2 * kinds),
            out_specs=[pl.BlockSpec((share, kinds * inner), by_row)]
            + [pl.BlockSpec((share, width), whole)] * slots,
        ),
        out_shape=[jax.ShapeDtypeStruct((rows, kinds * inner), bf16)]
        + [jax.ShapeDtypeStruct((share, width), f32 if i == 0 else bf16) for i in range(slots)],
        compiler_params=pltpu.CompilerParams(vmem_limit_bytes=44 << 20),
        cost_estimate=pl.CostEstimate(
            flops=2 * rows * width * inner * kinds,
            bytes_accessed=rows * width * 3 + kinds * (width * inner * 2 + rows * inner * 4),
            transcendentals=0,
        ),
    )(ids, *pieces, *own, *oth)
    return out[0], out[1:]


def hold(*groups):
    return lax.optimization_barrier(groups)


def local(
    tokens,
    ln1_gain,
    ln1_shift,
    q_weight,
    k_weight,
    v_weight,
    q_bias,
    k_bias,
    v_bias,
    o_weight,
    ln2_gain,
    ln2_shift,
    gate_weight,
    up_weight,
    down_weight,
    cotangent,
    doc_lengths,
    picture_starts,
):
    me = lax.axis_index("shard")
    ctx = lax.axis_index("context")
    ctxs = lax.axis_size("context")
    ten = lax.axis_index("tensor")
    slots = lax.axis_size("tensor")
    rows, width = tokens.shape[1:]
    half = width // 2
    share = rows // slots
    inner = q_weight.shape[1]
    groups = inner // PAIR
    heads_here = inner // HEAD_DIM
    docs = doc_lengths.shape[1]
    pics = picture_starts.shape[1]
    length = ctxs * rows
    quarter = half // ctxs
    bq = min(512, rows)
    bk = min(512, rows)
    assert ctxs % groups == 0 and ctxs & (ctxs - 1) == 0 and slots & (slots - 1) == 0

    def by_shard(x):
        turned = jnp.concatenate([x[..., half:], x[..., :half]], axis=-1)
        return jnp.where(me == 0, x, turned)

    def slot_rows(x, i):
        return lax.dynamic_slice_in_dim(x, (ten ^ i) * share, share, 0)

    def other_half(x):
        return swap_with(x, "shard", 1)

    own_qkv = (q_weight, k_weight, v_weight)
    oth_qkv = tuple(other_half(w) for w in own_qkv)
    doc_ends = jnp.cumsum(doc_lengths[0])
    ids = jnp.concatenate(
        [
            jnp.stack([me, ctx, ten, ctx * 0]).astype(jnp.int32),
            doc_ends.astype(jnp.int32),
            picture_starts[0].astype(jnp.int32),
        ]
    )
    local_tables = rotary_tables(ctx * rows + jnp.arange(rows, dtype=jnp.int32))
    k_bias_wide = jnp.pad(
        k_bias.astype(f32).reshape(heads_here, ROT), ((0, 0), (0, HEAD_DIM - ROT))
    ).reshape(1, inner)
    h1, send = project(
        ids,
        tokens[0],
        ln1_gain.reshape(1, width),
        ln1_shift.reshape(1, width),
        own_qkv,
        oth_qkv,
        (q_bias.astype(f32).reshape(1, inner), k_bias_wide, v_bias.astype(f32).reshape(1, inner)),
        local_tables,
        groups,
        slots,
    )

    (send, later) = hold(
        send,
        (
            o_weight,
            gate_weight,
            up_weight,
            down_weight,
            cotangent[0],
            tokens[0],
            jnp.arange(length, dtype=jnp.int32),
        ),
    )
    o_weight, gate_weight, up_weight, down_weight, cot_rows, x_rows, positions = later
    pieces = [send[0]] + [swap_with(send[s % groups], "context", s) for s in range(1, ctxs)]
    down_oth, o_oth, gate_oth, up_oth = map(
        other_half, (down_weight, o_weight, gate_weight, up_weight)
    )
    full_tables = rotary_tables(positions)
    cot_all = by_shard(jnp.concatenate([slot_rows(cot_rows, i) for i in range(slots)], axis=0))
    x_share = by_shard(slot_rows(x_rows, 0)).astype(f32)
    down_full = jnp.concatenate([down_weight, down_oth], axis=1)
    o_full = jnp.concatenate([o_weight, o_oth], axis=1)
    dm_all = dot(cot_all, down_full, NT)
    gate_full = jnp.concatenate([gate_weight, gate_oth], axis=0)
    up_full = jnp.concatenate([up_weight, up_oth], axis=0)
    gain_two = by_shard(ln2_gain.astype(f32))
    shift_two = by_shard(ln2_shift.astype(f32))
    gain_one = by_shard(ln1_gain.astype(f32))
    pieces, ready = hold(
        pieces, (down_full, o_full, gate_full, up_full, cot_all, dm_all, full_tables, x_share)
    )
    down_full, o_full, gate_full, up_full, cot_all, dm_all, full_tables, x_share = ready

    attn_send, o_t, lse = attend(ids, pieces, groups, slots, docs, pics, bq, bk)
    attn, attn_parts = join(
        ids,
        [attn_send[0]] + [swap_with(attn_send[s], "context", s) for s in range(1, groups)],
        (o_weight,),
        (o_oth,),
        slots,
        NN,
    )

    def send_rows(parts):
        return [swap_with(parts[i].astype(bf16), "tensor", i) for i in range(1, slots)]

    def add_rows(own, received):
        for part in received:
            own = own + part.astype(f32)
        return own

    def gather_rows(block):
        return [block] + [swap_with(block, "tensor", i) for i in range(1, slots)]

    def slot_of(x, i):
        return x[i * share : (i + 1) * share]

    x1 = x_share + add_rows(attn_parts[0], send_rows(attn_parts))
    mean2 = jnp.mean(x1, axis=-1, keepdims=True)
    cent2 = x1 - mean2
    inv2 = lax.rsqrt(jnp.mean(cent2 * cent2, axis=-1, keepdims=True) + EPS)
    unit2 = cent2 * inv2
    h2 = gather_rows((unit2 * gain_two + shift_two).astype(bf16))

    hidden = []
    gate_grad = []
    up_grad = []
    norm2_parts = []
    dh2_received = []
    for i in range(slots):
        dm = slot_of(dm_all, i)
        g = dot(h2[i], gate_full)
        u = dot(h2[i], up_full)
        sig = jax.nn.sigmoid(g)
        act = g * sig
        hidden.append((act * u).astype(bf16))
        gate_grad.append((dm * u * sig * (1.0 + g * (1.0 - sig))).astype(bf16))
        up_grad.append((dm * act).astype(bf16))
        part = dot(gate_grad[i], gate_full, NT) + dot(up_grad[i], up_full, NT)
        norm2_parts.append(part if i == 0 else part.astype(bf16))
        if i + 1 < slots:
            norm2_parts[i], h2[i + 1] = hold(norm2_parts[i], h2[i + 1])
        if i > 0:
            dh2_received.append(swap_with(norm2_parts[i], "tensor", i))

    def blocks_of(mine, theirs, axis):
        def block(x, d):
            return lax.dynamic_slice_in_dim(x, (ctx ^ d) * quarter, quarter, axis).astype(f32)

        return {d: block(mine, d) + block(theirs, d) for d in range(ctxs)}

    def scatter_step(parts, bit):
        parts = dict(parts)
        for d in sorted((d for d in parts if d & bit), reverse=True):
            parts[d ^ bit] += swap_with(parts.pop(d).astype(bf16), "context", bit).astype(f32)
        return parts

    def scatter_rest(parts):
        bit = 2
        while bit < ctxs:
            parts = scatter_step(parts, bit)
            bit *= 2
        return parts[0]

    h2_all, gate_all, up_all, hidden_all = (
        jnp.concatenate(blocks, axis=0) for blocks in (h2, gate_grad, up_grad, hidden)
    )

    norm2_parts, h2_all, gate_all, up_all = hold(norm2_parts, h2_all, gate_all, up_all)
    gate_theirs = dot(h2_all[:, half:], gate_all, TN).astype(bf16)
    up_theirs = dot(h2_all[:, half:], up_all, TN).astype(bf16)
    h2_all, gate_theirs, up_theirs = hold(h2_all, gate_theirs, up_theirs)
    gate_theirs = other_half(gate_theirs)
    up_theirs = other_half(up_theirs)
    gate_mine = dot(h2_all[:, :half], gate_all, TN).astype(bf16)
    up_mine = dot(h2_all[:, :half], up_all, TN).astype(bf16)
    dh2_received, norm2_own, gate_mine, up_mine, gate_theirs, up_theirs = hold(
        dh2_received, norm2_parts[0], gate_mine, up_mine, gate_theirs, up_theirs
    )
    gate_parts = scatter_step(blocks_of(gate_mine, gate_theirs, 0), 1)
    up_parts = scatter_step(blocks_of(up_mine, up_theirs, 0), 1)
    dh2 = add_rows(norm2_own, dh2_received)
    cot_share = slot_of(cot_all, 0).astype(f32)
    e2 = dh2 * gain_two
    dx1 = cot_share + inv2 * (
        e2
        - jnp.mean(e2, axis=-1, keepdims=True)
        - unit2 * jnp.mean(e2 * unit2, axis=-1, keepdims=True)
    )
    dx1_slots = gather_rows(dx1.astype(bf16))

    hidden_all, cot_all, dx1_own = hold(hidden_all, cot_all, dx1_slots[0])
    down_theirs = dot(hidden_all, cot_all[:, half:], TN).astype(bf16)
    down_mine = dot(hidden_all, cot_all[:, :half], TN).astype(bf16)
    out_all = dot(hidden_all, down_full).astype(bf16)
    down_theirs = other_half(down_theirs)
    dx1_rest, dx1_own, out_all, down_mine = hold(dx1_slots[1:], dx1_own, out_all, down_mine)
    dx1b = jnp.concatenate([dx1_own] + dx1_rest, axis=0)
    d_attn = dot(dx1b, o_full, NT).astype(bf16)
    d_send = [
        lax.dynamic_slice_in_dim(d_attn, ((ctx & (groups - 1)) ^ s) * PAIR, PAIR, 1)
        for s in range(groups)
    ]
    d_send, dx1b = hold(d_send, dx1b)
    d_pieces = [d_send[0]] + [swap_with(d_send[s % groups], "context", s) for s in range(1, ctxs)]

    o_theirs = dot(attn, dx1b[:, half:], TN).astype(bf16)
    o_mine = dot(attn, dx1b[:, :half], TN).astype(bf16)
    o_theirs = other_half(o_theirs)

    d_pieces, out_all, o_mine, o_theirs, down_mine, down_theirs, gate_parts, up_parts = hold(
        d_pieces, out_all, o_mine, o_theirs, down_mine, down_theirs, gate_parts, up_parts
    )
    out_received = send_rows([slot_of(out_all, i) for i in range(slots)])
    gate_out = scatter_rest(gate_parts)
    up_out = scatter_rest(up_parts)
    down_parts = scatter_step(blocks_of(down_mine, down_theirs, 1), 1)
    back = attend_back(
        ids, pieces, d_pieces, o_t, lse, full_tables, groups, slots, docs, pics, bq, bk
    )
    back_rest = [swap_with(back[s], "context", s) for s in range(1, groups)]

    back_own, out_received, down_parts, o_mine = hold(back[0], out_received, down_parts, o_mine)
    output = by_shard((x1 + add_rows(slot_of(out_all, 0).astype(f32), out_received)).astype(bf16))[None]
    o_parts = scatter_step(blocks_of(o_mine, o_theirs, 1), 1)
    down_grad = scatter_rest(down_parts)
    o_grad = scatter_rest(o_parts)
    back_rest, output = hold(back_rest, output)

    d_qkv, norm1_parts = join(ids, [back_own] + back_rest, own_qkv, oth_qkv, slots, NT)
    norm1_parts, d_qkv = hold(norm1_parts, d_qkv)
    dh1_received = send_rows(norm1_parts)
    qkv_theirs = other_half(dot(h1[:, half:], d_qkv, TN).astype(bf16))
    qkv_mine = dot(h1[:, :half], d_qkv, TN).astype(bf16)
    qkv_parts = scatter_step(blocks_of(qkv_mine, qkv_theirs, 0), 1)
    qkv_grad = scatter_rest(qkv_parts)
    bias = jnp.sum(d_qkv.astype(f32), axis=0, keepdims=True)
    bias = sum_over(sum_over(bias, "shard"), "context")[0]
    dh1_received, qkv_mine = hold(dh1_received, qkv_mine)
    dh1 = add_rows(norm1_parts[0], dh1_received)

    mean1 = jnp.mean(x_share, axis=-1, keepdims=True)
    cent1 = x_share - mean1
    inv1 = lax.rsqrt(jnp.mean(cent1 * cent1, axis=-1, keepdims=True) + EPS)
    unit1 = cent1 * inv1
    e1 = dh1 * gain_one
    tokens_grad = dx1 + inv1 * (
        e1
        - jnp.mean(e1, axis=-1, keepdims=True)
        - unit1 * jnp.mean(e1 * unit1, axis=-1, keepdims=True)
    )
    tokens_grad = by_shard(tokens_grad)[None]

    k_bias_grad = bias[inner : 2 * inner].reshape(heads_here, HEAD_DIM)[:, :ROT]
    norms = jnp.stack(
        [
            jnp.sum(dh1 * unit1, axis=0),
            jnp.sum(dh1, axis=0),
            jnp.sum(dh2 * unit2, axis=0),
            jnp.sum(dh2, axis=0),
        ]
    )
    norms = by_shard(norms)
    for axis in ("shard", "context", "tensor"):
        norms = sum_over(norms, axis)
    return (
        output,
        tokens_grad,
        norms[0],
        norms[1],
        qkv_grad[:, :inner],
        qkv_grad[:, inner : 2 * inner],
        qkv_grad[:, 2 * inner :],
        bias[:inner],
        k_bias_grad.reshape(heads_here * ROT),
        bias[2 * inner :],
        o_grad,
        norms[2],
        norms[3],
        gate_out,
        up_out,
        down_grad,
    )


def solution(mesh):
    tokens = P("shard", "context", None)
    inward = P("shard", "tensor")
    outward = P("tensor", "shard")
    vector = P("tensor")
    placed = (
        tokens,
        P(),
        P(),
        inward,
        inward,
        inward,
        vector,
        vector,
        vector,
        outward,
        P(),
        P(),
        inward,
        inward,
        outward,
        tokens,
        P("shard", None),
        P("shard", None),
    )
    share = P("shard", ("context", "tensor"), None)
    grad_in = P(("shard", "context"), "tensor")
    grad_out = P("tensor", ("shard", "context"))

    return jax.shard_map(
        local,
        mesh=mesh,
        in_specs=placed,
        out_specs=(
            share,
            share,
            P(),
            P(),
            grad_in,
            grad_in,
            grad_in,
            vector,
            vector,
            vector,
            grad_out,
            P(),
            P(),
            grad_in,
            grad_in,
            grad_out,
        ),
        check_vma=False,
    )
```

```python
import functools

import jax
import jax.numpy as jnp
from jax import lax
from jax.experimental import pallas as pl
from jax.experimental.pallas import tpu as pltpu
from jax.sharding import PartitionSpec as P

HEAD_DIM = 64
ROT = 16
SPAN = 256
PAIR = 128
EPS = 1e-05
LOW = -1e30
LOWER = -2e30
SCALE = HEAD_DIM ** (-0.5)

f32 = jnp.float32
bf16 = jnp.bfloat16


NT = (((1,), (1,)), ((), ()))
NN = (((1,), (0,)), ((), ()))
TN = (((0,), (0,)), ((), ()))


def dot(a, b, dims=NN):
    return lax.dot_general(a, b, dims, preferred_element_type=f32)


def swap_with(x, axis, bit):
    size = lax.axis_size(axis)
    return lax.ppermute(x, axis, [(i, i ^ bit) for i in range(size)])


def sum_over(x, axis):
    terms = [x] + [swap_with(x, axis, i) for i in range(1, lax.axis_size(axis))]
    while len(terms) > 1:
        terms = [terms[i] + terms[i + 1] for i in range(0, len(terms), 2)]
    return terms[0]


def rotary_tables(positions):
    half = ROT // 2
    freq = 10000.0 ** (-(2.0 * jnp.arange(half).astype(f32)) / ROT)
    angles = freq[:, None] * positions.astype(f32)[None, :]
    parts = jnp.concatenate([jnp.cos(angles), jnp.sin(angles)], axis=0)
    lane = jnp.arange(PAIR) % HEAD_DIM
    row = jnp.arange(half)[:, None]
    hit = (lane[None, :] % half == row) & (lane[None, :] < ROT)
    spread_cos = jnp.concatenate([hit, jnp.zeros_like(hit)], axis=0).astype(f32)
    sign = jnp.where(lane < half, -1.0, 1.0)[None, :]
    spread_sin = jnp.concatenate([jnp.zeros_like(hit), hit], axis=0).astype(f32) * sign
    expand = functools.partial(
        lax.dot_general,
        dimension_numbers=TN,
        precision=lax.Precision.HIGHEST,
        preferred_element_type=f32,
    )
    rest = jnp.where(lane < ROT, 0.0, 1.0).astype(f32)
    return expand(parts, spread_cos) + rest[None, :], expand(parts, spread_sin)


def swap_halves(x):
    lane = lax.broadcasted_iota(jnp.int32, x.shape, 1) % HEAD_DIM
    return jnp.where(lane < ROT // 2, pltpu.roll(x, PAIR - ROT // 2, 1), pltpu.roll(x, ROT // 2, 1))


def project_kernel(
    groups,
    ids,
    x_own,
    x_oth,
    gain_own,
    gain_oth,
    shift_own,
    shift_oth,
    wq_own,
    wk_own,
    wv_own,
    wq_oth,
    wk_oth,
    wv_oth,
    q_bias,
    k_bias,
    v_bias,
    cos_ref,
    sin_ref,
    *rest,
):
    h_ref, pieces, (qs, ks, vs) = rest[0], rest[1 : 1 + groups], rest[1 + groups :]
    half = x_own.shape[1]
    a = x_own[...].astype(f32)
    b = x_oth[...].astype(f32)
    count = 1.0 / (2 * half)
    mean = (jnp.sum(a, axis=1, keepdims=True) + jnp.sum(b, axis=1, keepdims=True)) * count
    a = a - mean
    b = b - mean
    var = (jnp.sum(a * a, axis=1, keepdims=True) + jnp.sum(b * b, axis=1, keepdims=True)) * count
    inv = lax.rsqrt(var + EPS)
    ha = (a * inv * gain_own[...].astype(f32) + shift_own[...].astype(f32)).astype(bf16)
    hb = (b * inv * gain_oth[...].astype(f32) + shift_oth[...].astype(f32)).astype(bf16)
    h_ref[:, :half] = ha
    h_ref[:, half:] = hb
    qs[...] = dot(ha, wq_own[...]) + dot(hb, wq_oth[...]) + q_bias[...]
    ks[...] = dot(ha, wk_own[...]) + dot(hb, wk_oth[...]) + k_bias[...]
    vs[...] = dot(ha, wv_own[...]) + dot(hb, wv_oth[...]) + v_bias[...]
    cos = cos_ref[...]
    sin = sin_ref[...]
    for s in range(groups):
        group = (ids[1] & (groups - 1)) ^ s
        cols = pl.ds(pl.multiple_of(group * PAIR, PAIR), PAIR)
        q = qs[:, cols]
        k = ks[:, cols]
        pieces[s][:, :PAIR] = (q * cos + swap_halves(q) * sin).astype(bf16)
        pieces[s][:, PAIR : 2 * PAIR] = (k * cos + swap_halves(k) * sin).astype(bf16)
        pieces[s][:, 2 * PAIR :] = vs[:, cols].astype(bf16)


def project(ids, tokens, gain, shift, own, other, biases, tables, groups, slots):
    rows, width = tokens.shape
    half = width // 2
    share = rows // slots
    inner = own[0].shape[1]

    def row_block(i, ids):
        return ids[2] ^ i

    whole = lambda i, ids: (0, 0)
    weight = pl.BlockSpec((half, inner), whole)
    bias = pl.BlockSpec((1, inner), whole)
    in_specs = [
        pl.BlockSpec((share, half), lambda i, ids: (row_block(i, ids), ids[0])),
        pl.BlockSpec((share, half), lambda i, ids: (row_block(i, ids), 1 - ids[0])),
        pl.BlockSpec((1, half), lambda i, ids: (0, ids[0])),
        pl.BlockSpec((1, half), lambda i, ids: (0, 1 - ids[0])),
        pl.BlockSpec((1, half), lambda i, ids: (0, ids[0])),
        pl.BlockSpec((1, half), lambda i, ids: (0, 1 - ids[0])),
    ]
    in_specs += [weight] * 6 + [bias] * 3
    in_specs += [pl.BlockSpec((share, PAIR), lambda i, ids: (row_block(i, ids), 0))] * 2
    out = pl.pallas_call(
        functools.partial(project_kernel, groups),
        grid_spec=pltpu.PrefetchScalarGridSpec(
            num_scalar_prefetch=1,
            grid=(slots,),
            in_specs=in_specs,
            out_specs=[pl.BlockSpec((share, width), lambda i, ids: (i, 0))]
            + [pl.BlockSpec((share, 3 * PAIR), lambda i, ids: (i, 0))] * groups,
            scratch_shapes=[pltpu.VMEM((share, inner), f32)] * 3,
        ),
        out_shape=[jax.ShapeDtypeStruct((rows, width), bf16)]
        + [jax.ShapeDtypeStruct((rows, 3 * PAIR), bf16)] * groups,
        compiler_params=pltpu.CompilerParams(vmem_limit_bytes=56 << 20),
        cost_estimate=pl.CostEstimate(
            flops=2 * rows * width * inner * 3,
            bytes_accessed=rows * width * 4 + 3 * width * inner * 2 + rows * inner * 6,
            transcendentals=rows,
        ),
        name="project",
    )(ids, tokens, tokens, gain, gain, shift, shift, *own, *other, *biases, *tables)
    return out[0], out[1:]


def reach(ids, p, docs, pics, length):
    start = jnp.zeros_like(p)
    end = jnp.full_like(p, length)
    for j in range(docs):
        e = ids[4 + j]
        start = jnp.where(p >= e, jnp.maximum(start, e), start)
        end = jnp.where(p < e, jnp.minimum(end, e), end)
    far = p + 1
    for j in range(pics):
        b = ids[4 + docs + j]
        inside = (p >= b) & (p < b + SPAN)
        far = jnp.where(inside, jnp.maximum(far, jnp.minimum(b + SPAN, end)), far)
    return start, far


def block_ranges(ids, first, bq, bk, docs, pics, length):
    lo_a, hi_a = reach(ids, first, docs, pics, length)
    lo_b, hi_b = reach(ids, first + (bq - 1), docs, pics, length)
    begin = lo_a // bk
    stop = (hi_b + (bk - 1)) // bk
    full_begin = jnp.clip((lo_b + (bk - 1)) // bk, begin, stop)
    full_stop = jnp.clip(hi_a // bk, full_begin, stop)
    return begin, full_begin, full_stop, stop


def piece_copies(ids, pieces, whole, sems, slots, share, outward=False):
    copies = []
    for s, piece in enumerate(pieces):
        for i in range(slots):
            first = ((ids[1] ^ s) * slots + (ids[2] ^ i)) * share
            there = whole.at[pl.ds(pl.multiple_of(first, share), share)]
            here = piece.at[pl.ds(i * share, share)]
            src, dst = (there, here) if outward else (here, there)
            copies.append(pltpu.make_async_copy(src, dst, sems.at[s * slots + i]))
    return copies


def attend_kernel(dims, ids, *refs):
    pieces, groups, slots, share, length, docs, pics, bq, bk = dims
    ins = refs[:pieces]
    outs = refs[pieces : pieces + groups]
    o_t, lse = refs[pieces + groups : pieces + groups + 2]
    qkv, vx, ob, acc, m_ref, sem_in, sem_out = refs[pieces + groups + 2 :]
    loads = piece_copies(ids, ins, qkv, sem_in, slots, share)
    for c in loads:
        c.start()
    for c in loads:
        c.wait()

    def prepare(j, _):
        rows = pl.ds(pl.multiple_of(j * bk, bk), bk)
        v_t = qkv[rows, 2 * PAIR :].astype(f32).T
        ones = jnp.ones((16, bk), bf16)
        for h in range(2):
            vx[h, :HEAD_DIM, rows] = v_t[h * HEAD_DIM : (h + 1) * HEAD_DIM].astype(bf16)
            vx[h, HEAD_DIM:, rows] = ones
        return 0

    lax.fori_loop(0, length // bk, prepare, 0)
    lane = lax.broadcasted_iota(jnp.int32, (bq, PAIR), 1)

    def query_block(i, _):
        first = i * bq
        rows = pl.ds(pl.multiple_of(first, bq), bq)
        q = qkv[rows, :PAIR].astype(f32) * SCALE
        heads = [
            jnp.where((lane < HEAD_DIM) == (h == 0), q, 0.0).astype(bf16) for h in range(2)
        ]
        for h in range(2):
            acc[h] = jnp.zeros_like(acc[h])
            m_ref[h] = jnp.full_like(m_ref[h], LOW)
        lo, hi = reach(
            ids, first + lax.broadcasted_iota(jnp.int32, (1, bq), 1), docs, pics, length
        )
        begin, full_begin, full_stop, stop = block_ranges(
            ids, first, bq, bk, docs, pics, length
        )

        def visit(masked, j, _):
            keys = pl.ds(pl.multiple_of(j * bk, bk), bk)
            k = qkv[keys, PAIR : 2 * PAIR]
            if masked:
                p = j * bk + lax.broadcasted_iota(jnp.int32, (bk, bq), 0)
                ok = (p >= lo) & (p < hi)
            for h in range(2):
                s = dot(k, heads[h], NT)
                if masked:
                    s = jnp.where(ok, s, LOWER)
                old = m_ref[h, 0:1]
                new = jnp.maximum(old, jnp.max(s, axis=0, keepdims=True))
                w = jnp.exp(s - new).astype(bf16)
                acc[h] = acc[h] * jnp.exp(old - new) + dot(vx[h, :, keys], w)
                m_ref[h, 0:1] = new
            return 0

        lax.fori_loop(begin, full_begin, functools.partial(visit, True), 0)
        lax.fori_loop(full_begin, full_stop, functools.partial(visit, False), 0)
        lax.fori_loop(full_stop, stop, functools.partial(visit, True), 0)
        for h in range(2):
            total = acc[h, HEAD_DIM : HEAD_DIM + 1]
            o_t[h * HEAD_DIM : (h + 1) * HEAD_DIM, rows] = acc[h, :HEAD_DIM] / total
            lse[h : h + 1, rows] = m_ref[h, 0:1] + jnp.log(total)
        ob[rows] = o_t[:, rows].T.astype(bf16)
        return 0

    lax.fori_loop(0, length // bq, query_block, 0)
    stores = piece_copies(ids, outs, ob, sem_out, slots, share, outward=True)
    for c in stores:
        c.start()
    for c in stores:
        c.wait()


def attend_cost(length, matmuls):
    pairs = length * length // 2
    return pl.CostEstimate(
        flops=2 * pairs * 256 * 2 * matmuls,
        bytes_accessed=length * PAIR * 2 * 8,
        transcendentals=2 * pairs,
    )


def attend(ids, pieces, groups, slots, docs, pics, bq, bk):
    rows = pieces[0].shape[0]
    n = len(pieces)
    length = rows * n
    share = rows // slots
    dims = (n, groups, slots, share, length, docs, pics, bq, bk)
    anywhere = pl.BlockSpec(memory_space=pl.ANY)
    out = pl.pallas_call(
        functools.partial(attend_kernel, dims),
        grid_spec=pltpu.PrefetchScalarGridSpec(
            num_scalar_prefetch=1,
            grid=(1,),
            in_specs=[anywhere] * n,
            out_specs=[anywhere] * groups
            + [
                pl.BlockSpec((PAIR, length), lambda i, ids: (0, 0)),
                pl.BlockSpec((8, length), lambda i, ids: (0, 0)),
            ],
            scratch_shapes=[
                pltpu.VMEM((length, 3 * PAIR), bf16),
                pltpu.VMEM((2, HEAD_DIM + 16, length), bf16),
                pltpu.VMEM((length, PAIR), bf16),
                pltpu.VMEM((2, HEAD_DIM + 16, bq), f32),
                pltpu.VMEM((2, 8, bq), f32),
                pltpu.SemaphoreType.DMA((n * slots,)),
                pltpu.SemaphoreType.DMA((groups * slots,)),
            ],
        ),
        out_shape=[jax.ShapeDtypeStruct((rows, PAIR), bf16)] * groups
        + [
            jax.ShapeDtypeStruct((PAIR, length), f32),
            jax.ShapeDtypeStruct((8, length), f32),
        ],
        compiler_params=pltpu.CompilerParams(vmem_limit_bytes=56 << 20),
        cost_estimate=attend_cost(length, 2),
        name="attend",
    )(ids, *pieces)
    return out[:groups], out[groups], out[groups + 1]


def attend_back_kernel(dims, ids, *refs):
    pieces, groups, slots, share, length, docs, pics, bq, bk = dims
    ins = refs[:pieces]
    grads = refs[pieces : 2 * pieces]
    o_t, lse, cos_ref, sin_ref = refs[2 * pieces : 2 * pieces + 4]
    outs = refs[2 * pieces + 4 : 2 * pieces + 4 + groups]
    qkv, dob, kt, dq_t, dk, dv, sem_in, sem_grad, sem_out = refs[2 * pieces + 4 + groups :]
    loads = piece_copies(ids, ins, qkv, sem_in, slots, share)
    loads += piece_copies(ids, grads, dob, sem_grad, slots, share)
    for c in loads:
        c.start()
    for c in loads:
        c.wait()

    def prepare(j, _):
        rows = pl.ds(pl.multiple_of(j * bk, bk), bk)
        kt[:, rows] = qkv[rows, PAIR : 2 * PAIR].astype(f32).T.astype(bf16)
        dk[rows] = jnp.zeros((bk, PAIR), f32)
        dv[rows] = jnp.zeros((bk, PAIR), f32)
        return 0

    lax.fori_loop(0, length // bk, prepare, 0)
    lane = lax.broadcasted_iota(jnp.int32, (bq, PAIR), 1)

    def turn_back(x, rows):
        return x * cos_ref[rows] - swap_halves(x) * sin_ref[rows]

    def query_block(i, _):
        first = i * bq
        rows = pl.ds(pl.multiple_of(first, bq), bq)
        q = qkv[rows, :PAIR].astype(f32) * SCALE
        do = dob[rows].astype(f32)
        q_of = []
        do_of = []
        for h in range(2):
            mine = (lane < HEAD_DIM) == (h == 0)
            q_of.append(jnp.where(mine, q, 0.0).astype(bf16))
            do_of.append(jnp.where(mine, do, 0.0).astype(bf16))
        prod = do.T * o_t[:, rows]
        delta = [
            jnp.sum(prod[h * HEAD_DIM : (h + 1) * HEAD_DIM], axis=0, keepdims=True)
            for h in range(2)
        ]
        dq_t[...] = jnp.zeros_like(dq_t)
        lo, hi = reach(
            ids, first + lax.broadcasted_iota(jnp.int32, (1, bq), 1), docs, pics, length
        )
        begin, full_begin, full_stop, stop = block_ranges(
            ids, first, bq, bk, docs, pics, length
        )

        def visit(masked, j, _):
            keys = pl.ds(pl.multiple_of(j * bk, bk), bk)
            k = qkv[keys, PAIR : 2 * PAIR]
            v = qkv[keys, 2 * PAIR :]
            if masked:
                p = j * bk + lax.broadcasted_iota(jnp.int32, (bk, bq), 0)
                ok = (p >= lo) & (p < hi)
            dk_sum = dk[keys]
            dv_sum = dv[keys]
            for h in range(2):
                feats = slice(h * HEAD_DIM, (h + 1) * HEAD_DIM)
                s = dot(k, q_of[h], NT)
                if masked:
                    s = jnp.where(ok, s, LOWER)
                w = jnp.exp(s - lse[h : h + 1, rows])
                dw = dot(v, do_of[h], NT)
                ds = (w * (dw - delta[h])).astype(bf16)
                dv_sum = dv_sum + dot(w.astype(bf16), do_of[h])
                dk_sum = dk_sum + dot(ds, q_of[h])
                dq_t[feats] += dot(kt[feats, keys], ds)
            dk[keys] = dk_sum
            dv[keys] = dv_sum
            return 0

        lax.fori_loop(begin, full_begin, functools.partial(visit, True), 0)
        lax.fori_loop(full_begin, full_stop, functools.partial(visit, False), 0)
        lax.fori_loop(full_stop, stop, functools.partial(visit, True), 0)
        dq = dq_t[...].T * SCALE
        qkv[rows, :PAIR] = turn_back(dq, rows).astype(bf16)
        return 0

    lax.fori_loop(0, length // bq, query_block, 0)

    def finish(j, _):
        rows = pl.ds(pl.multiple_of(j * bk, bk), bk)
        qkv[rows, PAIR : 2 * PAIR] = turn_back(dk[rows], rows).astype(bf16)
        qkv[rows, 2 * PAIR :] = dv[rows].astype(bf16)
        return 0

    lax.fori_loop(0, length // bk, finish, 0)
    stores = piece_copies(ids, outs, qkv, sem_out, slots, share, outward=True)
    for c in stores:
        c.start()
    for c in stores:
        c.wait()


def attend_back(ids, pieces, grads, o_t, lse, tables, groups, slots, docs, pics, bq, bk):
    rows = pieces[0].shape[0]
    n = len(pieces)
    length = rows * n
    share = rows // slots
    dims = (n, groups, slots, share, length, docs, pics, bq, bk)
    anywhere = pl.BlockSpec(memory_space=pl.ANY)
    once = dict(pipeline_mode=pl.Buffered(1))
    return pl.pallas_call(
        functools.partial(attend_back_kernel, dims),
        grid_spec=pltpu.PrefetchScalarGridSpec(
            num_scalar_prefetch=1,
            grid=(1,),
            in_specs=[anywhere] * (2 * n)
            + [
                pl.BlockSpec((PAIR, length), lambda i, ids: (0, 0), **once),
                pl.BlockSpec((8, length), lambda i, ids: (0, 0), **once),
                pl.BlockSpec((length, PAIR), lambda i, ids: (0, 0), **once),
                pl.BlockSpec((length, PAIR), lambda i, ids: (0, 0), **once),
            ],
            out_specs=[anywhere] * groups,
            scratch_shapes=[
                pltpu.VMEM((length, 3 * PAIR), bf16),
                pltpu.VMEM((length, PAIR), bf16),
                pltpu.VMEM((PAIR, length), bf16),
                pltpu.VMEM((PAIR, bq), f32),
                pltpu.VMEM((length, PAIR), f32),
                pltpu.VMEM((length, PAIR), f32),
                pltpu.SemaphoreType.DMA((n * slots,)),
                pltpu.SemaphoreType.DMA((n * slots,)),
                pltpu.SemaphoreType.DMA((groups * slots,)),
            ],
        ),
        out_shape=[jax.ShapeDtypeStruct((rows, 3 * PAIR), bf16)] * groups,
        compiler_params=pltpu.CompilerParams(vmem_limit_bytes=56 << 20),
        cost_estimate=attend_cost(length, 5),
        name="attend_back",
    )(ids, *pieces, *grads, o_t, lse, *tables)


def join_kernel(groups, kinds, slots, dims, ids, *refs):
    pieces = refs[:groups]
    own = refs[groups : groups + kinds]
    oth = refs[groups + kinds : groups + 2 * kinds]
    joined = refs[groups + 2 * kinds]
    parts = refs[groups + 2 * kinds + 1 :]
    inner = groups * PAIR
    half = parts[0].shape[1] // 2
    for s in range(groups):
        group = (ids[1] & (groups - 1)) ^ s
        for j in range(kinds):
            cols = pl.ds(pl.multiple_of(j * inner + group * PAIR, PAIR), PAIR)
            joined[:, cols] = pieces[s][:, j * PAIR : (j + 1) * PAIR]
    for side, weights in enumerate((own, oth)):
        total = None
        for j, w in enumerate(weights):
            term = dot(joined[:, j * inner : (j + 1) * inner], w[...], dims)
            total = term if total is None else total + term
        for i in range(slots):

            @pl.when(pl.program_id(0) == i)
            def _():
                parts[i][:, side * half : (side + 1) * half] = total.astype(parts[i].dtype)


def join(ids, pieces, own, oth, slots, dims):
    groups = len(pieces)
    kinds = len(own)
    rows = pieces[0].shape[0]
    share = rows // slots
    inner = groups * PAIR
    width = 2 * (own[0].shape[0] if dims == NT else own[0].shape[1])
    whole = lambda i, ids: (0, 0)
    by_row = lambda i, ids: (i, 0)
    out = pl.pallas_call(
        functools.partial(join_kernel, groups, kinds, slots, dims),
        grid_spec=pltpu.PrefetchScalarGridSpec(
            num_scalar_prefetch=1,
            grid=(slots,),
            in_specs=[pl.BlockSpec((share, kinds * PAIR), by_row)] * groups
            + [pl.BlockSpec(own[0].shape, whole)] * (2 * kinds),
            out_specs=[pl.BlockSpec((share, kinds * inner), by_row)]
            + [pl.BlockSpec((share, width), whole)] * slots,
        ),
        out_shape=[jax.ShapeDtypeStruct((rows, kinds * inner), bf16)]
        + [jax.ShapeDtypeStruct((share, width), f32 if i == 0 else bf16) for i in range(slots)],
        compiler_params=pltpu.CompilerParams(vmem_limit_bytes=44 << 20),
        cost_estimate=pl.CostEstimate(
            flops=2 * rows * width * inner * kinds,
            bytes_accessed=rows * width * 3 + kinds * (width * inner * 2 + rows * inner * 4),
            transcendentals=0,
        ),
    )(ids, *pieces, *own, *oth)
    return out[0], out[1:]


def hold(*groups):
    return lax.optimization_barrier(groups)


def local(
    tokens,
    ln1_gain,
    ln1_shift,
    q_weight,
    k_weight,
    v_weight,
    q_bias,
    k_bias,
    v_bias,
    o_weight,
    ln2_gain,
    ln2_shift,
    gate_weight,
    up_weight,
    down_weight,
    cotangent,
    doc_lengths,
    picture_starts,
):
    me = lax.axis_index("shard")
    ctx = lax.axis_index("context")
    ctxs = lax.axis_size("context")
    ten = lax.axis_index("tensor")
    slots = lax.axis_size("tensor")
    rows, width = tokens.shape[1:]
    half = width // 2
    share = rows // slots
    inner = q_weight.shape[1]
    groups = inner // PAIR
    heads_here = inner // HEAD_DIM
    docs = doc_lengths.shape[1]
    pics = picture_starts.shape[1]
    length = ctxs * rows
    quarter = half // ctxs
    bq = min(512, rows)
    bk = min(512, rows)
    assert ctxs % groups == 0 and ctxs & (ctxs - 1) == 0 and slots & (slots - 1) == 0

    def by_shard(x):
        turned = jnp.concatenate([x[..., half:], x[..., :half]], axis=-1)
        return jnp.where(me == 0, x, turned)

    def slot_rows(x, i):
        return lax.dynamic_slice_in_dim(x, (ten ^ i) * share, share, 0)

    def other_half(x):
        return swap_with(x, "shard", 1)

    own_qkv = (q_weight, k_weight, v_weight)
    oth_qkv = tuple(other_half(w) for w in own_qkv)
    doc_ends = jnp.cumsum(doc_lengths[0])
    ids = jnp.concatenate(
        [
            jnp.stack([me, ctx, ten, ctx * 0]).astype(jnp.int32),
            doc_ends.astype(jnp.int32),
            picture_starts[0].astype(jnp.int32),
        ]
    )
    local_tables = rotary_tables(ctx * rows + jnp.arange(rows, dtype=jnp.int32))
    k_bias_wide = jnp.pad(
        k_bias.astype(f32).reshape(heads_here, ROT), ((0, 0), (0, HEAD_DIM - ROT))
    ).reshape(1, inner)
    h1, send = project(
        ids,
        tokens[0],
        ln1_gain.reshape(1, width),
        ln1_shift.reshape(1, width),
        own_qkv,
        oth_qkv,
        (q_bias.astype(f32).reshape(1, inner), k_bias_wide, v_bias.astype(f32).reshape(1, inner)),
        local_tables,
        groups,
        slots,
    )

    (send, later) = hold(
        send,
        (
            o_weight,
            gate_weight,
            up_weight,
            down_weight,
            cotangent[0],
            tokens[0],
            jnp.arange(length, dtype=jnp.int32),
        ),
    )
    o_weight, gate_weight, up_weight, down_weight, cot_rows, x_rows, positions = later
    pieces = [send[0]] + [swap_with(send[s % groups], "context", s) for s in range(1, ctxs)]
    down_oth, o_oth, gate_oth, up_oth = map(
        other_half, (down_weight, o_weight, gate_weight, up_weight)
    )
    full_tables = rotary_tables(positions)
    cot_all = by_shard(jnp.concatenate([slot_rows(cot_rows, i) for i in range(slots)], axis=0))
    x_share = by_shard(slot_rows(x_rows, 0)).astype(f32)
    down_full = jnp.concatenate([down_weight, down_oth], axis=1)
    o_full = jnp.concatenate([o_weight, o_oth], axis=1)
    dm_all = dot(cot_all, down_full, NT)
    gate_full = jnp.concatenate([gate_weight, gate_oth], axis=0)
    up_full = jnp.concatenate([up_weight, up_oth], axis=0)
    gain_two = by_shard(ln2_gain.astype(f32))
    shift_two = by_shard(ln2_shift.astype(f32))
    gain_one = by_shard(ln1_gain.astype(f32))
    pieces, ready = hold(
        pieces, (down_full, o_full, gate_full, up_full, cot_all, dm_all, full_tables, x_share)
    )
    down_full, o_full, gate_full, up_full, cot_all, dm_all, full_tables, x_share = ready

    attn_send, o_t, lse = attend(ids, pieces, groups, slots, docs, pics, bq, bk)
    attn, attn_parts = join(
        ids,
        [attn_send[0]] + [swap_with(attn_send[s], "context", s) for s in range(1, groups)],
        (o_weight,),
        (o_oth,),
        slots,
        NN,
    )

    mid = share // 2

    def send_rows(parts):
        return [swap_with(parts[i].astype(bf16), "tensor", i) for i in range(1, slots)]

    def relay_sums(parts):
        if slots != 4:
            return send_rows(parts)
        one, two, far = (parts[i].astype(bf16) for i in range(1, 4))
        far_two = swap_with(far[:mid], "tensor", 1)
        far_one = swap_with(far[mid:], "tensor", 2)
        first = swap_with(one[:mid], "tensor", 1)
        last = swap_with(two[mid:], "tensor", 2)
        two = (two[:mid].astype(f32) + far_two.astype(f32)).astype(bf16)
        one = (one[mid:].astype(f32) + far_one.astype(f32)).astype(bf16)
        two = swap_with(two, "tensor", 2)
        one = swap_with(one, "tensor", 1)
        return [
            jnp.concatenate([first, one], axis=0),
            jnp.concatenate([two, last], axis=0),
        ]

    def add_rows(own, received):
        for part in received:
            own = own + part.astype(f32)
        return own

    def gather_rows(block):
        if slots != 4:
            return [block] + [swap_with(block, "tensor", i) for i in range(1, slots)]
        one_last = swap_with(block[mid:], "tensor", 1)
        two_first = swap_with(block[:mid], "tensor", 2)
        one_first = swap_with(block[:mid], "tensor", 1)
        two_last = swap_with(block[mid:], "tensor", 2)
        far_first = swap_with(two_first, "tensor", 1)
        far_last = swap_with(one_last, "tensor", 2)
        return [
            block,
            jnp.concatenate([one_first, one_last], axis=0),
            jnp.concatenate([two_first, two_last], axis=0),
            jnp.concatenate([far_first, far_last], axis=0),
        ]

    def slot_of(x, i):
        return x[i * share : (i + 1) * share]

    x1 = x_share + add_rows(attn_parts[0], relay_sums(attn_parts))
    mean2 = jnp.mean(x1, axis=-1, keepdims=True)
    cent2 = x1 - mean2
    inv2 = lax.rsqrt(jnp.mean(cent2 * cent2, axis=-1, keepdims=True) + EPS)
    unit2 = cent2 * inv2
    h2 = gather_rows((unit2 * gain_two + shift_two).astype(bf16))

    hidden = []
    gate_grad = []
    up_grad = []
    norm2_parts = []
    dh2_received = []
    for i in range(slots):
        dm = slot_of(dm_all, i)
        g = dot(h2[i], gate_full)
        u = dot(h2[i], up_full)
        sig = jax.nn.sigmoid(g)
        act = g * sig
        hidden.append((act * u).astype(bf16))
        gate_grad.append((dm * u * sig * (1.0 + g * (1.0 - sig))).astype(bf16))
        up_grad.append((dm * act).astype(bf16))
        part = dot(gate_grad[i], gate_full, NT) + dot(up_grad[i], up_full, NT)
        norm2_parts.append(part if i == 0 else part.astype(bf16))
        if i + 1 < slots:
            norm2_parts[i], h2[i + 1] = hold(norm2_parts[i], h2[i + 1])
        if i > 0:
            dh2_received.append(swap_with(norm2_parts[i], "tensor", i))

    def blocks_of(mine, theirs, axis):
        def block(x, d):
            return lax.dynamic_slice_in_dim(x, (ctx ^ d) * quarter, quarter, axis).astype(f32)

        return {d: block(mine, d) + block(theirs, d) for d in range(ctxs)}

    def scatter_step(parts, bit):
        parts = dict(parts)
        for d in sorted((d for d in parts if d & bit), reverse=True):
            parts[d ^ bit] += swap_with(parts.pop(d).astype(bf16), "context", bit).astype(f32)
        return parts

    def scatter_rest(parts):
        bit = 2
        while bit < ctxs:
            parts = scatter_step(parts, bit)
            bit *= 2
        return parts[0]

    h2_all, gate_all, up_all, hidden_all = (
        jnp.concatenate(blocks, axis=0) for blocks in (h2, gate_grad, up_grad, hidden)
    )

    gate_theirs = dot(h2_all[:, half:], gate_all, TN).astype(bf16)
    up_theirs = dot(h2_all[:, half:], up_all, TN).astype(bf16)
    gate_theirs = other_half(gate_theirs)
    up_theirs = other_half(up_theirs)
    gate_mine = dot(h2_all[:, :half], gate_all, TN).astype(bf16)
    up_mine = dot(h2_all[:, :half], up_all, TN).astype(bf16)
    gate_parts = scatter_step(blocks_of(gate_mine, gate_theirs, 0), 1)
    up_parts = scatter_step(blocks_of(up_mine, up_theirs, 0), 1)
    dh2 = add_rows(norm2_parts[0], dh2_received)
    cot_share = slot_of(cot_all, 0).astype(f32)
    e2 = dh2 * gain_two
    dx1 = cot_share + inv2 * (
        e2
        - jnp.mean(e2, axis=-1, keepdims=True)
        - unit2 * jnp.mean(e2 * unit2, axis=-1, keepdims=True)
    )
    dx1_slots = gather_rows(dx1.astype(bf16))

    down_theirs = dot(hidden_all, cot_all[:, half:], TN).astype(bf16)
    down_mine = dot(hidden_all, cot_all[:, :half], TN).astype(bf16)
    out_all = dot(hidden_all, down_full).astype(bf16)
    down_theirs = other_half(down_theirs)
    dx1b = jnp.concatenate(dx1_slots, axis=0)
    d_attn = dot(dx1b, o_full, NT).astype(bf16)
    d_send = [
        lax.dynamic_slice_in_dim(d_attn, ((ctx & (groups - 1)) ^ s) * PAIR, PAIR, 1)
        for s in range(groups)
    ]
    d_send, dx1b, out_all = hold(d_send, dx1b, out_all)
    d_pieces = [d_send[0]] + [swap_with(d_send[s % groups], "context", s) for s in range(1, ctxs)]

    o_theirs = dot(attn, dx1b[:, half:], TN).astype(bf16)
    o_mine = dot(attn, dx1b[:, :half], TN).astype(bf16)
    o_theirs = other_half(o_theirs)

    out_received = send_rows([slot_of(out_all, i) for i in range(slots)])
    gate_out = scatter_rest(gate_parts)
    up_out = scatter_rest(up_parts)
    down_parts = scatter_step(blocks_of(down_mine, down_theirs, 1), 1)
    back = attend_back(
        ids, pieces, d_pieces, o_t, lse, full_tables, groups, slots, docs, pics, bq, bk
    )
    back_rest = [swap_with(back[s], "context", s) for s in range(1, groups)]

    output = by_shard(
        (x1 + add_rows(slot_of(out_all, 0).astype(f32), out_received)).astype(bf16)
    )[None]
    o_parts = scatter_step(blocks_of(o_mine, o_theirs, 1), 1)
    down_grad = scatter_rest(down_parts)
    o_grad = scatter_rest(o_parts)

    d_qkv, norm1_parts = join(ids, [back[0]] + back_rest, own_qkv, oth_qkv, slots, NT)
    norm1_parts, d_qkv = hold(norm1_parts, d_qkv)
    dh1_received = send_rows(norm1_parts)
    qkv_theirs = other_half(dot(h1[:, half:], d_qkv, TN).astype(bf16))
    qkv_mine = dot(h1[:, :half], d_qkv, TN).astype(bf16)
    qkv_parts = scatter_step(blocks_of(qkv_mine, qkv_theirs, 0), 1)
    qkv_grad = scatter_rest(qkv_parts)
    dh1 = add_rows(norm1_parts[0], dh1_received)

    mean1 = jnp.mean(x_share, axis=-1, keepdims=True)
    cent1 = x_share - mean1
    inv1 = lax.rsqrt(jnp.mean(cent1 * cent1, axis=-1, keepdims=True) + EPS)
    unit1 = cent1 * inv1
    e1 = dh1 * gain_one
    tokens_grad = dx1 + inv1 * (
        e1
        - jnp.mean(e1, axis=-1, keepdims=True)
        - unit1 * jnp.mean(e1 * unit1, axis=-1, keepdims=True)
    )
    tokens_grad = by_shard(tokens_grad)[None]

    norms = jnp.stack(
        [
            jnp.sum(dh1 * unit1, axis=0),
            jnp.sum(dh1, axis=0),
            jnp.sum(dh2 * unit2, axis=0),
            jnp.sum(dh2, axis=0),
        ]
    )
    norms = sum_over(by_shard(norms), "tensor")
    bias = jnp.sum(d_qkv.astype(f32), axis=0, keepdims=True)
    sums = sum_over(jnp.concatenate([norms.reshape(1, 4 * width), bias], axis=1), "shard")
    sums = sum_over(sums, "context")
    norms = sums[0, : 4 * width].reshape(4, width)
    bias = sums[0, 4 * width :]
    k_bias_grad = bias[inner : 2 * inner].reshape(heads_here, HEAD_DIM)[:, :ROT]
    return (
        output,
        tokens_grad,
        norms[0],
        norms[1],
        qkv_grad[:, :inner],
        qkv_grad[:, inner : 2 * inner],
        qkv_grad[:, 2 * inner :],
        bias[:inner],
        k_bias_grad.reshape(heads_here * ROT),
        bias[2 * inner :],
        o_grad,
        norms[2],
        norms[3],
        gate_out,
        up_out,
        down_grad,
    )


def solution(mesh):
    tokens = P("shard", "context", None)
    inward = P("shard", "tensor")
    outward = P("tensor", "shard")
    vector = P("tensor")
    placed = (
        tokens,
        P(),
        P(),
        inward,
        inward,
        inward,
        vector,
        vector,
        vector,
        outward,
        P(),
        P(),
        inward,
        inward,
        outward,
        tokens,
        P("shard", None),
        P("shard", None),
    )
    share = P("shard", ("context", "tensor"), None)
    grad_in = P(("shard", "context"), "tensor")
    grad_out = P("tensor", ("shard", "context"))

    return jax.shard_map(
        local,
        mesh=mesh,
        in_specs=placed,
        out_specs=(
            share,
            share,
            P(),
            P(),
            grad_in,
            grad_in,
            grad_in,
            vector,
            vector,
            vector,
            grad_out,
            P(),
            P(),
            grad_in,
            grad_in,
            grad_out,
        ),
        check_vma=False,
    )
```

```python
import functools

import jax
import jax.numpy as jnp
from jax import lax
from jax.experimental import pallas as pl
from jax.experimental.pallas import tpu as pltpu
from jax.sharding import PartitionSpec as P

HEAD_DIM = 64
ROT = 16
SPAN = 256
PAIR = 128
EPS = 1e-05
LOW = -1e30
LOWER = -2e30
SCALE = HEAD_DIM ** (-0.5)

SHARD = "shard"
CONTEXT = "context"
TENSOR = "tensor"

f32 = jnp.float32
bf16 = jnp.bfloat16


NT = (((1,), (1,)), ((), ()))
NN = (((1,), (0,)), ((), ()))
TN = (((0,), (0,)), ((), ()))


def dot(a, b, dims=NN):
    return lax.dot_general(a, b, dims, preferred_element_type=f32)


def swap_with(x, axis, bit):
    size = lax.axis_size(axis)
    return lax.ppermute(x, axis, [(i, i ^ bit) for i in range(size)])


def sum_over(x, axis):
    terms = [x] + [swap_with(x, axis, i) for i in range(1, lax.axis_size(axis))]
    while len(terms) > 1:
        terms = [terms[i] + terms[i + 1] for i in range(0, len(terms), 2)]
    return terms[0]


def rotary_tables(positions):
    half = ROT // 2
    freq = 10000.0 ** (-(2.0 * jnp.arange(half).astype(f32)) / ROT)
    angles = freq[:, None] * positions.astype(f32)[None, :]
    parts = jnp.concatenate([jnp.cos(angles), jnp.sin(angles)], axis=0)
    lane = jnp.arange(PAIR) % HEAD_DIM
    row = jnp.arange(half)[:, None]
    hit = (lane[None, :] % half == row) & (lane[None, :] < ROT)
    spread_cos = jnp.concatenate([hit, jnp.zeros_like(hit)], axis=0).astype(f32)
    sign = jnp.where(lane < half, -1.0, 1.0)[None, :]
    spread_sin = jnp.concatenate([jnp.zeros_like(hit), hit], axis=0).astype(f32) * sign
    expand = functools.partial(
        lax.dot_general,
        dimension_numbers=TN,
        precision=lax.Precision.HIGHEST,
        preferred_element_type=f32,
    )
    rest = jnp.where(lane < ROT, 0.0, 1.0).astype(f32)
    return expand(parts, spread_cos) + rest[None, :], expand(parts, spread_sin)


def swap_halves(x):
    lane = lax.broadcasted_iota(jnp.int32, x.shape, 1) % HEAD_DIM
    return jnp.where(lane < ROT // 2, pltpu.roll(x, PAIR - ROT // 2, 1), pltpu.roll(x, ROT // 2, 1))


def project_kernel(
    groups,
    ids,
    x_own,
    x_oth,
    gain_own,
    gain_oth,
    shift_own,
    shift_oth,
    wq_own,
    wk_own,
    wv_own,
    wq_oth,
    wk_oth,
    wv_oth,
    q_bias,
    k_bias,
    v_bias,
    cos_ref,
    sin_ref,
    *rest,
):
    h_ref, pieces, (qs, ks, vs) = rest[0], rest[1 : 1 + groups], rest[1 + groups :]
    half = x_own.shape[1]
    a = x_own[...].astype(f32)
    b = x_oth[...].astype(f32)
    count = 1.0 / (2 * half)
    mean = (jnp.sum(a, axis=1, keepdims=True) + jnp.sum(b, axis=1, keepdims=True)) * count
    a = a - mean
    b = b - mean
    var = (jnp.sum(a * a, axis=1, keepdims=True) + jnp.sum(b * b, axis=1, keepdims=True)) * count
    inv = lax.rsqrt(var + EPS)
    ha = (a * inv * gain_own[...].astype(f32) + shift_own[...].astype(f32)).astype(bf16)
    hb = (b * inv * gain_oth[...].astype(f32) + shift_oth[...].astype(f32)).astype(bf16)
    h_ref[:, :half] = ha
    h_ref[:, half:] = hb
    qs[...] = dot(ha, wq_own[...]) + dot(hb, wq_oth[...]) + q_bias[...]
    ks[...] = dot(ha, wk_own[...]) + dot(hb, wk_oth[...]) + k_bias[...]
    vs[...] = dot(ha, wv_own[...]) + dot(hb, wv_oth[...]) + v_bias[...]
    cos = cos_ref[...]
    sin = sin_ref[...]
    for s in range(groups):
        group = (ids[1] & (groups - 1)) ^ s
        cols = pl.ds(pl.multiple_of(group * PAIR, PAIR), PAIR)
        q = qs[:, cols]
        k = ks[:, cols]
        pieces[s][:, :PAIR] = (q * cos + swap_halves(q) * sin).astype(bf16)
        pieces[s][:, PAIR : 2 * PAIR] = (k * cos + swap_halves(k) * sin).astype(bf16)
        pieces[s][:, 2 * PAIR :] = vs[:, cols].astype(bf16)


def project(ids, tokens, gain, shift, own, other, biases, tables, groups, slots):
    rows, width = tokens.shape
    half = width // 2
    share = rows // slots
    inner = own[0].shape[1]

    def row_block(i, ids):
        return ids[2] ^ i

    whole = lambda i, ids: (0, 0)
    weight = pl.BlockSpec((half, inner), whole)
    bias = pl.BlockSpec((1, inner), whole)
    in_specs = [
        pl.BlockSpec((share, half), lambda i, ids: (row_block(i, ids), ids[0])),
        pl.BlockSpec((share, half), lambda i, ids: (row_block(i, ids), 1 - ids[0])),
        pl.BlockSpec((1, half), lambda i, ids: (0, ids[0])),
        pl.BlockSpec((1, half), lambda i, ids: (0, 1 - ids[0])),
        pl.BlockSpec((1, half), lambda i, ids: (0, ids[0])),
        pl.BlockSpec((1, half), lambda i, ids: (0, 1 - ids[0])),
    ]
    in_specs += [weight] * 6 + [bias] * 3
    in_specs += [pl.BlockSpec((share, PAIR), lambda i, ids: (row_block(i, ids), 0))] * 2
    out = pl.pallas_call(
        functools.partial(project_kernel, groups),
        grid_spec=pltpu.PrefetchScalarGridSpec(
            num_scalar_prefetch=1,
            grid=(slots,),
            in_specs=in_specs,
            out_specs=[pl.BlockSpec((share, width), lambda i, ids: (i, 0))]
            + [pl.BlockSpec((share, 3 * PAIR), lambda i, ids: (i, 0))] * groups,
            scratch_shapes=[pltpu.VMEM((share, inner), f32)] * 3,
        ),
        out_shape=[jax.ShapeDtypeStruct((rows, width), bf16)]
        + [jax.ShapeDtypeStruct((rows, 3 * PAIR), bf16)] * groups,
        compiler_params=pltpu.CompilerParams(vmem_limit_bytes=56 << 20),
        cost_estimate=pl.CostEstimate(
            flops=2 * rows * width * inner * 3,
            bytes_accessed=rows * width * 4 + 3 * width * inner * 2 + rows * inner * 6,
            transcendentals=rows,
        ),
        name="project",
    )(ids, tokens, tokens, gain, gain, shift, shift, *own, *other, *biases, *tables)
    return out[0], out[1:]


def reach(ids, p, docs, pics, length):
    start = jnp.zeros_like(p)
    end = jnp.full_like(p, length)
    for j in range(docs):
        e = ids[4 + j]
        start = jnp.where(p >= e, jnp.maximum(start, e), start)
        end = jnp.where(p < e, jnp.minimum(end, e), end)
    far = p + 1
    for j in range(pics):
        b = ids[4 + docs + j]
        inside = (p >= b) & (p < b + SPAN)
        far = jnp.where(inside, jnp.maximum(far, jnp.minimum(b + SPAN, end)), far)
    return start, far


def block_ranges(ids, first, bq, bk, docs, pics, length):
    lo_a, hi_a = reach(ids, first, docs, pics, length)
    lo_b, hi_b = reach(ids, first + (bq - 1), docs, pics, length)
    begin = lo_a // bk
    stop = (hi_b + (bk - 1)) // bk
    full_begin = jnp.clip((lo_b + (bk - 1)) // bk, begin, stop)
    full_stop = jnp.clip(hi_a // bk, full_begin, stop)
    return begin, full_begin, full_stop, stop


def piece_copies(ids, pieces, whole, sems, slots, share, outward=False):
    copies = []
    for s, piece in enumerate(pieces):
        for i in range(slots):
            first = ((ids[1] ^ s) * slots + (ids[2] ^ i)) * share
            there = whole.at[pl.ds(pl.multiple_of(first, share), share)]
            here = piece.at[pl.ds(i * share, share)]
            src, dst = (there, here) if outward else (here, there)
            copies.append(pltpu.make_async_copy(src, dst, sems.at[s * slots + i]))
    return copies


def attend_kernel(dims, ids, *refs):
    pieces, groups, slots, share, length, docs, pics, bq, bk = dims
    ins = refs[:pieces]
    outs = refs[pieces : pieces + groups]
    o_t, lse = refs[pieces + groups : pieces + groups + 2]
    qkv, vx, ob, acc, m_ref, sem_in, sem_out = refs[pieces + groups + 2 :]
    loads = piece_copies(ids, ins, qkv, sem_in, slots, share)
    for c in loads:
        c.start()
    for c in loads:
        c.wait()

    def prepare(j, _):
        rows = pl.ds(pl.multiple_of(j * bk, bk), bk)
        v_t = qkv[rows, 2 * PAIR :].astype(f32).T
        ones = jnp.ones((16, bk), bf16)
        for h in range(2):
            vx[h, :HEAD_DIM, rows] = v_t[h * HEAD_DIM : (h + 1) * HEAD_DIM].astype(bf16)
            vx[h, HEAD_DIM:, rows] = ones
        return 0

    lax.fori_loop(0, length // bk, prepare, 0)
    lane = lax.broadcasted_iota(jnp.int32, (bq, PAIR), 1)

    def query_block(i, _):
        first = i * bq
        rows = pl.ds(pl.multiple_of(first, bq), bq)
        q = qkv[rows, :PAIR].astype(f32) * SCALE
        heads = [
            jnp.where((lane < HEAD_DIM) == (h == 0), q, 0.0).astype(bf16) for h in range(2)
        ]
        for h in range(2):
            acc[h] = jnp.zeros_like(acc[h])
            m_ref[h] = jnp.full_like(m_ref[h], LOW)
        lo, hi = reach(
            ids, first + lax.broadcasted_iota(jnp.int32, (1, bq), 1), docs, pics, length
        )
        begin, full_begin, full_stop, stop = block_ranges(
            ids, first, bq, bk, docs, pics, length
        )

        def visit(masked, j, _):
            keys = pl.ds(pl.multiple_of(j * bk, bk), bk)
            k = qkv[keys, PAIR : 2 * PAIR]
            if masked:
                p = j * bk + lax.broadcasted_iota(jnp.int32, (bk, bq), 0)
                ok = (p >= lo) & (p < hi)
            scores = [dot(k, heads[h], NT) for h in range(2)]
            if masked:
                scores = [jnp.where(ok, s, LOWER) for s in scores]
            old = [m_ref[h, 0:1] for h in range(2)]
            tops = [jnp.max(s, axis=0, keepdims=True) for s in scores]
            new = [jnp.maximum(a, b) for a, b in zip(old, tops)]
            fade = [jnp.exp(a - b) for a, b in zip(old, new)]
            ws = [jnp.exp(s - n).astype(bf16) for s, n in zip(scores, new)]
            sums = [dot(vx[h, :, keys], ws[h]) for h in range(2)]
            for h in range(2):
                acc[h] = acc[h] * fade[h] + sums[h]
                m_ref[h, 0:1] = new[h]
            return 0

        lax.fori_loop(begin, full_begin, functools.partial(visit, True), 0)
        lax.fori_loop(full_begin, full_stop, functools.partial(visit, False), 0)
        lax.fori_loop(full_stop, stop, functools.partial(visit, True), 0)
        for h in range(2):
            total = acc[h, HEAD_DIM : HEAD_DIM + 1]
            o_t[h * HEAD_DIM : (h + 1) * HEAD_DIM, rows] = acc[h, :HEAD_DIM] / total
            lse[h : h + 1, rows] = m_ref[h, 0:1] + jnp.log(total)
        ob[rows] = o_t[:, rows].T.astype(bf16)
        return 0

    lax.fori_loop(0, length // bq, query_block, 0)
    stores = piece_copies(ids, outs, ob, sem_out, slots, share, outward=True)
    for c in stores:
        c.start()
    for c in stores:
        c.wait()


def attend_cost(length, matmuls):
    pairs = length * length // 2
    return pl.CostEstimate(
        flops=2 * pairs * 256 * 2 * matmuls,
        bytes_accessed=length * PAIR * 2 * 8,
        transcendentals=2 * pairs,
    )


def attend(ids, pieces, groups, slots, docs, pics, bq, bk):
    rows = pieces[0].shape[0]
    n = len(pieces)
    length = rows * n
    share = rows // slots
    dims = (n, groups, slots, share, length, docs, pics, bq, bk)
    anywhere = pl.BlockSpec(memory_space=pl.ANY)
    out = pl.pallas_call(
        functools.partial(attend_kernel, dims),
        grid_spec=pltpu.PrefetchScalarGridSpec(
            num_scalar_prefetch=1,
            grid=(1,),
            in_specs=[anywhere] * n,
            out_specs=[anywhere] * groups
            + [
                pl.BlockSpec((PAIR, length), lambda i, ids: (0, 0)),
                pl.BlockSpec((8, length), lambda i, ids: (0, 0)),
            ],
            scratch_shapes=[
                pltpu.VMEM((length, 3 * PAIR), bf16),
                pltpu.VMEM((2, HEAD_DIM + 16, length), bf16),
                pltpu.VMEM((length, PAIR), bf16),
                pltpu.VMEM((2, HEAD_DIM + 16, bq), f32),
                pltpu.VMEM((2, 8, bq), f32),
                pltpu.SemaphoreType.DMA((n * slots,)),
                pltpu.SemaphoreType.DMA((groups * slots,)),
            ],
        ),
        out_shape=[jax.ShapeDtypeStruct((rows, PAIR), bf16)] * groups
        + [
            jax.ShapeDtypeStruct((PAIR, length), f32),
            jax.ShapeDtypeStruct((8, length), f32),
        ],
        compiler_params=pltpu.CompilerParams(vmem_limit_bytes=56 << 20),
        cost_estimate=attend_cost(length, 2),
        name="attend",
    )(ids, *pieces)
    return out[:groups], out[groups], out[groups + 1]


def attend_back_kernel(dims, ids, *refs):
    pieces, groups, slots, share, length, docs, pics, bq, bk = dims
    ins = refs[:pieces]
    grads = refs[pieces : 2 * pieces]
    o_t, lse, cos_ref, sin_ref = refs[2 * pieces : 2 * pieces + 4]
    outs = refs[2 * pieces + 4 : 2 * pieces + 4 + groups]
    qkv, dob, kt, dq_t, dk, dv, sem_in, sem_grad, sem_out = refs[2 * pieces + 4 + groups :]
    loads = piece_copies(ids, ins, qkv, sem_in, slots, share)
    loads += piece_copies(ids, grads, dob, sem_grad, slots, share)
    for c in loads:
        c.start()
    for c in loads:
        c.wait()

    def prepare(j, _):
        rows = pl.ds(pl.multiple_of(j * bk, bk), bk)
        kt[:, rows] = qkv[rows, PAIR : 2 * PAIR].astype(f32).T.astype(bf16)
        dk[rows] = jnp.zeros((bk, PAIR), f32)
        dv[rows] = jnp.zeros((bk, PAIR), f32)
        return 0

    lax.fori_loop(0, length // bk, prepare, 0)
    lane = lax.broadcasted_iota(jnp.int32, (bq, PAIR), 1)

    def turn_back(x, rows):
        return x * cos_ref[rows] - swap_halves(x) * sin_ref[rows]

    def query_block(i, _):
        first = i * bq
        rows = pl.ds(pl.multiple_of(first, bq), bq)
        q = qkv[rows, :PAIR].astype(f32) * SCALE
        do = dob[rows].astype(f32)
        q_of = []
        do_of = []
        for h in range(2):
            mine = (lane < HEAD_DIM) == (h == 0)
            q_of.append(jnp.where(mine, q, 0.0).astype(bf16))
            do_of.append(jnp.where(mine, do, 0.0).astype(bf16))
        prod = do.T * o_t[:, rows]
        delta = [
            jnp.sum(prod[h * HEAD_DIM : (h + 1) * HEAD_DIM], axis=0, keepdims=True)
            for h in range(2)
        ]
        dq_t[...] = jnp.zeros_like(dq_t)
        lo, hi = reach(
            ids, first + lax.broadcasted_iota(jnp.int32, (1, bq), 1), docs, pics, length
        )
        begin, full_begin, full_stop, stop = block_ranges(
            ids, first, bq, bk, docs, pics, length
        )

        def visit(masked, j, _):
            keys = pl.ds(pl.multiple_of(j * bk, bk), bk)
            k = qkv[keys, PAIR : 2 * PAIR]
            v = qkv[keys, 2 * PAIR :]
            if masked:
                p = j * bk + lax.broadcasted_iota(jnp.int32, (bk, bq), 0)
                ok = (p >= lo) & (p < hi)
            dk_sum = dk[keys]
            dv_sum = dv[keys]
            for h in range(2):
                feats = slice(h * HEAD_DIM, (h + 1) * HEAD_DIM)
                s = dot(k, q_of[h], NT)
                if masked:
                    s = jnp.where(ok, s, LOWER)
                w = jnp.exp(s - lse[h : h + 1, rows])
                dw = dot(v, do_of[h], NT)
                ds = (w * (dw - delta[h])).astype(bf16)
                dv_sum = dv_sum + dot(w.astype(bf16), do_of[h])
                dk_sum = dk_sum + dot(ds, q_of[h])
                dq_t[feats] += dot(kt[feats, keys], ds)
            dk[keys] = dk_sum
            dv[keys] = dv_sum
            return 0

        lax.fori_loop(begin, full_begin, functools.partial(visit, True), 0)
        lax.fori_loop(full_begin, full_stop, functools.partial(visit, False), 0)
        lax.fori_loop(full_stop, stop, functools.partial(visit, True), 0)
        dq = dq_t[...].T * SCALE
        qkv[rows, :PAIR] = turn_back(dq, rows).astype(bf16)
        return 0

    lax.fori_loop(0, length // bq, query_block, 0)

    def finish(j, _):
        rows = pl.ds(pl.multiple_of(j * bk, bk), bk)
        qkv[rows, PAIR : 2 * PAIR] = turn_back(dk[rows], rows).astype(bf16)
        qkv[rows, 2 * PAIR :] = dv[rows].astype(bf16)
        return 0

    lax.fori_loop(0, length // bk, finish, 0)
    stores = piece_copies(ids, outs, qkv, sem_out, slots, share, outward=True)
    for c in stores:
        c.start()
    for c in stores:
        c.wait()


def attend_back(ids, pieces, grads, o_t, lse, tables, groups, slots, docs, pics, bq, bk):
    rows = pieces[0].shape[0]
    n = len(pieces)
    length = rows * n
    share = rows // slots
    dims = (n, groups, slots, share, length, docs, pics, bq, bk)
    anywhere = pl.BlockSpec(memory_space=pl.ANY)
    once = dict(pipeline_mode=pl.Buffered(1))
    return pl.pallas_call(
        functools.partial(attend_back_kernel, dims),
        grid_spec=pltpu.PrefetchScalarGridSpec(
            num_scalar_prefetch=1,
            grid=(1,),
            in_specs=[anywhere] * (2 * n)
            + [
                pl.BlockSpec((PAIR, length), lambda i, ids: (0, 0), **once),
                pl.BlockSpec((8, length), lambda i, ids: (0, 0), **once),
                pl.BlockSpec((length, PAIR), lambda i, ids: (0, 0), **once),
                pl.BlockSpec((length, PAIR), lambda i, ids: (0, 0), **once),
            ],
            out_specs=[anywhere] * groups,
            scratch_shapes=[
                pltpu.VMEM((length, 3 * PAIR), bf16),
                pltpu.VMEM((length, PAIR), bf16),
                pltpu.VMEM((PAIR, length), bf16),
                pltpu.VMEM((PAIR, bq), f32),
                pltpu.VMEM((length, PAIR), f32),
                pltpu.VMEM((length, PAIR), f32),
                pltpu.SemaphoreType.DMA((n * slots,)),
                pltpu.SemaphoreType.DMA((n * slots,)),
                pltpu.SemaphoreType.DMA((groups * slots,)),
            ],
        ),
        out_shape=[jax.ShapeDtypeStruct((rows, 3 * PAIR), bf16)] * groups,
        compiler_params=pltpu.CompilerParams(vmem_limit_bytes=56 << 20),
        cost_estimate=attend_cost(length, 5),
        name="attend_back",
    )(ids, *pieces, *grads, o_t, lse, *tables)


def join_kernel(groups, kinds, slots, dims, ids, *refs):
    pieces = refs[:groups]
    own = refs[groups : groups + kinds]
    oth = refs[groups + kinds : groups + 2 * kinds]
    joined = refs[groups + 2 * kinds]
    parts = refs[groups + 2 * kinds + 1 :]
    inner = groups * PAIR
    half = parts[0].shape[1] // 2
    for s in range(groups):
        group = (ids[1] & (groups - 1)) ^ s
        for j in range(kinds):
            cols = pl.ds(pl.multiple_of(j * inner + group * PAIR, PAIR), PAIR)
            joined[:, cols] = pieces[s][:, j * PAIR : (j + 1) * PAIR]
    for side, weights in enumerate((own, oth)):
        total = None
        for j, w in enumerate(weights):
            term = dot(joined[:, j * inner : (j + 1) * inner], w[...], dims)
            total = term if total is None else total + term
        for i in range(slots):

            @pl.when(pl.program_id(0) == i)
            def _():
                parts[i][:, side * half : (side + 1) * half] = total.astype(parts[i].dtype)


def join(ids, pieces, own, oth, slots, dims):
    groups = len(pieces)
    kinds = len(own)
    rows = pieces[0].shape[0]
    share = rows // slots
    inner = groups * PAIR
    width = 2 * (own[0].shape[0] if dims == NT else own[0].shape[1])
    whole = lambda i, ids: (0, 0)
    by_row = lambda i, ids: (i, 0)
    out = pl.pallas_call(
        functools.partial(join_kernel, groups, kinds, slots, dims),
        grid_spec=pltpu.PrefetchScalarGridSpec(
            num_scalar_prefetch=1,
            grid=(slots,),
            in_specs=[pl.BlockSpec((share, kinds * PAIR), by_row)] * groups
            + [pl.BlockSpec(own[0].shape, whole)] * (2 * kinds),
            out_specs=[pl.BlockSpec((share, kinds * inner), by_row)]
            + [pl.BlockSpec((share, width), whole)] * slots,
        ),
        out_shape=[jax.ShapeDtypeStruct((rows, kinds * inner), bf16)]
        + [jax.ShapeDtypeStruct((share, width), f32 if i == 0 else bf16) for i in range(slots)],
        compiler_params=pltpu.CompilerParams(vmem_limit_bytes=44 << 20),
        cost_estimate=pl.CostEstimate(
            flops=2 * rows * width * inner * kinds,
            bytes_accessed=rows * width * 3 + kinds * (width * inner * 2 + rows * inner * 4),
            transcendentals=0,
        ),
    )(ids, *pieces, *own, *oth)
    return out[0], out[1:]


def hold(*groups):
    return lax.optimization_barrier(groups)


def local(
    tokens,
    ln1_gain,
    ln1_shift,
    q_weight,
    k_weight,
    v_weight,
    q_bias,
    k_bias,
    v_bias,
    o_weight,
    ln2_gain,
    ln2_shift,
    gate_weight,
    up_weight,
    down_weight,
    cotangent,
    doc_lengths,
    picture_starts,
):
    me = lax.axis_index(SHARD)
    ctx = lax.axis_index(CONTEXT)
    ctxs = lax.axis_size(CONTEXT)
    ten = lax.axis_index(TENSOR)
    slots = lax.axis_size(TENSOR)
    rows, width = tokens.shape[1:]
    half = width // 2
    share = rows // slots
    inner = q_weight.shape[1]
    groups = inner // PAIR
    heads_here = inner // HEAD_DIM
    docs = doc_lengths.shape[1]
    pics = picture_starts.shape[1]
    length = ctxs * rows
    quarter = half // ctxs
    bq = min(512, rows)
    bk = min(512, rows)
    assert ctxs % groups == 0 and ctxs & (ctxs - 1) == 0 and slots & (slots - 1) == 0

    def by_shard(x):
        turned = jnp.concatenate([x[..., half:], x[..., :half]], axis=-1)
        return jnp.where(me == 0, x, turned)

    def slot_rows(x, i):
        return lax.dynamic_slice_in_dim(x, (ten ^ i) * share, share, 0)

    def other_half(x):
        return swap_with(x, SHARD, 1)

    own_qkv = (q_weight, k_weight, v_weight)
    oth_qkv = tuple(other_half(w) for w in own_qkv)
    doc_ends = jnp.cumsum(doc_lengths[0])
    ids = jnp.concatenate(
        [
            jnp.stack([me, ctx, ten, ctx * 0]).astype(jnp.int32),
            doc_ends.astype(jnp.int32),
            picture_starts[0].astype(jnp.int32),
        ]
    )
    local_tables = rotary_tables(ctx * rows + jnp.arange(rows, dtype=jnp.int32))
    k_bias_wide = jnp.pad(
        k_bias.astype(f32).reshape(heads_here, ROT), ((0, 0), (0, HEAD_DIM - ROT))
    ).reshape(1, inner)
    h1, send = project(
        ids,
        tokens[0],
        ln1_gain.reshape(1, width),
        ln1_shift.reshape(1, width),
        own_qkv,
        oth_qkv,
        (q_bias.astype(f32).reshape(1, inner), k_bias_wide, v_bias.astype(f32).reshape(1, inner)),
        local_tables,
        groups,
        slots,
    )

    (send, later) = hold(
        send,
        (
            o_weight,
            gate_weight,
            up_weight,
            down_weight,
            cotangent[0],
            tokens[0],
            jnp.arange(length, dtype=jnp.int32),
        ),
    )
    o_weight, gate_weight, up_weight, down_weight, cot_rows, x_rows, positions = later
    pieces = [send[0]] + [swap_with(send[s % groups], CONTEXT, s) for s in range(1, ctxs)]
    down_oth, o_oth, gate_oth, up_oth = map(
        other_half, (down_weight, o_weight, gate_weight, up_weight)
    )
    full_tables = rotary_tables(positions)
    cot_all = by_shard(jnp.concatenate([slot_rows(cot_rows, i) for i in range(slots)], axis=0))
    x_share = by_shard(slot_rows(x_rows, 0)).astype(f32)
    down_full = jnp.concatenate([down_weight, down_oth], axis=1)
    o_full = jnp.concatenate([o_weight, o_oth], axis=1)
    dm_all = dot(cot_all, down_full, NT)
    gate_full = jnp.concatenate([gate_weight, gate_oth], axis=0)
    up_full = jnp.concatenate([up_weight, up_oth], axis=0)
    gain_two = by_shard(ln2_gain.astype(f32))
    shift_two = by_shard(ln2_shift.astype(f32))
    gain_one = by_shard(ln1_gain.astype(f32))
    pieces, ready = hold(
        pieces, (down_full, o_full, gate_full, up_full, cot_all, dm_all, full_tables, x_share)
    )
    down_full, o_full, gate_full, up_full, cot_all, dm_all, full_tables, x_share = ready

    attn_send, o_t, lse = attend(ids, pieces, groups, slots, docs, pics, bq, bk)
    attn, attn_parts = join(
        ids,
        [attn_send[0]] + [swap_with(attn_send[s], CONTEXT, s) for s in range(1, groups)],
        (o_weight,),
        (o_oth,),
        slots,
        NN,
    )

    mid = share // 2

    def send_rows(parts):
        return [swap_with(parts[i].astype(bf16), TENSOR, i) for i in range(1, slots)]

    def relay_sums(parts):
        if slots != 4:
            return send_rows(parts)
        one, two, far = (parts[i].astype(bf16) for i in range(1, 4))
        far_two = swap_with(far[:mid], TENSOR, 1)
        far_one = swap_with(far[mid:], TENSOR, 2)
        first = swap_with(one[:mid], TENSOR, 1)
        last = swap_with(two[mid:], TENSOR, 2)
        two = (two[:mid].astype(f32) + far_two.astype(f32)).astype(bf16)
        one = (one[mid:].astype(f32) + far_one.astype(f32)).astype(bf16)
        two = swap_with(two, TENSOR, 2)
        one = swap_with(one, TENSOR, 1)
        return [
            jnp.concatenate([first, one], axis=0),
            jnp.concatenate([two, last], axis=0),
        ]

    def add_rows(own, received):
        for part in received:
            own = own + part.astype(f32)
        return own

    def gather_rows(block):
        if slots != 4:
            return [block] + [swap_with(block, TENSOR, i) for i in range(1, slots)]
        one_last = swap_with(block[mid:], TENSOR, 1)
        two_first = swap_with(block[:mid], TENSOR, 2)
        one_first = swap_with(block[:mid], TENSOR, 1)
        two_last = swap_with(block[mid:], TENSOR, 2)
        far_first = swap_with(two_first, TENSOR, 1)
        far_last = swap_with(one_last, TENSOR, 2)
        return [
            block,
            jnp.concatenate([one_first, one_last], axis=0),
            jnp.concatenate([two_first, two_last], axis=0),
            jnp.concatenate([far_first, far_last], axis=0),
        ]

    def slot_of(x, i):
        return x[i * share : (i + 1) * share]

    x1 = x_share + add_rows(attn_parts[0], relay_sums(attn_parts))
    mean2 = jnp.mean(x1, axis=-1, keepdims=True)
    cent2 = x1 - mean2
    inv2 = lax.rsqrt(jnp.mean(cent2 * cent2, axis=-1, keepdims=True) + EPS)
    unit2 = cent2 * inv2
    h2 = gather_rows((unit2 * gain_two + shift_two).astype(bf16))

    hidden = []
    gate_grad = []
    up_grad = []
    norm2_parts = []
    dh2_received = []
    for i in range(slots):
        dm = slot_of(dm_all, i)
        g = dot(h2[i], gate_full)
        u = dot(h2[i], up_full)
        sig = jax.nn.sigmoid(g)
        act = g * sig
        hidden.append((act * u).astype(bf16))
        gate_grad.append((dm * u * sig * (1.0 + g * (1.0 - sig))).astype(bf16))
        up_grad.append((dm * act).astype(bf16))
        part = dot(gate_grad[i], gate_full, NT) + dot(up_grad[i], up_full, NT)
        norm2_parts.append(part if i == 0 else part.astype(bf16))
        if i + 1 < slots:
            norm2_parts[i], h2[i + 1] = hold(norm2_parts[i], h2[i + 1])
        if i > 0:
            dh2_received.append(swap_with(norm2_parts[i], TENSOR, i))

    def blocks_of(mine, theirs, axis):
        def block(x, d):
            return lax.dynamic_slice_in_dim(x, (ctx ^ d) * quarter, quarter, axis).astype(f32)

        return {d: block(mine, d) + block(theirs, d) for d in range(ctxs)}

    def scatter_step(parts, bit):
        parts = dict(parts)
        for d in sorted((d for d in parts if d & bit), reverse=True):
            parts[d ^ bit] += swap_with(parts.pop(d).astype(bf16), CONTEXT, bit).astype(f32)
        return parts

    def scatter_rest(parts):
        bit = 2
        while bit < ctxs:
            parts = scatter_step(parts, bit)
            bit *= 2
        return parts[0]

    h2_all, gate_all, up_all, hidden_all = (
        jnp.concatenate(blocks, axis=0) for blocks in (h2, gate_grad, up_grad, hidden)
    )

    gate_theirs = dot(h2_all[:, half:], gate_all, TN).astype(bf16)
    up_theirs = dot(h2_all[:, half:], up_all, TN).astype(bf16)
    gate_theirs = other_half(gate_theirs)
    up_theirs = other_half(up_theirs)
    gate_mine = dot(h2_all[:, :half], gate_all, TN).astype(bf16)
    up_mine = dot(h2_all[:, :half], up_all, TN).astype(bf16)
    gate_parts = scatter_step(blocks_of(gate_mine, gate_theirs, 0), 1)
    up_parts = scatter_step(blocks_of(up_mine, up_theirs, 0), 1)
    dh2 = add_rows(norm2_parts[0], dh2_received)
    cot_share = slot_of(cot_all, 0).astype(f32)
    e2 = dh2 * gain_two
    dx1 = cot_share + inv2 * (
        e2
        - jnp.mean(e2, axis=-1, keepdims=True)
        - unit2 * jnp.mean(e2 * unit2, axis=-1, keepdims=True)
    )
    dx1_slots = gather_rows(dx1.astype(bf16))

    down_theirs = dot(hidden_all, cot_all[:, half:], TN).astype(bf16)
    down_mine = dot(hidden_all, cot_all[:, :half], TN).astype(bf16)
    out_all = dot(hidden_all, down_full).astype(bf16)
    down_theirs = other_half(down_theirs)
    dx1b = jnp.concatenate(dx1_slots, axis=0)
    d_attn = dot(dx1b, o_full, NT).astype(bf16)
    d_send = [
        lax.dynamic_slice_in_dim(d_attn, ((ctx & (groups - 1)) ^ s) * PAIR, PAIR, 1)
        for s in range(groups)
    ]
    d_send, dx1b, out_all = hold(d_send, dx1b, out_all)
    d_pieces = [d_send[0]] + [
        swap_with(d_send[s % groups], CONTEXT, s) for s in range(1, ctxs)
    ]

    o_theirs = dot(attn, dx1b[:, half:], TN).astype(bf16)
    o_mine = dot(attn, dx1b[:, :half], TN).astype(bf16)
    o_theirs = other_half(o_theirs)

    out_received = send_rows([slot_of(out_all, i) for i in range(slots)])
    gate_out = scatter_rest(gate_parts)
    up_out = scatter_rest(up_parts)
    down_parts = scatter_step(blocks_of(down_mine, down_theirs, 1), 1)
    back = attend_back(
        ids, pieces, d_pieces, o_t, lse, full_tables, groups, slots, docs, pics, bq, bk
    )
    back_rest = [swap_with(back[s], CONTEXT, s) for s in range(1, groups)]

    output = by_shard(
        (x1 + add_rows(slot_of(out_all, 0).astype(f32), out_received)).astype(bf16)
    )[None]
    o_parts = scatter_step(blocks_of(o_mine, o_theirs, 1), 1)
    down_grad = scatter_rest(down_parts)
    o_grad = scatter_rest(o_parts)

    d_qkv, norm1_parts = join(ids, [back[0]] + back_rest, own_qkv, oth_qkv, slots, NT)
    norm1_parts, d_qkv = hold(norm1_parts, d_qkv)
    dh1_received = send_rows(norm1_parts)
    qkv_theirs = other_half(dot(h1[:, half:], d_qkv, TN).astype(bf16))
    qkv_mine = dot(h1[:, :half], d_qkv, TN).astype(bf16)
    qkv_parts = scatter_step(blocks_of(qkv_mine, qkv_theirs, 0), 1)
    qkv_grad = scatter_rest(qkv_parts)
    dh1 = add_rows(norm1_parts[0], dh1_received)

    mean1 = jnp.mean(x_share, axis=-1, keepdims=True)
    cent1 = x_share - mean1
    inv1 = lax.rsqrt(jnp.mean(cent1 * cent1, axis=-1, keepdims=True) + EPS)
    unit1 = cent1 * inv1
    e1 = dh1 * gain_one
    tokens_grad = dx1 + inv1 * (
        e1
        - jnp.mean(e1, axis=-1, keepdims=True)
        - unit1 * jnp.mean(e1 * unit1, axis=-1, keepdims=True)
    )
    tokens_grad = by_shard(tokens_grad)[None]

    norms = jnp.stack(
        [
            jnp.sum(dh1 * unit1, axis=0),
            jnp.sum(dh1, axis=0),
            jnp.sum(dh2 * unit2, axis=0),
            jnp.sum(dh2, axis=0),
        ]
    )
    norms = sum_over(by_shard(norms), TENSOR)
    bias = jnp.sum(d_qkv.astype(f32), axis=0, keepdims=True)
    sums = sum_over(jnp.concatenate([norms.reshape(1, 4 * width), bias], axis=1), SHARD)
    sums = sum_over(sums, CONTEXT)
    norms = sums[0, : 4 * width].reshape(4, width)
    bias = sums[0, 4 * width :]
    k_bias_grad = bias[inner : 2 * inner].reshape(heads_here, HEAD_DIM)[:, :ROT]
    return (
        output,
        tokens_grad,
        norms[0],
        norms[1],
        qkv_grad[:, :inner],
        qkv_grad[:, inner : 2 * inner],
        qkv_grad[:, 2 * inner :],
        bias[:inner],
        k_bias_grad.reshape(heads_here * ROT),
        bias[2 * inner :],
        o_grad,
        norms[2],
        norms[3],
        gate_out,
        up_out,
        down_grad,
    )


def solution(mesh):
    tokens = P(SHARD, CONTEXT, None)
    inward = P(SHARD, TENSOR)
    outward = P(TENSOR, SHARD)
    vector = P(TENSOR)
    placed = (
        tokens,
        P(),
        P(),
        inward,
        inward,
        inward,
        vector,
        vector,
        vector,
        outward,
        P(),
        P(),
        inward,
        inward,
        outward,
        tokens,
        P(SHARD, None),
        P(SHARD, None),
    )
    share = P(SHARD, (CONTEXT, TENSOR), None)
    grad_in = P((SHARD, CONTEXT), TENSOR)
    grad_out = P(TENSOR, (SHARD, CONTEXT))

    return jax.shard_map(
        local,
        mesh=mesh,
        in_specs=placed,
        out_specs=(
            share,
            share,
            P(),
            P(),
            grad_in,
            grad_in,
            grad_in,
            vector,
            vector,
            vector,
            grad_out,
            P(),
            P(),
            grad_in,
            grad_in,
            grad_out,
        ),
        check_vma=False,
    )
```

```python
import functools

import jax
import jax.numpy as jnp
from jax import lax
from jax.experimental import pallas as pl
from jax.experimental.pallas import tpu as pltpu
from jax.sharding import PartitionSpec as P

HEAD_DIM = 64
ROT = 16
SPAN = 256
PAIR = 128
EPS = 1e-05
LOW = -1e30
LOWER = -2e30
SCALE = HEAD_DIM ** (-0.5)

SHARD = "shard"
CONTEXT = "context"
TENSOR = "tensor"

f32 = jnp.float32
bf16 = jnp.bfloat16


NT = (((1,), (1,)), ((), ()))
NN = (((1,), (0,)), ((), ()))
TN = (((0,), (0,)), ((), ()))


def dot(a, b, dims=NN):
    return lax.dot_general(a, b, dims, preferred_element_type=f32)


def swap_with(x, axis, bit):
    size = lax.axis_size(axis)
    return lax.ppermute(x, axis, [(i, i ^ bit) for i in range(size)])


def sum_over(x, axis):
    terms = [x] + [swap_with(x, axis, i) for i in range(1, lax.axis_size(axis))]
    while len(terms) > 1:
        terms = [terms[i] + terms[i + 1] for i in range(0, len(terms), 2)]
    return terms[0]


def rotary_tables(positions):
    half = ROT // 2
    freq = 10000.0 ** (-(2.0 * jnp.arange(half).astype(f32)) / ROT)
    angles = freq[:, None] * positions.astype(f32)[None, :]
    parts = jnp.concatenate([jnp.cos(angles), jnp.sin(angles)], axis=0)
    lane = jnp.arange(PAIR) % HEAD_DIM
    row = jnp.arange(half)[:, None]
    hit = (lane[None, :] % half == row) & (lane[None, :] < ROT)
    spread_cos = jnp.concatenate([hit, jnp.zeros_like(hit)], axis=0).astype(f32)
    sign = jnp.where(lane < half, -1.0, 1.0)[None, :]
    spread_sin = jnp.concatenate([jnp.zeros_like(hit), hit], axis=0).astype(f32) * sign
    expand = functools.partial(
        lax.dot_general,
        dimension_numbers=TN,
        precision=lax.Precision.HIGHEST,
        preferred_element_type=f32,
    )
    rest = jnp.where(lane < ROT, 0.0, 1.0).astype(f32)
    return expand(parts, spread_cos) + rest[None, :], expand(parts, spread_sin)


def swap_halves(x):
    lane = lax.broadcasted_iota(jnp.int32, x.shape, 1) % HEAD_DIM
    return jnp.where(lane < ROT // 2, pltpu.roll(x, PAIR - ROT // 2, 1), pltpu.roll(x, ROT // 2, 1))


def project_kernel(
    groups,
    ids,
    x_own,
    x_oth,
    gain_own,
    gain_oth,
    shift_own,
    shift_oth,
    wq_own,
    wk_own,
    wv_own,
    wq_oth,
    wk_oth,
    wv_oth,
    q_bias,
    k_bias,
    v_bias,
    cos_ref,
    sin_ref,
    *rest,
):
    h_ref, pieces, (qs, ks, vs) = rest[0], rest[1 : 1 + groups], rest[1 + groups :]
    half = x_own.shape[1]
    a = x_own[...].astype(f32)
    b = x_oth[...].astype(f32)
    count = 1.0 / (2 * half)
    mean = (jnp.sum(a, axis=1, keepdims=True) + jnp.sum(b, axis=1, keepdims=True)) * count
    a = a - mean
    b = b - mean
    var = (jnp.sum(a * a, axis=1, keepdims=True) + jnp.sum(b * b, axis=1, keepdims=True)) * count
    inv = lax.rsqrt(var + EPS)
    ha = (a * inv * gain_own[...].astype(f32) + shift_own[...].astype(f32)).astype(bf16)
    hb = (b * inv * gain_oth[...].astype(f32) + shift_oth[...].astype(f32)).astype(bf16)
    h_ref[:, :half] = ha
    h_ref[:, half:] = hb
    qs[...] = dot(ha, wq_own[...]) + dot(hb, wq_oth[...]) + q_bias[...]
    ks[...] = dot(ha, wk_own[...]) + dot(hb, wk_oth[...]) + k_bias[...]
    vs[...] = dot(ha, wv_own[...]) + dot(hb, wv_oth[...]) + v_bias[...]
    cos = cos_ref[...]
    sin = sin_ref[...]
    for s in range(groups):
        group = (ids[1] & (groups - 1)) ^ s
        cols = pl.ds(pl.multiple_of(group * PAIR, PAIR), PAIR)
        q = qs[:, cols]
        k = ks[:, cols]
        pieces[s][:, :PAIR] = (q * cos + swap_halves(q) * sin).astype(bf16)
        pieces[s][:, PAIR : 2 * PAIR] = (k * cos + swap_halves(k) * sin).astype(bf16)
        pieces[s][:, 2 * PAIR :] = vs[:, cols].astype(bf16)


def project(ids, tokens, gain, shift, own, other, biases, tables, groups, slots):
    rows, width = tokens.shape
    half = width // 2
    share = rows // slots
    inner = own[0].shape[1]

    def row_block(i, ids):
        return ids[2] ^ i

    whole = lambda i, ids: (0, 0)
    weight = pl.BlockSpec((half, inner), whole)
    bias = pl.BlockSpec((1, inner), whole)
    in_specs = [
        pl.BlockSpec((share, half), lambda i, ids: (row_block(i, ids), ids[0])),
        pl.BlockSpec((share, half), lambda i, ids: (row_block(i, ids), 1 - ids[0])),
        pl.BlockSpec((1, half), lambda i, ids: (0, ids[0])),
        pl.BlockSpec((1, half), lambda i, ids: (0, 1 - ids[0])),
        pl.BlockSpec((1, half), lambda i, ids: (0, ids[0])),
        pl.BlockSpec((1, half), lambda i, ids: (0, 1 - ids[0])),
    ]
    in_specs += [weight] * 6 + [bias] * 3
    in_specs += [pl.BlockSpec((share, PAIR), lambda i, ids: (row_block(i, ids), 0))] * 2
    out = pl.pallas_call(
        functools.partial(project_kernel, groups),
        grid_spec=pltpu.PrefetchScalarGridSpec(
            num_scalar_prefetch=1,
            grid=(slots,),
            in_specs=in_specs,
            out_specs=[pl.BlockSpec((share, width), lambda i, ids: (i, 0))]
            + [pl.BlockSpec((share, 3 * PAIR), lambda i, ids: (i, 0))] * groups,
            scratch_shapes=[pltpu.VMEM((share, inner), f32)] * 3,
        ),
        out_shape=[jax.ShapeDtypeStruct((rows, width), bf16)]
        + [jax.ShapeDtypeStruct((rows, 3 * PAIR), bf16)] * groups,
        compiler_params=pltpu.CompilerParams(vmem_limit_bytes=56 << 20),
        cost_estimate=pl.CostEstimate(
            flops=2 * rows * width * inner * 3,
            bytes_accessed=rows * width * 4 + 3 * width * inner * 2 + rows * inner * 6,
            transcendentals=rows,
        ),
        name="project",
    )(ids, tokens, tokens, gain, gain, shift, shift, *own, *other, *biases, *tables)
    return out[0], out[1:]


def reach(ids, p, docs, pics, length):
    start = jnp.zeros_like(p)
    end = jnp.full_like(p, length)
    for j in range(docs):
        e = ids[4 + j]
        start = jnp.where(p >= e, jnp.maximum(start, e), start)
        end = jnp.where(p < e, jnp.minimum(end, e), end)
    far = p + 1
    for j in range(pics):
        b = ids[4 + docs + j]
        inside = (p >= b) & (p < b + SPAN)
        far = jnp.where(inside, jnp.maximum(far, jnp.minimum(b + SPAN, end)), far)
    return start, far


def block_ranges(ids, first, bq, bk, docs, pics, length):
    lo_a, hi_a = reach(ids, first, docs, pics, length)
    lo_b, hi_b = reach(ids, first + (bq - 1), docs, pics, length)
    begin = lo_a // bk
    stop = (hi_b + (bk - 1)) // bk
    full_begin = jnp.clip((lo_b + (bk - 1)) // bk, begin, stop)
    full_stop = jnp.clip(hi_a // bk, full_begin, stop)
    return begin, full_begin, full_stop, stop


def piece_copies(ids, pieces, whole, sems, slots, share, outward=False):
    copies = []
    for s, piece in enumerate(pieces):
        for i in range(slots):
            first = ((ids[1] ^ s) * slots + (ids[2] ^ i)) * share
            there = whole.at[pl.ds(pl.multiple_of(first, share), share)]
            here = piece.at[pl.ds(i * share, share)]
            src, dst = (there, here) if outward else (here, there)
            copies.append(pltpu.make_async_copy(src, dst, sems.at[s * slots + i]))
    return copies


def attend_kernel(dims, ids, *refs):
    pieces, groups, slots, share, length, docs, pics, bq, bk = dims
    ins = refs[:pieces]
    outs = refs[pieces : pieces + groups]
    o_t, lse = refs[pieces + groups : pieces + groups + 2]
    qkv, vx, ob, acc, m_ref, sem_in, sem_out = refs[pieces + groups + 2 :]
    loads = piece_copies(ids, ins, qkv, sem_in, slots, share)
    for c in loads:
        c.start()
    for c in loads:
        c.wait()

    def prepare(j, _):
        rows = pl.ds(pl.multiple_of(j * bk, bk), bk)
        v_t = qkv[rows, 2 * PAIR :].astype(f32).T
        ones = jnp.ones((16, bk), bf16)
        for h in range(2):
            vx[h, :HEAD_DIM, rows] = v_t[h * HEAD_DIM : (h + 1) * HEAD_DIM].astype(bf16)
            vx[h, HEAD_DIM:, rows] = ones
        return 0

    lax.fori_loop(0, length // bk, prepare, 0)
    lane = lax.broadcasted_iota(jnp.int32, (bq, PAIR), 1)

    def query_block(i, _):
        first = i * bq
        rows = pl.ds(pl.multiple_of(first, bq), bq)
        q = qkv[rows, :PAIR].astype(f32) * SCALE
        heads = [
            jnp.where((lane < HEAD_DIM) == (h == 0), q, 0.0).astype(bf16) for h in range(2)
        ]
        for h in range(2):
            acc[h] = jnp.zeros_like(acc[h])
            m_ref[h] = jnp.full_like(m_ref[h], LOW)
        lo, hi = reach(
            ids, first + lax.broadcasted_iota(jnp.int32, (1, bq), 1), docs, pics, length
        )
        begin, full_begin, full_stop, stop = block_ranges(
            ids, first, bq, bk, docs, pics, length
        )

        def visit(masked, j, _):
            keys = pl.ds(pl.multiple_of(j * bk, bk), bk)
            k = qkv[keys, PAIR : 2 * PAIR]
            if masked:
                p = j * bk + lax.broadcasted_iota(jnp.int32, (bk, bq), 0)
                ok = (p >= lo) & (p < hi)
            scores = [dot(k, heads[h], NT) for h in range(2)]
            if masked:
                scores = [jnp.where(ok, s, LOWER) for s in scores]
            old = [m_ref[h, 0:1] for h in range(2)]
            tops = [jnp.max(s, axis=0, keepdims=True) for s in scores]
            new = [jnp.maximum(a, b) for a, b in zip(old, tops)]
            fade = [jnp.exp(a - b) for a, b in zip(old, new)]
            ws = [jnp.exp(s - n).astype(bf16) for s, n in zip(scores, new)]
            sums = [dot(vx[h, :, keys], ws[h]) for h in range(2)]
            for h in range(2):
                acc[h] = acc[h] * fade[h] + sums[h]
                m_ref[h, 0:1] = new[h]
            return 0

        lax.fori_loop(begin, full_begin, functools.partial(visit, True), 0)
        lax.fori_loop(full_begin, full_stop, functools.partial(visit, False), 0)
        lax.fori_loop(full_stop, stop, functools.partial(visit, True), 0)
        for h in range(2):
            total = acc[h, HEAD_DIM : HEAD_DIM + 1]
            o_t[h * HEAD_DIM : (h + 1) * HEAD_DIM, rows] = acc[h, :HEAD_DIM] / total
            lse[h : h + 1, rows] = m_ref[h, 0:1] + jnp.log(total)
        ob[rows] = o_t[:, rows].T.astype(bf16)
        return 0

    lax.fori_loop(0, length // bq, query_block, 0)
    stores = piece_copies(ids, outs, ob, sem_out, slots, share, outward=True)
    for c in stores:
        c.start()
    for c in stores:
        c.wait()


def attend_cost(length, matmuls):
    pairs = length * length // 2
    return pl.CostEstimate(
        flops=2 * pairs * 256 * 2 * matmuls,
        bytes_accessed=length * PAIR * 2 * 8,
        transcendentals=2 * pairs,
    )


def attend(ids, pieces, groups, slots, docs, pics, bq, bk):
    rows = pieces[0].shape[0]
    n = len(pieces)
    length = rows * n
    share = rows // slots
    dims = (n, groups, slots, share, length, docs, pics, bq, bk)
    anywhere = pl.BlockSpec(memory_space=pl.ANY)
    out = pl.pallas_call(
        functools.partial(attend_kernel, dims),
        grid_spec=pltpu.PrefetchScalarGridSpec(
            num_scalar_prefetch=1,
            grid=(1,),
            in_specs=[anywhere] * n,
            out_specs=[anywhere] * groups
            + [
                pl.BlockSpec((PAIR, length), lambda i, ids: (0, 0)),
                pl.BlockSpec((8, length), lambda i, ids: (0, 0)),
            ],
            scratch_shapes=[
                pltpu.VMEM((length, 3 * PAIR), bf16),
                pltpu.VMEM((2, HEAD_DIM + 16, length), bf16),
                pltpu.VMEM((length, PAIR), bf16),
                pltpu.VMEM((2, HEAD_DIM + 16, bq), f32),
                pltpu.VMEM((2, 8, bq), f32),
                pltpu.SemaphoreType.DMA((n * slots,)),
                pltpu.SemaphoreType.DMA((groups * slots,)),
            ],
        ),
        out_shape=[jax.ShapeDtypeStruct((rows, PAIR), bf16)] * groups
        + [
            jax.ShapeDtypeStruct((PAIR, length), f32),
            jax.ShapeDtypeStruct((8, length), f32),
        ],
        compiler_params=pltpu.CompilerParams(vmem_limit_bytes=56 << 20),
        cost_estimate=attend_cost(length, 2),
        name="attend",
    )(ids, *pieces)
    return out[:groups], out[groups], out[groups + 1]


def attend_back_kernel(dims, ids, *refs):
    pieces, groups, slots, share, length, docs, pics, bq, bk = dims
    ins = refs[:pieces]
    grads = refs[pieces : 2 * pieces]
    o_t, lse, cos_ref, sin_ref = refs[2 * pieces : 2 * pieces + 4]
    outs = refs[2 * pieces + 4 : 2 * pieces + 4 + groups]
    qkv, dob, kt, dq_t, dk, dv, sem_in, sem_grad, sem_out = refs[2 * pieces + 4 + groups :]
    loads = piece_copies(ids, ins, qkv, sem_in, slots, share)
    loads += piece_copies(ids, grads, dob, sem_grad, slots, share)
    for c in loads:
        c.start()
    for c in loads:
        c.wait()

    def prepare(j, _):
        rows = pl.ds(pl.multiple_of(j * bk, bk), bk)
        kt[:, rows] = qkv[rows, PAIR : 2 * PAIR].astype(f32).T.astype(bf16)
        dk[rows] = jnp.zeros((bk, PAIR), f32)
        dv[rows] = jnp.zeros((bk, PAIR), f32)
        return 0

    lax.fori_loop(0, length // bk, prepare, 0)
    lane = lax.broadcasted_iota(jnp.int32, (bq, PAIR), 1)

    def turn_back(x, rows):
        return x * cos_ref[rows] - swap_halves(x) * sin_ref[rows]

    def query_block(i, _):
        first = i * bq
        rows = pl.ds(pl.multiple_of(first, bq), bq)
        q = qkv[rows, :PAIR].astype(f32) * SCALE
        do = dob[rows].astype(f32)
        q_of = []
        do_of = []
        for h in range(2):
            mine = (lane < HEAD_DIM) == (h == 0)
            q_of.append(jnp.where(mine, q, 0.0).astype(bf16))
            do_of.append(jnp.where(mine, do, 0.0).astype(bf16))
        prod = do.T * o_t[:, rows]
        delta = [
            jnp.sum(prod[h * HEAD_DIM : (h + 1) * HEAD_DIM], axis=0, keepdims=True)
            for h in range(2)
        ]
        dq_t[...] = jnp.zeros_like(dq_t)
        lo, hi = reach(
            ids, first + lax.broadcasted_iota(jnp.int32, (1, bq), 1), docs, pics, length
        )
        begin, full_begin, full_stop, stop = block_ranges(
            ids, first, bq, bk, docs, pics, length
        )

        def visit(masked, j, _):
            keys = pl.ds(pl.multiple_of(j * bk, bk), bk)
            k = qkv[keys, PAIR : 2 * PAIR]
            v = qkv[keys, 2 * PAIR :]
            if masked:
                p = j * bk + lax.broadcasted_iota(jnp.int32, (bk, bq), 0)
                ok = (p >= lo) & (p < hi)
            dk_sum = dk[keys]
            dv_sum = dv[keys]
            for h in range(2):
                feats = slice(h * HEAD_DIM, (h + 1) * HEAD_DIM)
                s = dot(k, q_of[h], NT)
                if masked:
                    s = jnp.where(ok, s, LOWER)
                w = jnp.exp(s - lse[h : h + 1, rows])
                dw = dot(v, do_of[h], NT)
                ds = (w * (dw - delta[h])).astype(bf16)
                dv_sum = dv_sum + dot(w.astype(bf16), do_of[h])
                dk_sum = dk_sum + dot(ds, q_of[h])
                dq_t[feats] += dot(kt[feats, keys], ds)
            dk[keys] = dk_sum
            dv[keys] = dv_sum
            return 0

        lax.fori_loop(begin, full_begin, functools.partial(visit, True), 0)
        lax.fori_loop(full_begin, full_stop, functools.partial(visit, False), 0)
        lax.fori_loop(full_stop, stop, functools.partial(visit, True), 0)
        dq = dq_t[...].T * SCALE
        qkv[rows, :PAIR] = turn_back(dq, rows).astype(bf16)
        return 0

    lax.fori_loop(0, length // bq, query_block, 0)

    def finish(j, _):
        rows = pl.ds(pl.multiple_of(j * bk, bk), bk)
        qkv[rows, PAIR : 2 * PAIR] = turn_back(dk[rows], rows).astype(bf16)
        qkv[rows, 2 * PAIR :] = dv[rows].astype(bf16)
        return 0

    lax.fori_loop(0, length // bk, finish, 0)
    stores = piece_copies(ids, outs, qkv, sem_out, slots, share, outward=True)
    for c in stores:
        c.start()
    for c in stores:
        c.wait()


def attend_back(ids, pieces, grads, o_t, lse, tables, groups, slots, docs, pics, bq, bk):
    rows = pieces[0].shape[0]
    n = len(pieces)
    length = rows * n
    share = rows // slots
    dims = (n, groups, slots, share, length, docs, pics, bq, bk)
    anywhere = pl.BlockSpec(memory_space=pl.ANY)
    once = dict(pipeline_mode=pl.Buffered(1))
    return pl.pallas_call(
        functools.partial(attend_back_kernel, dims),
        grid_spec=pltpu.PrefetchScalarGridSpec(
            num_scalar_prefetch=1,
            grid=(1,),
            in_specs=[anywhere] * (2 * n)
            + [
                pl.BlockSpec((PAIR, length), lambda i, ids: (0, 0), **once),
                pl.BlockSpec((8, length), lambda i, ids: (0, 0), **once),
                pl.BlockSpec((length, PAIR), lambda i, ids: (0, 0), **once),
                pl.BlockSpec((length, PAIR), lambda i, ids: (0, 0), **once),
            ],
            out_specs=[anywhere] * groups,
            scratch_shapes=[
                pltpu.VMEM((length, 3 * PAIR), bf16),
                pltpu.VMEM((length, PAIR), bf16),
                pltpu.VMEM((PAIR, length), bf16),
                pltpu.VMEM((PAIR, bq), f32),
                pltpu.VMEM((length, PAIR), f32),
                pltpu.VMEM((length, PAIR), f32),
                pltpu.SemaphoreType.DMA((n * slots,)),
                pltpu.SemaphoreType.DMA((n * slots,)),
                pltpu.SemaphoreType.DMA((groups * slots,)),
            ],
        ),
        out_shape=[jax.ShapeDtypeStruct((rows, 3 * PAIR), bf16)] * groups,
        compiler_params=pltpu.CompilerParams(vmem_limit_bytes=56 << 20),
        cost_estimate=attend_cost(length, 5),
        name="attend_back",
    )(ids, *pieces, *grads, o_t, lse, *tables)


def join_kernel(groups, kinds, slots, dims, ids, *refs):
    pieces = refs[:groups]
    own = refs[groups : groups + kinds]
    oth = refs[groups + kinds : groups + 2 * kinds]
    joined = refs[groups + 2 * kinds : groups + 3 * kinds]
    parts = refs[groups + 3 * kinds :]
    half = parts[0].shape[1] // 2
    for s in range(groups):
        group = (ids[1] & (groups - 1)) ^ s
        for j in range(kinds):
            cols = pl.ds(pl.multiple_of(group * PAIR, PAIR), PAIR)
            joined[j][:, cols] = pieces[s][:, j * PAIR : (j + 1) * PAIR]
    for side, weights in enumerate((own, oth)):
        total = None
        for j, w in enumerate(weights):
            term = dot(joined[j][...], w[...], dims)
            total = term if total is None else total + term
        for i in range(slots):

            @pl.when(pl.program_id(0) == i)
            def _():
                parts[i][:, side * half : (side + 1) * half] = total.astype(parts[i].dtype)


def join(ids, pieces, own, oth, slots, dims):
    groups = len(pieces)
    kinds = len(own)
    rows = pieces[0].shape[0]
    share = rows // slots
    inner = groups * PAIR
    width = 2 * (own[0].shape[0] if dims == NT else own[0].shape[1])
    whole = lambda i, ids: (0, 0)
    by_row = lambda i, ids: (i, 0)
    out = pl.pallas_call(
        functools.partial(join_kernel, groups, kinds, slots, dims),
        grid_spec=pltpu.PrefetchScalarGridSpec(
            num_scalar_prefetch=1,
            grid=(slots,),
            in_specs=[pl.BlockSpec((share, kinds * PAIR), by_row)] * groups
            + [pl.BlockSpec(own[0].shape, whole)] * (2 * kinds),
            out_specs=[pl.BlockSpec((share, inner), by_row)] * kinds
            + [pl.BlockSpec((share, width), whole)] * slots,
        ),
        out_shape=[jax.ShapeDtypeStruct((rows, inner), bf16)] * kinds
        + [jax.ShapeDtypeStruct((share, width), f32 if i == 0 else bf16) for i in range(slots)],
        compiler_params=pltpu.CompilerParams(vmem_limit_bytes=44 << 20),
        cost_estimate=pl.CostEstimate(
            flops=2 * rows * width * inner * kinds,
            bytes_accessed=rows * width * 3 + kinds * (width * inner * 2 + rows * inner * 4),
            transcendentals=0,
        ),
    )(ids, *pieces, *own, *oth)
    return out[:kinds], out[kinds:]


def hold(*groups):
    return lax.optimization_barrier(groups)


def local(
    tokens,
    ln1_gain,
    ln1_shift,
    q_weight,
    k_weight,
    v_weight,
    q_bias,
    k_bias,
    v_bias,
    o_weight,
    ln2_gain,
    ln2_shift,
    gate_weight,
    up_weight,
    down_weight,
    cotangent,
    doc_lengths,
    picture_starts,
):
    me = lax.axis_index(SHARD)
    ctx = lax.axis_index(CONTEXT)
    ctxs = lax.axis_size(CONTEXT)
    ten = lax.axis_index(TENSOR)
    slots = lax.axis_size(TENSOR)
    rows, width = tokens.shape[1:]
    half = width // 2
    share = rows // slots
    inner = q_weight.shape[1]
    groups = inner // PAIR
    heads_here = inner // HEAD_DIM
    docs = doc_lengths.shape[1]
    pics = picture_starts.shape[1]
    length = ctxs * rows
    quarter = half // ctxs
    bq = min(512, rows)
    bk = min(512, rows)
    assert ctxs % groups == 0 and ctxs & (ctxs - 1) == 0 and slots & (slots - 1) == 0

    def by_shard(x):
        turned = jnp.concatenate([x[..., half:], x[..., :half]], axis=-1)
        return jnp.where(me == 0, x, turned)

    def slot_rows(x, i):
        return lax.dynamic_slice_in_dim(x, (ten ^ i) * share, share, 0)

    def other_half(x):
        return swap_with(x, SHARD, 1)

    own_qkv = (q_weight, k_weight, v_weight)
    oth_qkv = tuple(other_half(w) for w in own_qkv)
    doc_ends = jnp.cumsum(doc_lengths[0])
    ids = jnp.concatenate(
        [
            jnp.stack([me, ctx, ten, ctx * 0]).astype(jnp.int32),
            doc_ends.astype(jnp.int32),
            picture_starts[0].astype(jnp.int32),
        ]
    )
    local_tables = rotary_tables(ctx * rows + jnp.arange(rows, dtype=jnp.int32))
    k_bias_wide = jnp.pad(
        k_bias.astype(f32).reshape(heads_here, ROT), ((0, 0), (0, HEAD_DIM - ROT))
    ).reshape(1, inner)
    h1, send = project(
        ids,
        tokens[0],
        ln1_gain.reshape(1, width),
        ln1_shift.reshape(1, width),
        own_qkv,
        oth_qkv,
        (q_bias.astype(f32).reshape(1, inner), k_bias_wide, v_bias.astype(f32).reshape(1, inner)),
        local_tables,
        groups,
        slots,
    )

    (send, later) = hold(
        send,
        (
            o_weight,
            gate_weight,
            up_weight,
            down_weight,
            cotangent[0],
            tokens[0],
            jnp.arange(length, dtype=jnp.int32),
        ),
    )
    o_weight, gate_weight, up_weight, down_weight, cot_rows, x_rows, positions = later
    pieces = [send[0]] + [swap_with(send[s % groups], CONTEXT, s) for s in range(1, ctxs)]
    down_oth, o_oth, gate_oth, up_oth = map(
        other_half, (down_weight, o_weight, gate_weight, up_weight)
    )
    full_tables = rotary_tables(positions)
    cot_all = by_shard(jnp.concatenate([slot_rows(cot_rows, i) for i in range(slots)], axis=0))
    x_share = by_shard(slot_rows(x_rows, 0)).astype(f32)
    down_full = jnp.concatenate([down_weight, down_oth], axis=1)
    o_full = jnp.concatenate([o_weight, o_oth], axis=1)
    dm_all = dot(cot_all, down_full, NT)
    gate_full = jnp.concatenate([gate_weight, gate_oth], axis=0)
    up_full = jnp.concatenate([up_weight, up_oth], axis=0)
    gain_two = by_shard(ln2_gain.astype(f32))
    shift_two = by_shard(ln2_shift.astype(f32))
    gain_one = by_shard(ln1_gain.astype(f32))
    pieces, ready = hold(
        pieces, (down_full, o_full, gate_full, up_full, cot_all, dm_all, full_tables, x_share)
    )
    down_full, o_full, gate_full, up_full, cot_all, dm_all, full_tables, x_share = ready

    attn_send, o_t, lse = attend(ids, pieces, groups, slots, docs, pics, bq, bk)
    (attn,), attn_parts = join(
        ids,
        [attn_send[0]] + [swap_with(attn_send[s], CONTEXT, s) for s in range(1, groups)],
        (o_weight,),
        (o_oth,),
        slots,
        NN,
    )

    mid = share // 2

    def send_rows(parts):
        return [swap_with(parts[i].astype(bf16), TENSOR, i) for i in range(1, slots)]

    def relay_sums(parts):
        if slots != 4:
            return send_rows(parts)
        one, two, far = (parts[i].astype(bf16) for i in range(1, 4))
        far_two = swap_with(far[:mid], TENSOR, 1)
        far_one = swap_with(far[mid:], TENSOR, 2)
        first = swap_with(one[:mid], TENSOR, 1)
        last = swap_with(two[mid:], TENSOR, 2)
        two = (two[:mid].astype(f32) + far_two.astype(f32)).astype(bf16)
        one = (one[mid:].astype(f32) + far_one.astype(f32)).astype(bf16)
        two = swap_with(two, TENSOR, 2)
        one = swap_with(one, TENSOR, 1)
        return [
            jnp.concatenate([first, one], axis=0),
            jnp.concatenate([two, last], axis=0),
        ]

    def add_rows(own, received):
        for part in received:
            own = own + part.astype(f32)
        return own

    def gather_rows(block):
        if slots != 4:
            return [block] + [swap_with(block, TENSOR, i) for i in range(1, slots)]
        one_last = swap_with(block[mid:], TENSOR, 1)
        two_first = swap_with(block[:mid], TENSOR, 2)
        one_first = swap_with(block[:mid], TENSOR, 1)
        two_last = swap_with(block[mid:], TENSOR, 2)
        far_first = swap_with(two_first, TENSOR, 1)
        far_last = swap_with(one_last, TENSOR, 2)
        return [
            block,
            jnp.concatenate([one_first, one_last], axis=0),
            jnp.concatenate([two_first, two_last], axis=0),
            jnp.concatenate([far_first, far_last], axis=0),
        ]

    def slot_of(x, i):
        return x[i * share : (i + 1) * share]

    x1 = x_share + add_rows(attn_parts[0], relay_sums(attn_parts))
    mean2 = jnp.mean(x1, axis=-1, keepdims=True)
    cent2 = x1 - mean2
    inv2 = lax.rsqrt(jnp.mean(cent2 * cent2, axis=-1, keepdims=True) + EPS)
    unit2 = cent2 * inv2
    h2 = gather_rows((unit2 * gain_two + shift_two).astype(bf16))

    hidden = []
    gate_grad = []
    up_grad = []
    norm2_parts = []
    dh2_received = []
    for i in range(slots):
        dm = slot_of(dm_all, i)
        g = dot(h2[i], gate_full)
        u = dot(h2[i], up_full)
        sig = jax.nn.sigmoid(g)
        act = g * sig
        hidden.append((act * u).astype(bf16))
        gate_grad.append((dm * u * sig * (1.0 + g * (1.0 - sig))).astype(bf16))
        up_grad.append((dm * act).astype(bf16))
        part = dot(gate_grad[i], gate_full, NT) + dot(up_grad[i], up_full, NT)
        norm2_parts.append(part if i == 0 else part.astype(bf16))
        if i + 1 < slots:
            norm2_parts[i], h2[i + 1] = hold(norm2_parts[i], h2[i + 1])
        if i > 0:
            dh2_received.append(swap_with(norm2_parts[i], TENSOR, i))

    def blocks_of(mine, theirs, axis):
        def block(x, d):
            return lax.dynamic_slice_in_dim(x, (ctx ^ d) * quarter, quarter, axis).astype(f32)

        return {d: block(mine, d) + block(theirs, d) for d in range(ctxs)}

    def scatter_step(parts, bit):
        parts = dict(parts)
        for d in sorted((d for d in parts if d & bit), reverse=True):
            parts[d ^ bit] += swap_with(parts.pop(d).astype(bf16), CONTEXT, bit).astype(f32)
        return parts

    def scatter_rest(parts):
        bit = 2
        while bit < ctxs:
            parts = scatter_step(parts, bit)
            bit *= 2
        return parts[0]

    h2_all, gate_all, up_all, hidden_all = (
        jnp.concatenate(blocks, axis=0) for blocks in (h2, gate_grad, up_grad, hidden)
    )

    gate_theirs = dot(h2_all[:, half:], gate_all, TN).astype(bf16)
    up_theirs = dot(h2_all[:, half:], up_all, TN).astype(bf16)
    gate_theirs = other_half(gate_theirs)
    up_theirs = other_half(up_theirs)
    gate_mine = dot(h2_all[:, :half], gate_all, TN).astype(bf16)
    up_mine = dot(h2_all[:, :half], up_all, TN).astype(bf16)
    gate_parts = scatter_step(blocks_of(gate_mine, gate_theirs, 0), 1)
    up_parts = scatter_step(blocks_of(up_mine, up_theirs, 0), 1)
    dh2 = add_rows(norm2_parts[0], dh2_received)
    cot_share = slot_of(cot_all, 0).astype(f32)
    e2 = dh2 * gain_two
    dx1 = cot_share + inv2 * (
        e2
        - jnp.mean(e2, axis=-1, keepdims=True)
        - unit2 * jnp.mean(e2 * unit2, axis=-1, keepdims=True)
    )
    dx1_slots = gather_rows(dx1.astype(bf16))

    down_theirs = dot(hidden_all, cot_all[:, half:], TN).astype(bf16)
    down_mine = dot(hidden_all, cot_all[:, :half], TN).astype(bf16)
    out_all = dot(hidden_all, down_full).astype(bf16)
    down_theirs = other_half(down_theirs)
    dx1b = jnp.concatenate(dx1_slots, axis=0)
    d_attn = dot(dx1b, o_full, NT).astype(bf16)
    d_send = [
        lax.dynamic_slice_in_dim(d_attn, ((ctx & (groups - 1)) ^ s) * PAIR, PAIR, 1)
        for s in range(groups)
    ]
    d_send, dx1b, out_all = hold(d_send, dx1b, out_all)
    d_pieces = [d_send[0]] + [
        swap_with(d_send[s % groups], CONTEXT, s) for s in range(1, ctxs)
    ]

    o_theirs = dot(attn, dx1b[:, half:], TN).astype(bf16)
    o_mine = dot(attn, dx1b[:, :half], TN).astype(bf16)
    o_theirs = other_half(o_theirs)

    out_received = send_rows([slot_of(out_all, i) for i in range(slots)])
    gate_out = scatter_rest(gate_parts)
    up_out = scatter_rest(up_parts)
    down_parts = scatter_step(blocks_of(down_mine, down_theirs, 1), 1)
    back = attend_back(
        ids, pieces, d_pieces, o_t, lse, full_tables, groups, slots, docs, pics, bq, bk
    )
    back_rest = [swap_with(back[s], CONTEXT, s) for s in range(1, groups)]

    output = by_shard(
        (x1 + add_rows(slot_of(out_all, 0).astype(f32), out_received)).astype(bf16)
    )[None]
    o_parts = scatter_step(blocks_of(o_mine, o_theirs, 1), 1)
    down_grad = scatter_rest(down_parts)
    o_grad = scatter_rest(o_parts)

    d_qkv, norm1_parts = join(ids, [back[0]] + back_rest, own_qkv, oth_qkv, slots, NT)
    norm1_parts, d_qkv = hold(norm1_parts, d_qkv)
    dh1_received = send_rows(norm1_parts)
    qkv_theirs = []
    qkv_mine = []
    qkv_parts = []
    qkv_grad = []
    for j in range(3):
        qkv_theirs.append(other_half(dot(h1[:, half:], d_qkv[j], TN).astype(bf16)))
        qkv_mine.append(dot(h1[:, :half], d_qkv[j], TN).astype(bf16))
        qkv_parts.append(scatter_step(blocks_of(qkv_mine[j], qkv_theirs[j], 0), 1))
        qkv_grad.append(scatter_rest(qkv_parts[j]))
    dh1 = add_rows(norm1_parts[0], dh1_received)

    mean1 = jnp.mean(x_share, axis=-1, keepdims=True)
    cent1 = x_share - mean1
    inv1 = lax.rsqrt(jnp.mean(cent1 * cent1, axis=-1, keepdims=True) + EPS)
    unit1 = cent1 * inv1
    e1 = dh1 * gain_one
    tokens_grad = dx1 + inv1 * (
        e1
        - jnp.mean(e1, axis=-1, keepdims=True)
        - unit1 * jnp.mean(e1 * unit1, axis=-1, keepdims=True)
    )
    tokens_grad = by_shard(tokens_grad)[None]

    norms = jnp.stack(
        [
            jnp.sum(dh1 * unit1, axis=0),
            jnp.sum(dh1, axis=0),
            jnp.sum(dh2 * unit2, axis=0),
            jnp.sum(dh2, axis=0),
        ]
    )
    norms = sum_over(by_shard(norms), TENSOR)
    bias = jnp.concatenate(
        [jnp.sum(d.astype(f32), axis=0, keepdims=True) for d in d_qkv], axis=1
    )
    sums = sum_over(jnp.concatenate([norms.reshape(1, 4 * width), bias], axis=1), SHARD)
    sums = sum_over(sums, CONTEXT)
    norms = sums[0, : 4 * width].reshape(4, width)
    bias = sums[0, 4 * width :]
    k_bias_grad = bias[inner : 2 * inner].reshape(heads_here, HEAD_DIM)[:, :ROT]
    return (
        output,
        tokens_grad,
        norms[0],
        norms[1],
        *qkv_grad,
        bias[:inner],
        k_bias_grad.reshape(heads_here * ROT),
        bias[2 * inner :],
        o_grad,
        norms[2],
        norms[3],
        gate_out,
        up_out,
        down_grad,
    )


def solution(mesh):
    tokens = P(SHARD, CONTEXT, None)
    inward = P(SHARD, TENSOR)
    outward = P(TENSOR, SHARD)
    vector = P(TENSOR)
    placed = (
        tokens,
        P(),
        P(),
        inward,
        inward,
        inward,
        vector,
        vector,
        vector,
        outward,
        P(),
        P(),
        inward,
        inward,
        outward,
        tokens,
        P(SHARD, None),
        P(SHARD, None),
    )
    share = P(SHARD, (CONTEXT, TENSOR), None)
    grad_in = P((SHARD, CONTEXT), TENSOR)
    grad_out = P(TENSOR, (SHARD, CONTEXT))

    return jax.shard_map(
        local,
        mesh=mesh,
        in_specs=placed,
        out_specs=(
            share,
            share,
            P(),
            P(),
            grad_in,
            grad_in,
            grad_in,
            vector,
            vector,
            vector,
            grad_out,
            P(),
            P(),
            grad_in,
            grad_in,
            grad_out,
        ),
        check_vma=False,
    )
```

```python
import functools

import jax
import jax.numpy as jnp
from jax import lax
from jax.experimental import pallas as pl
from jax.experimental.pallas import tpu as pltpu
from jax.sharding import PartitionSpec as P

HEAD_DIM = 64
ROT = 16
SPAN = 256
PAIR = 128
EPS = 1e-05
LOW = -1e30
LOWER = -2e30
SCALE = HEAD_DIM ** (-0.5)

SHARD = "shard"
CONTEXT = "context"
TENSOR = "tensor"

f32 = jnp.float32
bf16 = jnp.bfloat16


NT = (((1,), (1,)), ((), ()))
NN = (((1,), (0,)), ((), ()))
TN = (((0,), (0,)), ((), ()))


def dot(a, b, dims=NN):
    return lax.dot_general(a, b, dims, preferred_element_type=f32)


def swap_with(x, axis, bit):
    size = lax.axis_size(axis)
    return lax.ppermute(x, axis, [(i, i ^ bit) for i in range(size)])


def sum_over(x, axis):
    terms = [x] + [swap_with(x, axis, i) for i in range(1, lax.axis_size(axis))]
    while len(terms) > 1:
        terms = [terms[i] + terms[i + 1] for i in range(0, len(terms), 2)]
    return terms[0]


def rotary_tables(positions):
    half = ROT // 2
    freq = 10000.0 ** (-(2.0 * jnp.arange(half).astype(f32)) / ROT)
    angles = freq[:, None] * positions.astype(f32)[None, :]
    parts = jnp.concatenate([jnp.cos(angles), jnp.sin(angles)], axis=0)
    lane = jnp.arange(PAIR) % HEAD_DIM
    row = jnp.arange(half)[:, None]
    hit = (lane[None, :] % half == row) & (lane[None, :] < ROT)
    spread_cos = jnp.concatenate([hit, jnp.zeros_like(hit)], axis=0).astype(f32)
    sign = jnp.where(lane < half, -1.0, 1.0)[None, :]
    spread_sin = jnp.concatenate([jnp.zeros_like(hit), hit], axis=0).astype(f32) * sign
    expand = functools.partial(
        lax.dot_general,
        dimension_numbers=TN,
        precision=lax.Precision.HIGHEST,
        preferred_element_type=f32,
    )
    rest = jnp.where(lane < ROT, 0.0, 1.0).astype(f32)
    return expand(parts, spread_cos) + rest[None, :], expand(parts, spread_sin)


def swap_halves(x):
    lane = lax.broadcasted_iota(jnp.int32, x.shape, 1) % HEAD_DIM
    return jnp.where(lane < ROT // 2, pltpu.roll(x, PAIR - ROT // 2, 1), pltpu.roll(x, ROT // 2, 1))


def project_kernel(
    groups,
    ids,
    x_own,
    x_oth,
    gain_own,
    gain_oth,
    shift_own,
    shift_oth,
    wq_own,
    wk_own,
    wv_own,
    wq_oth,
    wk_oth,
    wv_oth,
    q_bias,
    k_bias,
    v_bias,
    cos_ref,
    sin_ref,
    *rest,
):
    h_ref, pieces, (qs, ks, vs) = rest[0], rest[1 : 1 + groups], rest[1 + groups :]
    half = x_own.shape[1]
    a = x_own[...].astype(f32)
    b = x_oth[...].astype(f32)
    count = 1.0 / (2 * half)
    mean = (jnp.sum(a, axis=1, keepdims=True) + jnp.sum(b, axis=1, keepdims=True)) * count
    a = a - mean
    b = b - mean
    var = (jnp.sum(a * a, axis=1, keepdims=True) + jnp.sum(b * b, axis=1, keepdims=True)) * count
    inv = lax.rsqrt(var + EPS)
    ha = (a * inv * gain_own[...].astype(f32) + shift_own[...].astype(f32)).astype(bf16)
    hb = (b * inv * gain_oth[...].astype(f32) + shift_oth[...].astype(f32)).astype(bf16)
    h_ref[:, :half] = ha
    h_ref[:, half:] = hb
    qs[...] = dot(ha, wq_own[...]) + dot(hb, wq_oth[...]) + q_bias[...]
    ks[...] = dot(ha, wk_own[...]) + dot(hb, wk_oth[...]) + k_bias[...]
    vs[...] = dot(ha, wv_own[...]) + dot(hb, wv_oth[...]) + v_bias[...]
    cos = cos_ref[...]
    sin = sin_ref[...]
    for s in range(groups):
        group = (ids[1] & (groups - 1)) ^ s
        cols = pl.ds(pl.multiple_of(group * PAIR, PAIR), PAIR)
        q = qs[:, cols]
        k = ks[:, cols]
        pieces[s][:, :PAIR] = (q * cos + swap_halves(q) * sin).astype(bf16)
        pieces[s][:, PAIR : 2 * PAIR] = (k * cos + swap_halves(k) * sin).astype(bf16)
        pieces[s][:, 2 * PAIR :] = vs[:, cols].astype(bf16)


def project(ids, tokens, vectors, own, other, tables, groups, slots):
    rows, width = tokens.shape
    half = width // 2
    share = rows // slots
    inner = own[0].shape[1]

    def row_block(i, ids):
        return ids[2] ^ i

    whole = lambda i, ids: (0, 0)
    weight = pl.BlockSpec((half, inner), whole)
    first_bias = 2 * width // inner
    in_specs = [
        pl.BlockSpec((share, half), lambda i, ids: (row_block(i, ids), ids[0])),
        pl.BlockSpec((share, half), lambda i, ids: (row_block(i, ids), 1 - ids[0])),
        pl.BlockSpec((1, half), lambda i, ids: (0, ids[0])),
        pl.BlockSpec((1, half), lambda i, ids: (0, 1 - ids[0])),
        pl.BlockSpec((1, half), lambda i, ids: (0, 2 + ids[0])),
        pl.BlockSpec((1, half), lambda i, ids: (0, 3 - ids[0])),
    ]
    in_specs += [weight] * 6
    in_specs += [
        pl.BlockSpec((1, inner), lambda i, ids, j=j: (0, first_bias + j)) for j in range(3)
    ]
    in_specs += [pl.BlockSpec((share, PAIR), lambda i, ids: (row_block(i, ids), 0))] * 2
    out = pl.pallas_call(
        functools.partial(project_kernel, groups),
        grid_spec=pltpu.PrefetchScalarGridSpec(
            num_scalar_prefetch=1,
            grid=(slots,),
            in_specs=in_specs,
            out_specs=[pl.BlockSpec((share, width), lambda i, ids: (i, 0))]
            + [pl.BlockSpec((share, 3 * PAIR), lambda i, ids: (i, 0))] * groups,
            scratch_shapes=[pltpu.VMEM((share, inner), f32)] * 3,
        ),
        out_shape=[jax.ShapeDtypeStruct((rows, width), bf16)]
        + [jax.ShapeDtypeStruct((rows, 3 * PAIR), bf16)] * groups,
        compiler_params=pltpu.CompilerParams(vmem_limit_bytes=56 << 20),
        cost_estimate=pl.CostEstimate(
            flops=2 * rows * width * inner * 3,
            bytes_accessed=rows * width * 4 + 3 * width * inner * 2 + rows * inner * 6,
            transcendentals=rows,
        ),
        name="project",
    )(ids, tokens, tokens, *[vectors] * 4, *own, *other, *[vectors] * 3, *tables)
    return out[0], out[1:]


def reach(ids, p, docs, pics, length):
    start = jnp.zeros_like(p)
    end = jnp.full_like(p, length)
    for j in range(docs):
        e = ids[4 + j]
        start = jnp.where(p >= e, jnp.maximum(start, e), start)
        end = jnp.where(p < e, jnp.minimum(end, e), end)
    far = p + 1
    for j in range(pics):
        b = ids[4 + docs + j]
        inside = (p >= b) & (p < b + SPAN)
        far = jnp.where(inside, jnp.maximum(far, jnp.minimum(b + SPAN, end)), far)
    return start, far


def block_ranges(ids, first, bq, bk, docs, pics, length):
    lo_a, hi_a = reach(ids, first, docs, pics, length)
    lo_b, hi_b = reach(ids, first + (bq - 1), docs, pics, length)
    begin = lo_a // bk
    stop = (hi_b + (bk - 1)) // bk
    full_begin = jnp.clip((lo_b + (bk - 1)) // bk, begin, stop)
    full_stop = jnp.clip(hi_a // bk, full_begin, stop)
    return begin, full_begin, full_stop, stop


def piece_copies(ids, pieces, whole, sems, slots, share, outward=False):
    copies = []
    for s, piece in enumerate(pieces):
        for i in range(slots):
            first = ((ids[1] ^ s) * slots + (ids[2] ^ i)) * share
            there = whole.at[pl.ds(pl.multiple_of(first, share), share)]
            here = piece.at[pl.ds(i * share, share)]
            src, dst = (there, here) if outward else (here, there)
            copies.append(pltpu.make_async_copy(src, dst, sems.at[s * slots + i]))
    return copies


def attend_kernel(dims, ids, *refs):
    pieces, groups, slots, share, length, docs, pics, bq, bk = dims
    ins = refs[:pieces]
    outs = refs[pieces : pieces + groups]
    o_t, lse = refs[pieces + groups : pieces + groups + 2]
    qkv, vx, ob, acc, m_ref, sem_in, sem_out = refs[pieces + groups + 2 :]
    loads = piece_copies(ids, ins, qkv, sem_in, slots, share)
    for c in loads:
        c.start()
    for c in loads:
        c.wait()

    def prepare(j, _):
        rows = pl.ds(pl.multiple_of(j * bk, bk), bk)
        v_t = qkv[rows, 2 * PAIR :].astype(f32).T
        ones = jnp.ones((16, bk), bf16)
        for h in range(2):
            vx[h, :HEAD_DIM, rows] = v_t[h * HEAD_DIM : (h + 1) * HEAD_DIM].astype(bf16)
            vx[h, HEAD_DIM:, rows] = ones
        return 0

    lax.fori_loop(0, length // bk, prepare, 0)
    lane = lax.broadcasted_iota(jnp.int32, (bq, PAIR), 1)

    def query_block(i, _):
        first = i * bq
        rows = pl.ds(pl.multiple_of(first, bq), bq)
        q = qkv[rows, :PAIR].astype(f32) * SCALE
        heads = [
            jnp.where((lane < HEAD_DIM) == (h == 0), q, 0.0).astype(bf16) for h in range(2)
        ]
        for h in range(2):
            acc[h] = jnp.zeros_like(acc[h])
            m_ref[h] = jnp.full_like(m_ref[h], LOW)
        lo, hi = reach(
            ids, first + lax.broadcasted_iota(jnp.int32, (1, bq), 1), docs, pics, length
        )
        begin, full_begin, full_stop, stop = block_ranges(
            ids, first, bq, bk, docs, pics, length
        )

        def visit(masked, j, _):
            keys = pl.ds(pl.multiple_of(j * bk, bk), bk)
            k = qkv[keys, PAIR : 2 * PAIR]
            if masked:
                p = j * bk + lax.broadcasted_iota(jnp.int32, (bk, bq), 0)
                ok = (p >= lo) & (p < hi)
            scores = [dot(k, heads[h], NT) for h in range(2)]
            if masked:
                scores = [jnp.where(ok, s, LOWER) for s in scores]
            old = [m_ref[h, 0:1] for h in range(2)]
            tops = [jnp.max(s, axis=0, keepdims=True) for s in scores]
            new = [jnp.maximum(a, b) for a, b in zip(old, tops)]
            fade = [jnp.exp(a - b) for a, b in zip(old, new)]
            ws = [jnp.exp(s - n).astype(bf16) for s, n in zip(scores, new)]
            sums = [dot(vx[h, :, keys], ws[h]) for h in range(2)]
            for h in range(2):
                acc[h] = acc[h] * fade[h] + sums[h]
                m_ref[h, 0:1] = new[h]
            return 0

        lax.fori_loop(begin, full_begin, functools.partial(visit, True), 0)
        lax.fori_loop(full_begin, full_stop, functools.partial(visit, False), 0)
        lax.fori_loop(full_stop, stop, functools.partial(visit, True), 0)
        for h in range(2):
            total = acc[h, HEAD_DIM : HEAD_DIM + 1]
            o_t[h * HEAD_DIM : (h + 1) * HEAD_DIM, rows] = acc[h, :HEAD_DIM] / total
            lse[h : h + 1, rows] = m_ref[h, 0:1] + jnp.log(total)
        ob[rows] = o_t[:, rows].T.astype(bf16)
        return 0

    lax.fori_loop(0, length // bq, query_block, 0)
    stores = piece_copies(ids, outs, ob, sem_out, slots, share, outward=True)
    for c in stores:
        c.start()
    for c in stores:
        c.wait()


def attend_cost(length, matmuls):
    pairs = length * length // 2
    return pl.CostEstimate(
        flops=2 * pairs * 256 * 2 * matmuls,
        bytes_accessed=length * PAIR * 2 * 8,
        transcendentals=2 * pairs,
    )


def attend(ids, pieces, groups, slots, docs, pics, bq, bk):
    rows = pieces[0].shape[0]
    n = len(pieces)
    length = rows * n
    share = rows // slots
    dims = (n, groups, slots, share, length, docs, pics, bq, bk)
    anywhere = pl.BlockSpec(memory_space=pl.ANY)
    out = pl.pallas_call(
        functools.partial(attend_kernel, dims),
        grid_spec=pltpu.PrefetchScalarGridSpec(
            num_scalar_prefetch=1,
            grid=(1,),
            in_specs=[anywhere] * n,
            out_specs=[anywhere] * groups
            + [
                pl.BlockSpec((PAIR, length), lambda i, ids: (0, 0)),
                pl.BlockSpec((8, length), lambda i, ids: (0, 0)),
            ],
            scratch_shapes=[
                pltpu.VMEM((length, 3 * PAIR), bf16),
                pltpu.VMEM((2, HEAD_DIM + 16, length), bf16),
                pltpu.VMEM((length, PAIR), bf16),
                pltpu.VMEM((2, HEAD_DIM + 16, bq), f32),
                pltpu.VMEM((2, 8, bq), f32),
                pltpu.SemaphoreType.DMA((n * slots,)),
                pltpu.SemaphoreType.DMA((groups * slots,)),
            ],
        ),
        out_shape=[jax.ShapeDtypeStruct((rows, PAIR), bf16)] * groups
        + [
            jax.ShapeDtypeStruct((PAIR, length), f32),
            jax.ShapeDtypeStruct((8, length), f32),
        ],
        compiler_params=pltpu.CompilerParams(vmem_limit_bytes=56 << 20),
        cost_estimate=attend_cost(length, 2),
        name="attend",
    )(ids, *pieces)
    return out[:groups], out[groups], out[groups + 1]


def attend_back_kernel(dims, ids, *refs):
    pieces, groups, slots, share, length, docs, pics, bq, bk = dims
    ins = refs[:pieces]
    grads = refs[pieces : 2 * pieces]
    o_t, lse, cos_ref, sin_ref = refs[2 * pieces : 2 * pieces + 4]
    outs = refs[2 * pieces + 4 : 2 * pieces + 4 + groups]
    qkv, dob, kt, dq_t, dk, dv, sem_in, sem_grad, sem_out = refs[2 * pieces + 4 + groups :]
    loads = piece_copies(ids, ins, qkv, sem_in, slots, share)
    loads += piece_copies(ids, grads, dob, sem_grad, slots, share)
    for c in loads:
        c.start()
    for c in loads:
        c.wait()

    def prepare(j, _):
        rows = pl.ds(pl.multiple_of(j * bk, bk), bk)
        kt[:, rows] = qkv[rows, PAIR : 2 * PAIR].astype(f32).T.astype(bf16)
        dk[rows] = jnp.zeros((bk, PAIR), f32)
        dv[rows] = jnp.zeros((bk, PAIR), f32)
        return 0

    lax.fori_loop(0, length // bk, prepare, 0)
    lane = lax.broadcasted_iota(jnp.int32, (bq, PAIR), 1)

    def turn_back(x, rows):
        return x * cos_ref[rows] - swap_halves(x) * sin_ref[rows]

    def query_block(i, _):
        first = i * bq
        rows = pl.ds(pl.multiple_of(first, bq), bq)
        q = qkv[rows, :PAIR].astype(f32) * SCALE
        do = dob[rows].astype(f32)
        q_of = []
        do_of = []
        for h in range(2):
            mine = (lane < HEAD_DIM) == (h == 0)
            q_of.append(jnp.where(mine, q, 0.0).astype(bf16))
            do_of.append(jnp.where(mine, do, 0.0).astype(bf16))
        prod = do.T * o_t[:, rows]
        delta = [
            jnp.sum(prod[h * HEAD_DIM : (h + 1) * HEAD_DIM], axis=0, keepdims=True)
            for h in range(2)
        ]
        dq_t[...] = jnp.zeros_like(dq_t)
        lo, hi = reach(
            ids, first + lax.broadcasted_iota(jnp.int32, (1, bq), 1), docs, pics, length
        )
        begin, full_begin, full_stop, stop = block_ranges(
            ids, first, bq, bk, docs, pics, length
        )

        def visit(masked, j, _):
            keys = pl.ds(pl.multiple_of(j * bk, bk), bk)
            k = qkv[keys, PAIR : 2 * PAIR]
            v = qkv[keys, 2 * PAIR :]
            if masked:
                p = j * bk + lax.broadcasted_iota(jnp.int32, (bk, bq), 0)
                ok = (p >= lo) & (p < hi)
            dk_sum = dk[keys]
            dv_sum = dv[keys]
            for h in range(2):
                feats = slice(h * HEAD_DIM, (h + 1) * HEAD_DIM)
                s = dot(k, q_of[h], NT)
                if masked:
                    s = jnp.where(ok, s, LOWER)
                w = jnp.exp(s - lse[h : h + 1, rows])
                dw = dot(v, do_of[h], NT)
                ds = (w * (dw - delta[h])).astype(bf16)
                dv_sum = dv_sum + dot(w.astype(bf16), do_of[h])
                dk_sum = dk_sum + dot(ds, q_of[h])
                dq_t[feats] += dot(kt[feats, keys], ds)
            dk[keys] = dk_sum
            dv[keys] = dv_sum
            return 0

        lax.fori_loop(begin, full_begin, functools.partial(visit, True), 0)
        lax.fori_loop(full_begin, full_stop, functools.partial(visit, False), 0)
        lax.fori_loop(full_stop, stop, functools.partial(visit, True), 0)
        dq = dq_t[...].T * SCALE
        qkv[rows, :PAIR] = turn_back(dq, rows).astype(bf16)
        return 0

    lax.fori_loop(0, length // bq, query_block, 0)

    def finish(j, _):
        rows = pl.ds(pl.multiple_of(j * bk, bk), bk)
        qkv[rows, PAIR : 2 * PAIR] = turn_back(dk[rows], rows).astype(bf16)
        qkv[rows, 2 * PAIR :] = dv[rows].astype(bf16)
        return 0

    lax.fori_loop(0, length // bk, finish, 0)
    stores = piece_copies(ids, outs, qkv, sem_out, slots, share, outward=True)
    for c in stores:
        c.start()
    for c in stores:
        c.wait()


def attend_back(ids, pieces, grads, o_t, lse, tables, groups, slots, docs, pics, bq, bk):
    rows = pieces[0].shape[0]
    n = len(pieces)
    length = rows * n
    share = rows // slots
    dims = (n, groups, slots, share, length, docs, pics, bq, bk)
    anywhere = pl.BlockSpec(memory_space=pl.ANY)
    once = dict(pipeline_mode=pl.Buffered(1))
    return pl.pallas_call(
        functools.partial(attend_back_kernel, dims),
        grid_spec=pltpu.PrefetchScalarGridSpec(
            num_scalar_prefetch=1,
            grid=(1,),
            in_specs=[anywhere] * (2 * n)
            + [
                pl.BlockSpec((PAIR, length), lambda i, ids: (0, 0), **once),
                pl.BlockSpec((8, length), lambda i, ids: (0, 0), **once),
                pl.BlockSpec((length, PAIR), lambda i, ids: (0, 0), **once),
                pl.BlockSpec((length, PAIR), lambda i, ids: (0, 0), **once),
            ],
            out_specs=[anywhere] * groups,
            scratch_shapes=[
                pltpu.VMEM((length, 3 * PAIR), bf16),
                pltpu.VMEM((length, PAIR), bf16),
                pltpu.VMEM((PAIR, length), bf16),
                pltpu.VMEM((PAIR, bq), f32),
                pltpu.VMEM((length, PAIR), f32),
                pltpu.VMEM((length, PAIR), f32),
                pltpu.SemaphoreType.DMA((n * slots,)),
                pltpu.SemaphoreType.DMA((n * slots,)),
                pltpu.SemaphoreType.DMA((groups * slots,)),
            ],
        ),
        out_shape=[jax.ShapeDtypeStruct((rows, 3 * PAIR), bf16)] * groups,
        compiler_params=pltpu.CompilerParams(vmem_limit_bytes=56 << 20),
        cost_estimate=attend_cost(length, 5),
        name="attend_back",
    )(ids, *pieces, *grads, o_t, lse, *tables)


def join_kernel(groups, kinds, slots, dims, ids, *refs):
    pieces = refs[:groups]
    own = refs[groups : groups + kinds]
    oth = refs[groups + kinds : groups + 2 * kinds]
    joined = refs[groups + 2 * kinds : groups + 3 * kinds]
    parts = refs[groups + 3 * kinds :]
    half = parts[0].shape[1] // 2
    for s in range(groups):
        group = (ids[1] & (groups - 1)) ^ s
        for j in range(kinds):
            cols = pl.ds(pl.multiple_of(group * PAIR, PAIR), PAIR)
            joined[j][:, cols] = pieces[s][:, j * PAIR : (j + 1) * PAIR]
    for side, weights in enumerate((own, oth)):
        total = None
        for j, w in enumerate(weights):
            term = dot(joined[j][...], w[...], dims)
            total = term if total is None else total + term
        for i in range(slots):

            @pl.when(pl.program_id(0) == i)
            def _():
                parts[i][:, side * half : (side + 1) * half] = total.astype(parts[i].dtype)


def join(ids, pieces, own, oth, slots, dims):
    groups = len(pieces)
    kinds = len(own)
    rows = pieces[0].shape[0]
    share = rows // slots
    inner = groups * PAIR
    width = 2 * (own[0].shape[0] if dims == NT else own[0].shape[1])
    whole = lambda i, ids: (0, 0)
    by_row = lambda i, ids: (i, 0)
    out = pl.pallas_call(
        functools.partial(join_kernel, groups, kinds, slots, dims),
        grid_spec=pltpu.PrefetchScalarGridSpec(
            num_scalar_prefetch=1,
            grid=(slots,),
            in_specs=[pl.BlockSpec((share, kinds * PAIR), by_row)] * groups
            + [pl.BlockSpec(own[0].shape, whole)] * (2 * kinds),
            out_specs=[pl.BlockSpec((share, inner), by_row)] * kinds
            + [pl.BlockSpec((share, width), whole)] * slots,
        ),
        out_shape=[jax.ShapeDtypeStruct((rows, inner), bf16)] * kinds
        + [jax.ShapeDtypeStruct((share, width), f32 if i == 0 else bf16) for i in range(slots)],
        compiler_params=pltpu.CompilerParams(vmem_limit_bytes=44 << 20),
        cost_estimate=pl.CostEstimate(
            flops=2 * rows * width * inner * kinds,
            bytes_accessed=rows * width * 3 + kinds * (width * inner * 2 + rows * inner * 4),
            transcendentals=0,
        ),
    )(ids, *pieces, *own, *oth)
    return out[:kinds], out[kinds:]


def hold(*groups):
    return lax.optimization_barrier(groups)


def local(
    tokens,
    ln1_gain,
    ln1_shift,
    q_weight,
    k_weight,
    v_weight,
    q_bias,
    k_bias,
    v_bias,
    o_weight,
    ln2_gain,
    ln2_shift,
    gate_weight,
    up_weight,
    down_weight,
    cotangent,
    doc_lengths,
    picture_starts,
):
    me = lax.axis_index(SHARD)
    ctx = lax.axis_index(CONTEXT)
    ctxs = lax.axis_size(CONTEXT)
    ten = lax.axis_index(TENSOR)
    slots = lax.axis_size(TENSOR)
    rows, width = tokens.shape[1:]
    half = width // 2
    share = rows // slots
    inner = q_weight.shape[1]
    groups = inner // PAIR
    heads_here = inner // HEAD_DIM
    docs = doc_lengths.shape[1]
    pics = picture_starts.shape[1]
    length = ctxs * rows
    quarter = half // ctxs
    bq = min(512, rows)
    bk = min(512, rows)
    assert ctxs % groups == 0 and ctxs & (ctxs - 1) == 0 and slots & (slots - 1) == 0

    def by_shard(x):
        turned = jnp.concatenate([x[..., half:], x[..., :half]], axis=-1)
        return jnp.where(me == 0, x, turned)

    def slot_rows(x, i):
        return lax.dynamic_slice_in_dim(x, (ten ^ i) * share, share, 0)

    def other_half(x):
        return swap_with(x, SHARD, 1)

    own_qkv = (q_weight, k_weight, v_weight)
    oth_qkv = tuple(other_half(w) for w in own_qkv)
    doc_ends = jnp.cumsum(doc_lengths[0])
    ids = jnp.concatenate(
        [
            jnp.stack([me, ctx, ten, ctx * 0]).astype(jnp.int32),
            doc_ends.astype(jnp.int32),
            picture_starts[0].astype(jnp.int32),
        ]
    )
    local_tables = rotary_tables(ctx * rows + jnp.arange(rows, dtype=jnp.int32))
    k_bias_wide = jnp.pad(
        k_bias.reshape(heads_here, ROT), ((0, 0), (0, HEAD_DIM - ROT))
    ).reshape(inner)
    assert 2 * width % inner == 0
    vectors = jnp.concatenate(
        [ln1_gain, ln1_shift, q_bias, k_bias_wide, v_bias], axis=0
    ).astype(f32)[None]
    h1, send = project(ids, tokens[0], vectors, own_qkv, oth_qkv, local_tables, groups, slots)

    (send, later) = hold(
        send,
        (
            o_weight,
            gate_weight,
            up_weight,
            down_weight,
            cotangent[0],
            tokens[0],
            jnp.arange(length, dtype=jnp.int32),
        ),
    )
    o_weight, gate_weight, up_weight, down_weight, cot_rows, x_rows, positions = later
    pieces = [send[0]] + [swap_with(send[s % groups], CONTEXT, s) for s in range(1, ctxs)]
    down_oth, o_oth, gate_oth, up_oth = map(
        other_half, (down_weight, o_weight, gate_weight, up_weight)
    )
    full_tables = rotary_tables(positions)
    cot_all = by_shard(jnp.concatenate([slot_rows(cot_rows, i) for i in range(slots)], axis=0))
    x_share = by_shard(slot_rows(x_rows, 0)).astype(f32)
    down_full = jnp.concatenate([down_weight, down_oth], axis=1)
    o_full = jnp.concatenate([o_weight, o_oth], axis=1)
    dm_all = dot(cot_all, down_full, NT)
    gate_full = jnp.concatenate([gate_weight, gate_oth], axis=0)
    up_full = jnp.concatenate([up_weight, up_oth], axis=0)
    gain_two = by_shard(ln2_gain.astype(f32))
    shift_two = by_shard(ln2_shift.astype(f32))
    gain_one = by_shard(ln1_gain.astype(f32))
    pieces, ready = hold(
        pieces, (down_full, o_full, gate_full, up_full, cot_all, dm_all, full_tables, x_share)
    )
    down_full, o_full, gate_full, up_full, cot_all, dm_all, full_tables, x_share = ready

    attn_send, o_t, lse = attend(ids, pieces, groups, slots, docs, pics, bq, bk)
    (attn,), attn_parts = join(
        ids,
        [attn_send[0]] + [swap_with(attn_send[s], CONTEXT, s) for s in range(1, groups)],
        (o_weight,),
        (o_oth,),
        slots,
        NN,
    )

    mid = share // 2

    def send_rows(parts):
        return [swap_with(parts[i].astype(bf16), TENSOR, i) for i in range(1, slots)]

    def relay_sums(parts):
        if slots != 4:
            return send_rows(parts)
        one, two, far = (parts[i].astype(bf16) for i in range(1, 4))
        far_two = swap_with(far[:mid], TENSOR, 1)
        far_one = swap_with(far[mid:], TENSOR, 2)
        first = swap_with(one[:mid], TENSOR, 1)
        last = swap_with(two[mid:], TENSOR, 2)
        two = (two[:mid].astype(f32) + far_two.astype(f32)).astype(bf16)
        one = (one[mid:].astype(f32) + far_one.astype(f32)).astype(bf16)
        two = swap_with(two, TENSOR, 2)
        one = swap_with(one, TENSOR, 1)
        return [
            jnp.concatenate([first, one], axis=0),
            jnp.concatenate([two, last], axis=0),
        ]

    def add_rows(own, received):
        for part in received:
            own = own + part.astype(f32)
        return own

    def gather_rows(block):
        if slots != 4:
            return [block] + [swap_with(block, TENSOR, i) for i in range(1, slots)]
        one_last = swap_with(block[mid:], TENSOR, 1)
        two_first = swap_with(block[:mid], TENSOR, 2)
        one_first = swap_with(block[:mid], TENSOR, 1)
        two_last = swap_with(block[mid:], TENSOR, 2)
        far_first = swap_with(two_first, TENSOR, 1)
        far_last = swap_with(one_last, TENSOR, 2)
        return [
            block,
            jnp.concatenate([one_first, one_last], axis=0),
            jnp.concatenate([two_first, two_last], axis=0),
            jnp.concatenate([far_first, far_last], axis=0),
        ]

    def slot_of(x, i):
        return x[i * share : (i + 1) * share]

    x1 = x_share + add_rows(attn_parts[0], relay_sums(attn_parts))
    mean2 = jnp.mean(x1, axis=-1, keepdims=True)
    cent2 = x1 - mean2
    inv2 = lax.rsqrt(jnp.mean(cent2 * cent2, axis=-1, keepdims=True) + EPS)
    unit2 = cent2 * inv2
    h2 = gather_rows((unit2 * gain_two + shift_two).astype(bf16))

    hidden = []
    gate_grad = []
    up_grad = []
    norm2_parts = []
    dh2_received = []
    for i in range(slots):
        dm = slot_of(dm_all, i)
        g = dot(h2[i], gate_full)
        u = dot(h2[i], up_full)
        sig = jax.nn.sigmoid(g)
        act = g * sig
        hidden.append((act * u).astype(bf16))
        gate_grad.append((dm * u * sig * (1.0 + g * (1.0 - sig))).astype(bf16))
        up_grad.append((dm * act).astype(bf16))
        part = dot(gate_grad[i], gate_full, NT) + dot(up_grad[i], up_full, NT)
        norm2_parts.append(part if i == 0 else part.astype(bf16))
        if i + 1 < slots:
            norm2_parts[i], h2[i + 1] = hold(norm2_parts[i], h2[i + 1])
        if i > 0:
            dh2_received.append(swap_with(norm2_parts[i], TENSOR, i))

    def blocks_of(mine, theirs, axis):
        def block(x, d):
            return lax.dynamic_slice_in_dim(x, (ctx ^ d) * quarter, quarter, axis).astype(f32)

        return {d: block(mine, d) + block(theirs, d) for d in range(ctxs)}

    def scatter_step(parts, bit):
        parts = dict(parts)
        for d in sorted((d for d in parts if d & bit), reverse=True):
            parts[d ^ bit] += swap_with(parts.pop(d).astype(bf16), CONTEXT, bit).astype(f32)
        return parts

    def scatter_rest(parts):
        bit = 2
        while bit < ctxs:
            parts = scatter_step(parts, bit)
            bit *= 2
        return parts[0]

    h2_all, gate_all, up_all, hidden_all = (
        jnp.concatenate(blocks, axis=0) for blocks in (h2, gate_grad, up_grad, hidden)
    )

    gate_theirs = dot(h2_all[:, half:], gate_all, TN).astype(bf16)
    up_theirs = dot(h2_all[:, half:], up_all, TN).astype(bf16)
    gate_theirs = other_half(gate_theirs)
    up_theirs = other_half(up_theirs)
    gate_mine = dot(h2_all[:, :half], gate_all, TN).astype(bf16)
    up_mine = dot(h2_all[:, :half], up_all, TN).astype(bf16)
    gate_parts = scatter_step(blocks_of(gate_mine, gate_theirs, 0), 1)
    up_parts = scatter_step(blocks_of(up_mine, up_theirs, 0), 1)
    dh2 = add_rows(norm2_parts[0], dh2_received)
    cot_share = slot_of(cot_all, 0).astype(f32)
    e2 = dh2 * gain_two
    dx1 = cot_share + inv2 * (
        e2
        - jnp.mean(e2, axis=-1, keepdims=True)
        - unit2 * jnp.mean(e2 * unit2, axis=-1, keepdims=True)
    )
    dx1_slots = gather_rows(dx1.astype(bf16))

    down_theirs = dot(hidden_all, cot_all[:, half:], TN).astype(bf16)
    down_mine = dot(hidden_all, cot_all[:, :half], TN).astype(bf16)
    out_all = dot(hidden_all, down_full).astype(bf16)
    down_theirs = other_half(down_theirs)
    dx1b = jnp.concatenate(dx1_slots, axis=0)
    d_attn = dot(dx1b, o_full, NT).astype(bf16)
    d_send = [
        lax.dynamic_slice_in_dim(d_attn, ((ctx & (groups - 1)) ^ s) * PAIR, PAIR, 1)
        for s in range(groups)
    ]
    d_send, dx1b, out_all = hold(d_send, dx1b, out_all)
    d_pieces = [d_send[0]] + [
        swap_with(d_send[s % groups], CONTEXT, s) for s in range(1, ctxs)
    ]

    o_theirs = dot(attn, dx1b[:, half:], TN).astype(bf16)
    o_mine = dot(attn, dx1b[:, :half], TN).astype(bf16)
    o_theirs = other_half(o_theirs)

    out_received = send_rows([slot_of(out_all, i) for i in range(slots)])
    gate_out = scatter_rest(gate_parts)
    up_out = scatter_rest(up_parts)
    down_parts = scatter_step(blocks_of(down_mine, down_theirs, 1), 1)
    back = attend_back(
        ids, pieces, d_pieces, o_t, lse, full_tables, groups, slots, docs, pics, bq, bk
    )
    back_rest = [swap_with(back[s], CONTEXT, s) for s in range(1, groups)]

    output = by_shard(
        (x1 + add_rows(slot_of(out_all, 0).astype(f32), out_received)).astype(bf16)
    )[None]
    o_parts = scatter_step(blocks_of(o_mine, o_theirs, 1), 1)
    down_grad = scatter_rest(down_parts)
    o_grad = scatter_rest(o_parts)

    d_qkv, norm1_parts = join(ids, [back[0]] + back_rest, own_qkv, oth_qkv, slots, NT)
    norm1_parts, d_qkv = hold(norm1_parts, d_qkv)
    dh1_received = send_rows(norm1_parts)
    qkv_theirs = []
    qkv_mine = []
    qkv_parts = []
    qkv_grad = []
    for j in range(3):
        qkv_theirs.append(other_half(dot(h1[:, half:], d_qkv[j], TN).astype(bf16)))
        qkv_mine.append(dot(h1[:, :half], d_qkv[j], TN).astype(bf16))
        qkv_parts.append(scatter_step(blocks_of(qkv_mine[j], qkv_theirs[j], 0), 1))
        qkv_grad.append(scatter_rest(qkv_parts[j]))
    dh1 = add_rows(norm1_parts[0], dh1_received)

    mean1 = jnp.mean(x_share, axis=-1, keepdims=True)
    cent1 = x_share - mean1
    inv1 = lax.rsqrt(jnp.mean(cent1 * cent1, axis=-1, keepdims=True) + EPS)
    unit1 = cent1 * inv1
    e1 = dh1 * gain_one
    tokens_grad = dx1 + inv1 * (
        e1
        - jnp.mean(e1, axis=-1, keepdims=True)
        - unit1 * jnp.mean(e1 * unit1, axis=-1, keepdims=True)
    )
    tokens_grad = by_shard(tokens_grad)[None]

    norms = jnp.stack(
        [
            jnp.sum(dh1 * unit1, axis=0),
            jnp.sum(dh1, axis=0),
            jnp.sum(dh2 * unit2, axis=0),
            jnp.sum(dh2, axis=0),
        ]
    )
    norms = sum_over(by_shard(norms), TENSOR)
    bias = jnp.concatenate(
        [jnp.sum(d.astype(f32), axis=0, keepdims=True) for d in d_qkv], axis=1
    )
    sums = sum_over(jnp.concatenate([norms.reshape(1, 4 * width), bias], axis=1), SHARD)
    sums = sum_over(sums, CONTEXT)
    norms = sums[0, : 4 * width].reshape(4, width)
    bias = sums[0, 4 * width :]
    k_bias_grad = bias[inner : 2 * inner].reshape(heads_here, HEAD_DIM)[:, :ROT]
    return (
        output,
        tokens_grad,
        norms[0],
        norms[1],
        *qkv_grad,
        bias[:inner],
        k_bias_grad.reshape(heads_here * ROT),
        bias[2 * inner :],
        o_grad,
        norms[2],
        norms[3],
        gate_out,
        up_out,
        down_grad,
    )


def solution(mesh):
    tokens = P(SHARD, CONTEXT, None)
    inward = P(SHARD, TENSOR)
    outward = P(TENSOR, SHARD)
    vector = P(TENSOR)
    placed = (
        tokens,
        P(),
        P(),
        inward,
        inward,
        inward,
        vector,
        vector,
        vector,
        outward,
        P(),
        P(),
        inward,
        inward,
        outward,
        tokens,
        P(SHARD, None),
        P(SHARD, None),
    )
    share = P(SHARD, (CONTEXT, TENSOR), None)
    grad_in = P((SHARD, CONTEXT), TENSOR)
    grad_out = P(TENSOR, (SHARD, CONTEXT))

    return jax.shard_map(
        local,
        mesh=mesh,
        in_specs=placed,
        out_specs=(
            share,
            share,
            P(),
            P(),
            grad_in,
            grad_in,
            grad_in,
            vector,
            vector,
            vector,
            grad_out,
            P(),
            P(),
            grad_in,
            grad_in,
            grad_out,
        ),
        check_vma=False,
    )
```
